32 devices in a mesh: fsdp: 8 (over y, x, core), tensor: 4 (over z).
Axes of the slice: x: 2, y: 2, z: 4, core: 2. Of those that a mesh axis runs over, the one named last changes fastest.
Arguments:
- tokens: bfloat16 [4096, 1152], P(('fsdp', 'tensor')), may hold values from -6 to 6
- cotangent: bfloat16 [4096, 1152], P(('fsdp', 'tensor')), may hold values from -6 to 6
- first_gain: float32 [1152], replicated, may hold values from 0.5 to 1.5
- first_shift: float32 [1152], replicated, may hold values from -1.5 to 1.5
- query_weight: bfloat16 [1152, 1152], P('fsdp', 'tensor'), may hold values from -2 to 2
- key_weight: bfloat16 [1152, 1152], P('fsdp', 'tensor'), may hold values from -2 to 2
- value_weight: bfloat16 [1152, 1152], P('fsdp', 'tensor'), may hold values from -0.1875 to 0.1875
- query_bias: float32 [1152], P('tensor'), may hold values from -2.5 to 2.5
- value_bias: float32 [1152], P('tensor'), may hold values from -2.5 to 2.5
- out_weight: bfloat16 [1152, 1152], P('tensor', 'fsdp'), may hold values from -1.5 to 1.5
- out_bias: float32 [1152], replicated, may hold values from -2.5 to 2.5
- second_gain: float32 [1152], replicated, may hold values from 0.5 to 1.5
- second_shift: float32 [1152], replicated, may hold values from -1.5 to 1.5
- up_weight: bfloat16 [1152, 4304], P('fsdp', 'tensor'), may hold values from -0.1875 to 0.1875
- up_bias: float32 [4304], P('tensor'), may hold values from -2.5 to 2.5
- down_weight: bfloat16 [4304, 1152], P('tensor', 'fsdp'), may hold values from -0.09375 to 0.09375
- down_bias: float32 [1152], replicated, may hold values from -2.5 to 2.5
Outputs:
- layer_out: bfloat16 [4096, 1152], P(('fsdp', 'tensor'))
- input_grad: float32 [4096, 1152], P(('fsdp', 'tensor'))
- first_gain_gradient: float32 [1152], replicated
- first_shift_gradient: float32 [1152], replicated
- query_weight_gradient: float32 [1152, 1152], P('fsdp', 'tensor')
- key_weight_gradient: float32 [1152, 1152], P('fsdp', 'tensor')
- value_weight_gradient: float32 [1152, 1152], P('fsdp', 'tensor')
- query_bias_gradient: float32 [1152], P('tensor')
- value_bias_gradient: float32 [1152], P('tensor')
- out_weight_gradient: float32 [1152, 1152], P('tensor', 'fsdp')
- out_bias_gradient: float32 [1152], replicated
- second_gain_gradient: float32 [1152], replicated
- second_shift_gradient: float32 [1152], replicated
- up_weight_gradient: float32 [1152, 4304], P('fsdp', 'tensor')
- up_bias_gradient: float32 [4304], P('tensor')
- down_weight_gradient: float32 [4304, 1152], P('tensor', 'fsdp')
- down_bias_gradient: float32 [1152], replicated
The draws below stay inside these ranges and needn't reach their ends.
All inputs are finite; a program needn't handle non-finite values.
Results may differ from the reference program's by a relative error of at most 0.014.
Values may be sent and summed in bfloat16 or wider, within the bound.
A program may use at most 128 MiB of HBM per device.

```python
import math
import jax
import jax.numpy as jnp
from jax import lax

D = 1152
HEADS = 16
HD = 72
FF = 4304
SEQ = 256
TOKENS = 4096


def projection_draw(key, which):
    base_key = jax.random.fold_in(jax.random.fold_in(key, 9173), which)
    unit_scale = D ** (-0.5)
    drawn = jnp.clip(jax.random.normal(base_key, (D, D), jnp.float32), -4.0, 4.0)
    return jnp.clip(unit_scale * drawn, -2.0, 2.0)


def draw_query_weight(key, part):
    return projection_draw(key, 1).astype(jnp.bfloat16)


def draw_key_weight(key, part):
    return projection_draw(key, 2).astype(jnp.bfloat16)


def raised(array, rng, source, target, parts, factor):
    def block_of(position):
        return (jnp.arange(array.shape[position]) // (array.shape[position] // parts)).reshape((-1,) + (1,) * (array.ndim - 1 - position))

    near = jax.random.permutation(rng, parts)[block_of(target)]
    other_side = (block_of(target) + parts // 2) % parts
    return jnp.where((block_of(source) == near) | (block_of(source) == other_side), factor * array, array)


def level_of(stream_key, shape, cuts, low, top_value):
    factor_of = 1.0
    for axis_at, blocks in cuts:
        draws = jax.random.uniform(jax.random.fold_in(jax.random.fold_in(stream_key, 6), axis_at), (blocks,), jnp.float32, low / len(cuts), top_value / len(cuts))
        factor_of = factor_of * jnp.repeat(jnp.exp(draws), shape[axis_at] // blocks).reshape((-1,) + (1,) * (len(shape) - 1 - axis_at))
    return factor_of


def scatter_about(own_key, shape, spread, reach, shards=(), held_as=jnp.bfloat16):
    drawn = jax.random.normal(own_key, shape, jnp.float32) * spread
    if len(shards) > 0:
        drawn = level_of(own_key, shape, shards, -0.22, 0.18) * drawn
    return jnp.clip(drawn, min=-reach, max=reach).astype(held_as)


def heavy_noise(own_key, shape, width, limit, split, heavy, dtype=jnp.bfloat16):
    values = width * jax.random.normal(own_key, shape, jnp.float32)
    if split:
        values = values * level_of(own_key, shape, split, -0.22, 0.18)
    return jnp.clip(raised(values, jax.random.fold_in(own_key, 3), *heavy), -limit, limit).astype(dtype)


def setup_inputs(seed: int = 0) -> dict:
    key_list = jax.random.split(jax.random.key(seed), 18)
    tokens = scatter_about(key_list[0], (TOKENS, D), 1.0, 6.0, ((0, 32),))
    cotangent = heavy_noise(key_list[1], (TOKENS, D), 1.0, 6.0, ((0, 32),), (0, 1, 32, 2.75))
    first_gain = jnp.clip(1.0 + 0.1 * jax.random.normal(key_list[2], (D,), jnp.float32), 0.5, 1.5)
    first_shift = scatter_about(key_list[3], (D,), 0.3, 1.5, (), jnp.float32)
    query_weight = draw_query_weight(jax.random.fold_in(key_list[17], 71), 0)
    key_weight = draw_key_weight(jax.random.fold_in(key_list[17], 71), 0)
    value_weight = scatter_about(key_list[6], (D, D), D ** -0.5, 0.1875, ((0, 8), (1, 4)))
    query_bias = scatter_about(key_list[7], (D,), 0.5, 2.5, ((0, 4),), jnp.float32)
    value_bias = scatter_about(key_list[8], (D,), 0.5, 2.5, ((0, 4),), jnp.float32)
    out_weight = scatter_about(key_list[9], (D, D), (D // 64) ** -0.5, 1.5, ((0, 4), (1, 8)))
    out_bias = scatter_about(key_list[10], (D,), 0.5, 2.5, (), jnp.float32)
    second_gain = jnp.clip(1.0 + 0.1 * jax.random.normal(key_list[11], (D,), jnp.float32), 0.5, 1.5)
    second_shift = scatter_about(key_list[12], (D,), 0.3, 1.5, (), jnp.float32)
    up_weight = scatter_about(key_list[13], (D, FF), D ** -0.5, 0.1875, ((0, 8), (1, 4)))
    up_bias = scatter_about(key_list[14], (FF,), 0.5, 2.5, ((0, 4),), jnp.float32)
    down_weight = scatter_about(key_list[15], (FF, D), FF ** -0.5, 0.09375, ((0, 4), (1, 8)))
    down_bias = scatter_about(key_list[16], (D,), 0.5, 2.5, (), jnp.float32)
    return dict(tokens=tokens, cotangent=cotangent, first_gain=first_gain, first_shift=first_shift, query_weight=query_weight, key_weight=key_weight, value_weight=value_weight, query_bias=query_bias, value_bias=value_bias, out_weight=out_weight, out_bias=out_bias, second_gain=second_gain, second_shift=second_shift, up_weight=up_weight, up_bias=up_bias, down_weight=down_weight, down_bias=down_bias)


@jax.custom_vjp
def low(v):
    return lax.optimization_barrier(v.astype(jnp.bfloat16)).astype(jnp.float32)

@jax.custom_vjp
def low_back(v):
    return v

def low_keep(v):
    return (low(v), None)

def low_pass(kept, grad):
    return (grad,)

def back_keep(v):
    return (v, None)

def back_low(kept, grad):
    return (low(grad),)
low.defvjp(low_keep, low_pass)
low_back.defvjp(back_keep, back_low)
norm_eps = 1e-06
gelu_coef = 0.7978845608028654
cubic_coef = 0.044715
highest = lax.Precision.HIGHEST

def layer_norm(values, gain, shift):
    row_mean = lax.optimization_barrier(jnp.mean(values, axis=-1, keepdims=True))
    centred = values - row_mean
    variance = lax.optimization_barrier(jnp.mean(centred * centred, axis=-1, keepdims=True))
    return centred * lax.rsqrt(variance + norm_eps) * gain + shift

def matmul(left, right):
    return jnp.matmul(left, right, precision=highest)

def gelu_tanh(upper):
    return 0.5 * upper * (1.0 + jnp.tanh(gelu_coef * (upper + cubic_coef * upper * upper * upper)))

def block_forward(params, rows_in):
    first_gain, first_shift, query_weight, key_weight, value_weight, query_bias, value_bias, out_weight, out_bias, second_gain, second_shift, up_weight, up_bias, down_weight, down_bias = params
    shape_four = rows_in.shape[:2] + (HEADS, HD)
    normed_first = low(layer_norm(rows_in, first_gain, first_shift))
    queries = low(low_back(matmul(normed_first, query_weight) + query_bias))
    keys_all = low(low_back(matmul(normed_first, key_weight)))
    values = low(low_back(matmul(normed_first, value_weight) + value_bias))
    scores = jnp.einsum('nqhd,nkhd->nhqk', queries.reshape(shape_four), keys_all.reshape(shape_four), precision=highest)
    scores = low_back(scores * HD ** (-0.5))
    peak = lax.optimization_barrier(jnp.max(scores, axis=-1, keepdims=True))
    expo = jnp.exp(scores - peak)
    probs = low(expo / lax.optimization_barrier(jnp.sum(expo, axis=-1, keepdims=True)))
    mixed = jnp.einsum('nhqk,nkhd->nqhd', probs, values.reshape(shape_four), precision=highest)
    mixed = low(low_back(mixed.reshape(rows_in.shape)))
    middle = rows_in + low_back(matmul(mixed, out_weight) + out_bias)
    normed_second = low(layer_norm(middle, second_gain, second_shift))
    upper = low_back(matmul(normed_second, up_weight) + up_bias)
    hidden = low(gelu_tanh(upper))
    return middle + low_back(matmul(hidden, down_weight) + down_bias)

def add_pair(first_term, second_term):
    return first_term + second_term

def reference(tokens, cotangent, first_gain, first_shift, query_weight, key_weight, value_weight, query_bias, value_bias, out_weight, out_bias, second_gain, second_shift, up_weight, up_bias, down_weight, down_bias):
    params = tuple((piece_arg.astype(jnp.float32) for piece_arg in (first_gain, first_shift, query_weight, key_weight, value_weight, query_bias, value_bias, out_weight, out_bias, second_gain, second_shift, up_weight, up_bias, down_weight, down_bias)))
    images = TOKENS // SEQ
    per_block = math.gcd(images, max(1, 4096 // SEQ))
    blocks = images // per_block
    rows_all = tokens.astype(jnp.float32).reshape(blocks, per_block, SEQ, D)
    grads_all = cotangent.astype(jnp.float32).reshape(blocks, per_block, SEQ, D)

    def one_block(totals, pair):
        block_rows, block_grad = pair
        result, pullback = jax.vjp(block_forward, params, block_rows)
        param_grads, row_grads = pullback(block_grad)
        return (jax.tree.map(add_pair, totals, param_grads), (result, row_grads))
    start_totals = jax.tree.map(jnp.zeros_like, params)
    totals, (results, row_grads) = lax.scan(one_block, start_totals, (rows_all, grads_all))
    layer_out = results.reshape(TOKENS, D).astype(jnp.bfloat16)
    input_grad = row_grads.reshape(TOKENS, D)
    return (layer_out, input_grad, totals[0], totals[1], totals[2], totals[3], totals[4], totals[5], totals[6], totals[7], totals[8], totals[9], totals[10], totals[11], totals[12], totals[13], totals[14])
```

```python
import math

import jax
import jax.numpy as jnp
from jax import lax
from jax.experimental import pallas as pl
from jax.experimental.pallas import tpu as pltpu
from jax.sharding import PartitionSpec as P

D = 1152
HD = 72
FF = 4304
SEQ = 256


norm_eps = 1e-06
gelu_coef = 0.7978845608028654
cubic_coef = 0.044715


def dot_plain(left, right):
    return jnp.dot(left, right, preferred_element_type=jnp.float32)


def dot_right_t(left, right):
    return lax.dot_general(
        left, right, (((1,), (1,)), ((), ())), preferred_element_type=jnp.float32
    )


def dot_left_t(left, right):
    return lax.dot_general(
        left, right, (((0,), (0,)), ((), ())), preferred_element_type=jnp.float32
    )


def norm_rows(values, gain, shift):
    row_mean = jnp.mean(values, axis=1, keepdims=True)
    centred = values - row_mean
    inv_scale = lax.rsqrt(jnp.mean(centred * centred, axis=1, keepdims=True) + norm_eps)
    normed = centred * inv_scale
    return (normed * gain + shift, normed, inv_scale)


def norm_back(out_grad, normed, inv_scale, gain):
    scaled_grad = out_grad * gain
    grad_mean = jnp.mean(scaled_grad, axis=1, keepdims=True)
    cross_mean = jnp.mean(scaled_grad * normed, axis=1, keepdims=True)
    in_grad = inv_scale * (scaled_grad - grad_mean - normed * cross_mean)
    return (in_grad, jnp.sum(out_grad * normed, axis=0), jnp.sum(out_grad, axis=0))


def gelu_pair(upper):
    tangent = jnp.tanh(gelu_coef * (upper + cubic_coef * upper * upper * upper))
    gelu_value = 0.5 * upper * (1.0 + tangent)
    gelu_slope = 0.5 * (1.0 + tangent) + 0.5 * upper * (1.0 - tangent * tangent) * gelu_coef * (
        1.0 + 3.0 * cubic_coef * upper * upper
    )
    return (gelu_value, gelu_slope)


def split_heads(block_rows, head_count):
    col_width = block_rows.shape[1] // 3
    img_count = block_rows.shape[0] // SEQ
    shape_four = (img_count, SEQ, head_count, HD)
    queries = block_rows[:, :col_width].reshape(shape_four)
    keys_part = block_rows[:, col_width : 2 * col_width].reshape(shape_four)
    values = block_rows[:, 2 * col_width :].reshape(shape_four)
    return (queries, keys_part, values, shape_four)


def attend_forward(block_rows, head_count):
    queries, keys_part, values, shape_four = split_heads(block_rows, head_count)
    scores = jnp.einsum(
        "nqhd,nkhd->nhqk", queries, keys_part, preferred_element_type=jnp.float32
    ) * HD ** (-0.5)
    peak = jnp.max(scores, axis=-1, keepdims=True)
    expo = jnp.exp(scores - peak)
    totals = jnp.sum(expo, axis=-1, keepdims=True)
    prob_low = (expo / totals).astype(jnp.bfloat16)
    mixed = jnp.einsum("nhqk,nkhd->nqhd", prob_low, values, preferred_element_type=jnp.float32)
    row_total = block_rows.shape[0]
    mixed = mixed.reshape(row_total, head_count * HD).astype(jnp.bfloat16)
    return (mixed, (peak + jnp.log(totals))[..., 0])


def attend_backward(inputs, head_count):
    block_rows, grad_block, log_total = inputs
    queries, keys_part, values, shape_four = split_heads(block_rows, head_count)
    grad_out = grad_block.reshape(shape_four)
    scores = jnp.einsum(
        "nqhd,nkhd->nhqk", queries, keys_part, preferred_element_type=jnp.float32
    ) * HD ** (-0.5)
    probs = jnp.exp(scores - log_total[..., None])
    prob_low = probs.astype(jnp.bfloat16)
    value_grad = jnp.einsum(
        "nhqk,nqhd->nkhd", prob_low, grad_out, preferred_element_type=jnp.float32
    )
    prob_grad = jnp.einsum("nqhd,nkhd->nhqk", grad_out, values, preferred_element_type=jnp.float32)
    row_dot = jnp.sum(probs * prob_grad, axis=-1, keepdims=True)
    score_grad = (probs * (prob_grad - row_dot)).astype(jnp.bfloat16)
    query_grad = jnp.einsum(
        "nhqk,nkhd->nqhd", score_grad, keys_part, preferred_element_type=jnp.float32
    ) * HD ** (-0.5)
    key_grad = jnp.einsum(
        "nhqk,nqhd->nkhd", score_grad, queries, preferred_element_type=jnp.float32
    ) * HD ** (-0.5)
    row_total = block_rows.shape[0]
    col_width = head_count * HD
    return jnp.concatenate(
        (
            query_grad.reshape(row_total, col_width),
            key_grad.reshape(row_total, col_width),
            value_grad.reshape(row_total, col_width),
        ),
        axis=1,
    ).astype(jnp.bfloat16)


def on_device(
    tokens,
    cotangent,
    first_gain,
    first_shift,
    query_weight,
    key_weight,
    value_weight,
    query_bias,
    value_bias,
    out_weight,
    out_bias,
    second_gain,
    second_shift,
    up_weight,
    up_bias,
    down_weight,
    down_bias,
):
    full_query, full_key, full_value, full_outp, full_up, full_down = (
        lax.all_gather(query_weight, "fsdp", axis=0, tiled=True),
        lax.all_gather(key_weight, "fsdp", axis=0, tiled=True),
        lax.all_gather(value_weight, "fsdp", axis=0, tiled=True),
        lax.all_gather(out_weight, "fsdp", axis=1, tiled=True),
        lax.all_gather(up_weight, "fsdp", axis=0, tiled=True),
        lax.all_gather(down_weight, "fsdp", axis=1, tiled=True),
    )
    qkv_weight = jnp.concatenate((full_query, full_key, full_value), axis=1)
    local_width = full_query.shape[1]
    ffn_width = full_up.shape[1]
    head_count = local_width // HD
    token_rows = tokens.astype(jnp.float32)
    first_out, first_hat, first_scale = norm_rows(token_rows, first_gain, first_shift)
    all_first = lax.all_gather(first_out.astype(jnp.bfloat16), "tensor", axis=0, tiled=True)
    qkv_bias = jnp.concatenate((query_bias, jnp.zeros_like(query_bias), value_bias))
    qkv_rows = (dot_plain(all_first, qkv_weight) + qkv_bias).astype(jnp.bfloat16)
    group_rows = qkv_rows.shape[0]
    images = group_rows // SEQ
    per_block = math.gcd(images, max(1, 512 // SEQ))
    blocks = images // per_block
    stacked = qkv_rows.reshape(blocks, per_block * SEQ, 3 * local_width)

    def forward_block(block_rows):
        return attend_forward(block_rows, head_count)

    head_out, log_total = lax.map(forward_block, stacked)
    head_out = head_out.reshape(group_rows, local_width)
    attn_rows = lax.psum_scatter(
        dot_plain(head_out, full_outp), "tensor", scatter_dimension=0, tiled=True
    )
    mid_rows = token_rows + attn_rows + out_bias
    second_out, second_hat, second_scale = norm_rows(mid_rows, second_gain, second_shift)
    all_second = lax.all_gather(second_out.astype(jnp.bfloat16), "tensor", axis=0, tiled=True)
    up_pre = dot_plain(all_second, full_up) + up_bias
    hidden_value, hidden_slope = gelu_pair(up_pre)
    hidden_low = hidden_value.astype(jnp.bfloat16)
    mlp_rows = lax.psum_scatter(
        dot_plain(hidden_low, full_down).astype(jnp.bfloat16),
        "tensor",
        scatter_dimension=0,
        tiled=True,
    ).astype(jnp.float32)
    layer_out = (mid_rows + mlp_rows + down_bias).astype(jnp.bfloat16)
    out_grad = cotangent.astype(jnp.float32)
    all_out_grad = lax.all_gather(cotangent, "tensor", axis=0, tiled=True)
    down_grad = dot_left_t(hidden_low, all_out_grad)
    hidden_grad = dot_right_t(all_out_grad, full_down)
    upper_low = (hidden_grad * hidden_slope).astype(jnp.bfloat16)
    up_bias_grad = jnp.sum(upper_low.astype(jnp.float32), axis=0)
    up_grad = dot_left_t(all_second, upper_low)
    second_grad = lax.psum_scatter(
        dot_right_t(upper_low, full_up), "tensor", scatter_dimension=0, tiled=True
    )
    back_second, second_gain_grad, second_shift_grad = norm_back(
        second_grad, second_hat, second_scale, second_gain
    )
    mid_grad = out_grad + back_second
    mid_low = mid_grad.astype(jnp.bfloat16)
    all_mid_grad = lax.all_gather(mid_low, "tensor", axis=0, tiled=True)
    outp_grad = dot_left_t(head_out, all_mid_grad)
    head_grad = dot_right_t(all_mid_grad, full_outp).astype(jnp.bfloat16)

    def backward_block(inputs):
        return attend_backward(inputs, head_count)

    qkv_grad = lax.map(
        backward_block,
        (stacked, head_grad.reshape(blocks, per_block * SEQ, local_width), log_total),
    )
    qkv_grad = qkv_grad.reshape(group_rows, 3 * local_width)
    qkv_weight_grad = dot_left_t(all_first, qkv_grad)
    qkv_bias_grad = jnp.sum(qkv_grad.astype(jnp.float32), axis=0)
    first_grad = lax.psum_scatter(
        dot_right_t(qkv_grad, qkv_weight).astype(jnp.bfloat16),
        "tensor",
        scatter_dimension=0,
        tiled=True,
    ).astype(jnp.float32)
    back_first, first_gain_grad, first_shift_grad = norm_back(
        first_grad, first_hat, first_scale, first_gain
    )
    input_grad = mid_grad + back_first
    out_bias_grad = jnp.sum(mid_low.astype(jnp.float32), axis=0)
    down_bias_grad = jnp.sum(out_grad, axis=0)
    small_terms = jnp.concatenate(
        (
            first_gain_grad,
            first_shift_grad,
            out_bias_grad,
            second_gain_grad,
            second_shift_grad,
            down_bias_grad,
        )
    )
    tensor_index = lax.axis_index("tensor")
    head_terms = jnp.zeros((2 * D + FF,), jnp.float32)
    head_terms = lax.dynamic_update_slice(
        head_terms, qkv_bias_grad[:local_width], (tensor_index * local_width,)
    )
    head_terms = lax.dynamic_update_slice(
        head_terms, qkv_bias_grad[2 * local_width :], (D + tensor_index * local_width,)
    )
    head_terms = lax.dynamic_update_slice(
        head_terms, up_bias_grad, (2 * D + tensor_index * ffn_width,)
    )
    small_sums, head_sums = lax.psum((small_terms, head_terms), ("fsdp", "tensor"))
    query_bias_total = lax.dynamic_slice(head_sums, (tensor_index * local_width,), (local_width,))
    value_bias_total = lax.dynamic_slice(
        head_sums, (D + tensor_index * local_width,), (local_width,)
    )
    up_bias_total = lax.dynamic_slice(head_sums, (2 * D + tensor_index * ffn_width,), (ffn_width,))
    query_part, key_part, value_part, outp_part, up_part, down_part = (
        lax.psum_scatter(qkv_weight_grad[:, :local_width], "fsdp", scatter_dimension=0, tiled=True),
        lax.psum_scatter(
            qkv_weight_grad[:, local_width : 2 * local_width],
            "fsdp",
            scatter_dimension=0,
            tiled=True,
        ),
        lax.psum_scatter(
            qkv_weight_grad[:, 2 * local_width :], "fsdp", scatter_dimension=0, tiled=True
        ),
        lax.psum_scatter(outp_grad, "fsdp", scatter_dimension=1, tiled=True),
        lax.psum_scatter(up_grad, "fsdp", scatter_dimension=0, tiled=True),
        lax.psum_scatter(down_grad, "fsdp", scatter_dimension=1, tiled=True),
    )
    return (
        layer_out,
        input_grad,
        small_sums[0:D],
        small_sums[D : 2 * D],
        query_part,
        key_part,
        value_part,
        query_bias_total,
        value_bias_total,
        outp_part,
        small_sums[2 * D : 3 * D],
        small_sums[3 * D : 4 * D],
        small_sums[4 * D : 5 * D],
        up_part,
        up_bias_total,
        down_part,
        small_sums[5 * D : 6 * D],
    )


MESH_IDS = pl.DeviceIdType.MESH
LANES = 128


def round_up(value, step):
    return -(-value // step) * step


def layer_kernel(
    shapes,
    tokens_ref,
    cotangent_ref,
    vectors_ref,
    attn_piece,
    up_piece,
    down_piece,
    layer_ref,
    input_grad_ref,
    attn_grad_ref,
    up_grad_ref,
    down_grad_ref,
    vector_grad_ref,
    attn_w,
    up_w,
    down_w,
    attn_g,
    up_g,
    down_g,
    land_o,
    land_q,
    land_u,
    land_d,
    first_all,
    second_all,
    dy_all,
    mid_all,
    head_rows,
    head_grads,
    probs_all,
    mixed_heads,
    mixed_all,
    hidden_all,
    slope_all,
    upper_all,
    qkv_grads,
    part_a,
    part_b,
    core_send,
    core_land,
    deep_send,
    deep_land,
    first_hat,
    second_hat,
    mid_rows,
    mid_grad,
    row_scale,
    vec_send,
    vec_land,
    far_vectors,
    send_sems,
    recv_sems,
):
    rows, heads, width, qkv_lanes, piece = shapes
    bf16, f32 = jnp.bfloat16, jnp.float32
    pair = 2 * rows
    out_base = 3 * width
    win = out_base // LANES * LANES
    win_shift = out_base - win
    all_lanes = attn_w.shape[1]

    f = lax.axis_index("fsdp")
    t = lax.axis_index("tensor")
    c, k = lax.rem(f, 2), lax.div(f, 2)
    kx, ky = lax.rem(k, 2), lax.div(k, 2)
    zl, zh = lax.rem(t, 2), lax.div(t, 2)
    oc = 1 - c
    k_x, k_y, k_d = ky * 2 + (1 - kx), (1 - ky) * 2 + kx, (1 - ky) * 2 + (1 - kx)
    home = c == zh
    far_t = (1 - zh) * 2 + zl
    dev_x = {"fsdp": 2 * k_x + c, "tensor": t}
    dev_y = {"fsdp": 2 * k_y + c, "tensor": t}
    dev_c = {"fsdp": 2 * k + oc, "tensor": t}
    dev_z = {"fsdp": f, "tensor": zh * 2 + (1 - zl)}
    dev_far = {"fsdp": f, "tensor": far_t}
    dev_far_other = {"fsdp": 2 * k + oc, "tensor": far_t}

    counter = [0]
    pending = []

    def new_sem():
        counter[0] += 1
        return counter[0] - 1

    def remote(src, dst, device, sem, when=None):
        copy = pltpu.make_async_remote_copy(
            src_ref=src,
            dst_ref=dst,
            send_sem=send_sems.at[sem],
            recv_sem=recv_sems.at[sem],
            device_id=device,
            device_id_type=MESH_IDS,
        )
        if when is None:
            copy.start()
        else:
            pl.when(when)(copy.start)
        pending.append((copy, when))

    def remote_to(src, dst, device, send, recv, when=None):
        copy = pltpu.make_async_remote_copy(
            src_ref=src,
            dst_ref=dst,
            send_sem=send_sems.at[send],
            recv_sem=recv_sems.at[recv],
            device_id=device,
            device_id_type=MESH_IDS,
        )
        if when is None:
            copy.start()
        else:
            pl.when(when)(copy.start)
        pending.append((copy, when))

    def arrived(dst, sem):
        pltpu.make_async_copy(dst, dst, recv_sems.at[sem]).wait()

    def block(buf, index, lo, hi):
        return buf.at[pl.ds(pl.multiple_of(index * piece, piece), piece), lo:hi]

    def aligned(start, size):
        return pl.ds(pl.multiple_of(start, LANES), size)

    near, deep = zl * pair, (1 - zl) * pair

    def slot(side, core):
        return aligned(side + core * rows, rows)

    barrier = pltpu.get_barrier_semaphore()
    peers = (dev_x, dev_y, dev_c, dev_z, dev_far, dev_far_other)
    for peer in peers:
        pl.semaphore_signal(barrier, inc=1, device_id=peer, device_id_type=MESH_IDS)

    def spread_start(src, buf, lo, hi):
        base = counter[0]
        for _ in range(2):
            new_sem()
        take = pl.ds(0, piece)
        source = src.at[take, lo:hi]
        target = block(buf, f, lo, hi)

        @pl.when(home)
        def _():
            pltpu.make_async_copy(source, target, recv_sems.at[base + c]).start()

        remote_to(
            source,
            target,
            {"fsdp": 2 * k + zh, "tensor": t},
            base,
            base + c,
            when=jnp.logical_not(home),
        )
        remote_to(
            source, target, {"fsdp": 2 * k + zh, "tensor": far_t}, base + 1, base + c
        )
        return base

    def gather_start(buf, lo, hi, base):
        sems = [new_sem() for _ in range(6)]
        a_own, b_own = block(buf, 2 * k, lo, hi), block(buf, 2 * k + 1, lo, hi)
        arrived(a_own, base)
        remote(a_own, a_own, dev_x, sems[0])
        arrived(b_own, base + 1)
        remote(b_own, b_own, dev_y, sems[1])
        remote(a_own, a_own, dev_y, sems[2])
        remote(b_own, b_own, dev_x, sems[3])
        return sems

    def gather_forward(buf, lo, hi, sems):
        a_x, b_y = block(buf, 2 * k_x, lo, hi), block(buf, 2 * k_y + 1, lo, hi)
        arrived(a_x, sems[0])
        remote(a_x, a_x, dev_y, sems[4])
        arrived(b_y, sems[1])
        remote(b_y, b_y, dev_x, sems[5])

    def gather_finish(buf, lo, hi, sems):
        arrived(block(buf, 2 * k_y, lo, hi), sems[2])
        arrived(block(buf, 2 * k_x + 1, lo, hi), sems[3])
        arrived(block(buf, 2 * k_d, lo, hi), sems[4])
        arrived(block(buf, 2 * k_d + 1, lo, hi), sems[5])

    def share_start(buf):
        sems = [new_sem() for _ in range(3)]
        own = buf.at[slot(near, c)]
        remote(own, own, dev_z, sems[0])
        remote(own, own, dev_c, sems[1])
        return sems

    def share_near(buf, sems):
        arrived(buf.at[slot(near, oc)], sems[1])

    def share_forward(buf, sems):
        got = buf.at[slot(deep, c)]
        arrived(got, sems[0])
        remote(got, got, dev_c, sems[2])

    def share_deep(buf, sems):
        arrived(buf.at[slot(deep, oc)], sems[2])

    def sum_deep(which, part):
        sems = [new_sem() for _ in range(3)]
        core_send[which, 0] = part[slot(deep, oc), :].astype(bf16)
        remote(core_send.at[which, 0], core_land.at[which, 0], dev_c, sems[0])
        return sems

    def sum_pass(which, part, sems):
        arrived(core_land.at[which, 0], sems[0])
        total = part[slot(deep, c), :] + core_land[which, 0].astype(f32)
        deep_send[which] = total.astype(bf16)
        remote(deep_send.at[which], deep_land.at[which], dev_z, sems[1])

    def sum_near(which, part, sems):
        core_send[which, 1] = part[slot(near, oc), :].astype(bf16)
        remote(core_send.at[which, 1], core_land.at[which, 1], dev_c, sems[2])

    def sum_finish(which, part, sems):
        arrived(core_land.at[which, 1], sems[2])
        arrived(deep_land.at[which], sems[1])
        return (
            part[slot(near, c), :]
            + core_land[which, 1].astype(f32)
            + deep_land[which].astype(f32)
        )

    def reduce_first(grad, land, lo, hi):
        sems = [new_sem() for _ in range(8)]
        remote(block(grad, 2 * k_d, lo, hi), land.at[1], dev_y, sems[1])
        remote(block(grad, 2 * k_d + 1, lo, hi), land.at[3], dev_x, sems[3])
        remote(block(grad, 2 * k_y, lo, hi), land.at[0], dev_y, sems[0])
        remote(block(grad, 2 * k_x + 1, lo, hi), land.at[2], dev_x, sems[2])
        return sems

    def add_into(grad, index, lo, hi, land, place, sem):
        arrived(land.at[place], sem)
        at = pl.ds(pl.multiple_of(index * piece, piece), piece)
        grad[at, lo:hi] = (
            grad[at, lo:hi].astype(f32) + land[place].astype(f32)
        ).astype(bf16)

    def reduce_second(grad, land, lo, hi, sems):
        add_into(grad, 2 * k_x, lo, hi, land, 1, sems[1])
        remote(block(grad, 2 * k_x, lo, hi), land.at[4], dev_x, sems[4])
        add_into(grad, 2 * k_y + 1, lo, hi, land, 3, sems[3])
        remote(block(grad, 2 * k_y + 1, lo, hi), land.at[5], dev_y, sems[5])
        add_into(grad, 2 * k, lo, hi, land, 0, sems[0])
        add_into(grad, 2 * k + 1, lo, hi, land, 2, sems[2])

    def reduce_third(grad, land, lo, hi, sems):
        add_into(grad, 2 * k, lo, hi, land, 4, sems[4])
        add_into(grad, 2 * k + 1, lo, hi, land, 5, sems[5])
        extra = (new_sem(), new_sem())
        away = jnp.logical_not(home)
        for core in range(2):
            source = block(grad, 2 * k + core, lo, hi)
            mine = jnp.logical_and(home, c == core)

            @pl.when(mine)
            def _():
                pltpu.make_async_copy(
                    source, land.at[6], recv_sems.at[sems[6]]
                ).start()

            remote_to(
                source,
                land.at[6],
                {"fsdp": 2 * k + core, "tensor": t},
                extra[0],
                sems[6],
                when=jnp.logical_and(home, c != core),
            )
            remote_to(
                source,
                land.at[7],
                {"fsdp": 2 * k + core, "tensor": far_t},
                sems[6 + core],
                sems[7],
                when=away,
            )

    def reduce_finish(land, sems):
        arrived(land.at[6], sems[6])
        arrived(land.at[7], sems[7])
        return land[6].astype(f32) + land[7].astype(f32)

    first_gain, first_shift = vectors_ref[0:1, :], vectors_ref[1:2, :]
    out_bias, second_gain = vectors_ref[2:3, :], vectors_ref[3:4, :]
    second_shift, down_bias = vectors_ref[4:5, :], vectors_ref[5:6, :]

    with jax.named_scope("norm_one"):
        token_rows = tokens_ref[...].astype(f32)
        normed, hat, inv_scale = norm_rows(token_rows, first_gain, first_shift)
        first_all[slot(near, c), :] = normed.astype(bf16)
        first_hat[...] = hat
        row_scale[0] = jnp.broadcast_to(inv_scale, row_scale.shape[1:])
        dy_all[slot(near, c), :] = cotangent_ref[...]
        vec_send[0, 5:6, :] = jnp.sum(cotangent_ref[...].astype(f32), axis=0, keepdims=True)

    with jax.named_scope("entry"):
        pl.semaphore_wait(barrier, len(peers))

    vec_sem = new_sem()
    remote(vectors_ref, far_vectors, dev_far, vec_sem)
    q_base = spread_start(attn_piece, attn_w, 0, qkv_lanes)
    first_sems = share_start(first_all)
    o_base = spread_start(attn_piece, attn_w, qkv_lanes, all_lanes)
    u_base = spread_start(up_piece, up_w, 0, up_w.shape[1])
    dy_sems = share_start(dy_all)
    d_base = spread_start(down_piece, down_w, 0, down_w.shape[1])

    with jax.named_scope("clear"):
        head_rows[...] = jnp.zeros_like(head_rows)
        head_grads[...] = jnp.zeros_like(head_grads)
        mixed_all[...] = jnp.zeros_like(mixed_all)
        qkv_grads[...] = jnp.zeros_like(qkv_grads)

    with jax.named_scope("weights_q"):
        q_sems = gather_start(attn_w, 0, qkv_lanes, q_base)
    with jax.named_scope("share_first"):
        share_forward(first_all, first_sems)
    with jax.named_scope("weights_q2"):
        gather_forward(attn_w, 0, qkv_lanes, q_sems)
        o_sems = gather_start(attn_w, qkv_lanes, all_lanes, o_base)
        arrived(far_vectors, vec_sem)
        share_near(first_all, first_sems)
        share_deep(first_all, first_sems)
    with jax.named_scope("weights_q3"):
        gather_finish(attn_w, 0, qkv_lanes, q_sems)

    def unit_vector(row):
        return jnp.where(home, vectors_ref[row : row + 1, :], far_vectors[row : row + 1, :])

    qkv_bias = unit_vector(6)[:, :qkv_lanes]
    for side_at in range(2):
        with jax.named_scope("qkv"):
            side_rows = slice(side_at * pair, (side_at + 1) * pair)
            done = dot_plain(first_all[side_rows, :], attn_w[:, :qkv_lanes])
            done = (done + qkv_bias).astype(bf16)
            for image in range(2):
                to = slice(image * pair + side_at * rows, image * pair + (side_at + 1) * rows)
                for head in range(3 * heads):
                    head_rows[head, to, :HD] = done[
                        image * rows : (image + 1) * rows, head * HD : (head + 1) * HD
                    ]
    with jax.named_scope("weights_u"):
        gather_forward(attn_w, qkv_lanes, all_lanes, o_sems)
        u_sems = gather_start(up_w, 0, up_w.shape[1], u_base)
        share_forward(dy_all, dy_sems)

    scale = HD ** (-0.5)

    def image_head(step):
        head, image = lax.rem(step, heads), lax.div(step, heads)
        return head, aligned(image * pair, pair)

    def attend(step, carry):
        head, span = image_head(step)
        queries, keys_part = head_rows[head, span, :], head_rows[heads + head, span, :]
        values = head_rows[2 * heads + head, span, :]
        scores = dot_right_t(queries, keys_part) * scale
        expo = jnp.exp(scores - jnp.max(scores, axis=1, keepdims=True))
        probs = expo / jnp.sum(expo, axis=1, keepdims=True)
        probs_all[step] = probs
        mixed_heads[head, span, :] = dot_plain(probs.astype(bf16), values).astype(bf16)
        return carry

    with jax.named_scope("attend"):
        lax.fori_loop(0, 2 * heads, attend, 0)

    def pack(target, source, count, base):
        for side_at in range(2):
            for image in range(2):
                at = slice(side_at * pair + image * rows, side_at * pair + (image + 1) * rows)
                take = slice(image * pair + side_at * rows, image * pair + (side_at + 1) * rows)
                for head in range(count):
                    lo = base + head * HD
                    target[at, lo : lo + HD] = source[head, take, :HD]

    with jax.named_scope("mix"):
        pack(mixed_all, mixed_heads, heads, win_shift)

    def half(side):
        return aligned(side, pair)

    with jax.named_scope("weights_o"):
        gather_finish(attn_w, qkv_lanes, all_lanes, o_sems)
    with jax.named_scope("out"):
        part_a[half(deep), :] = dot_right_t(mixed_all[half(deep), :], attn_w[:, win:])
        out_sems = sum_deep(0, part_a)
        part_a[half(near), :] = dot_right_t(mixed_all[half(near), :], attn_w[:, win:])
    with jax.named_scope("out_pass"):
        sum_pass(0, part_a, out_sems)
        sum_near(0, part_a, out_sems)
    with jax.named_scope("weights_u2"):
        gather_forward(up_w, 0, up_w.shape[1], u_sems)
        d_sems = gather_start(down_w, 0, down_w.shape[1], d_base)
    with jax.named_scope("out_finish"):
        attn_rows = sum_finish(0, part_a, out_sems)
    with jax.named_scope("norm_two"):
        middle = tokens_ref[...].astype(f32) + attn_rows + out_bias
        mid_rows[...] = middle
        normed, hat, inv_scale = norm_rows(middle, second_gain, second_shift)
        second_all[slot(near, c), :] = normed.astype(bf16)
        second_hat[...] = hat
        row_scale[1] = jnp.broadcast_to(inv_scale, row_scale.shape[1:])
        second_sems = share_start(second_all)
    with jax.named_scope("weights_u3"):
        gather_finish(up_w, 0, up_w.shape[1], u_sems)
        share_near(second_all, second_sems)

    up_bias = unit_vector(7)
    chunk = 32

    def raise_half(side):
        part_b[half(side), :] = dot_plain(second_all[half(side), :], up_w[...])

        def gelu_rows(step, carry):
            at = pl.ds(pl.multiple_of(side + step * chunk, chunk), chunk)
            value, slope = gelu_pair(part_b[at, :] + up_bias)
            hidden_all[at, :] = value.astype(bf16)
            slope_all[at, :] = slope
            return carry

        lax.fori_loop(0, pair // chunk, gelu_rows, 0)

    with jax.named_scope("up_near"):
        raise_half(near)
    with jax.named_scope("share_second"):
        share_forward(second_all, second_sems)
        share_near(dy_all, dy_sems)
        share_deep(dy_all, dy_sems)
        share_deep(second_all, second_sems)
    with jax.named_scope("up_deep"):
        raise_half(deep)

    tile = 3 * LANES

    def outer(grad, left, right, lo, hi, more=None):
        def rows_of(step, carry):
            at = aligned(step * tile, tile)
            total = dot_left_t(left[:, at], right)
            if more is not None:
                total = total + dot_left_t(more[0][:, at], more[1])
            grad[at, lo:hi] = total.astype(bf16)
            return carry

        lax.fori_loop(0, D // tile, rows_of, 0)

    with jax.named_scope("weights_d2"):
        gather_forward(down_w, 0, down_w.shape[1], d_sems)
    with jax.named_scope("down_grad"):
        outer(down_g, dy_all, hidden_all[...], 0, down_g.shape[1])
        down_reduce = reduce_first(down_g, land_d, 0, down_g.shape[1])
    with jax.named_scope("weights_d3"):
        gather_finish(down_w, 0, down_w.shape[1], d_sems)

    def lower_half(side):
        part_b[half(side), :] = dot_plain(dy_all[half(side), :], down_w[...])

        def slope_rows(step, total):
            at = pl.ds(pl.multiple_of(side + step * chunk, chunk), chunk)
            low = (part_b[at, :] * slope_all[at, :]).astype(bf16)
            upper_all[at, :] = low
            return total + jnp.sum(low.astype(f32), axis=0, keepdims=True)

        return lax.fori_loop(
            0, pair // chunk, slope_rows, jnp.zeros((1, part_b.shape[1]), f32)
        )

    with jax.named_scope("lower_deep"):
        up_bias_sum = lower_half(deep)
        part_a[half(deep), :] = dot_right_t(upper_all[half(deep), :], up_w[...])
        second_sum_sems = sum_deep(1, part_a)
    with jax.named_scope("lower_near"):
        up_bias_sum = up_bias_sum + lower_half(near)
        vec_send[0, 6:7, :] = up_bias_sum
    with jax.named_scope("second_pass"):
        sum_pass(1, part_a, second_sum_sems)
    with jax.named_scope("second_near"):
        part_a[half(near), :] = dot_right_t(upper_all[half(near), :], up_w[...])
        sum_near(1, part_a, second_sum_sems)
    with jax.named_scope("up_grad"):
        outer(up_g, second_all, upper_all[...], 0, up_g.shape[1])
        up_reduce = reduce_first(up_g, land_u, 0, up_g.shape[1])
    with jax.named_scope("second_finish"):
        second_grad = sum_finish(1, part_a, second_sum_sems)
    with jax.named_scope("norm_two_back"):
        back, gain_sum, shift_sum = norm_back(
            second_grad, second_hat[...], row_scale[1][:, :1], second_gain
        )
        vec_send[0, 3:4, :] = gain_sum[None, :]
        vec_send[0, 4:5, :] = shift_sum[None, :]
        total = cotangent_ref[...].astype(f32) + back
        mid_grad[...] = total
        low = total.astype(bf16)
        mid_all[slot(near, c), :] = low
        vec_send[0, 2:3, :] = jnp.sum(low.astype(f32), axis=0, keepdims=True)
        mid_sems = share_start(mid_all)
    with jax.named_scope("mlp_out"):
        part_b[half(deep), :] = dot_right_t(hidden_all[half(deep), :], down_w[...])
        mlp_sems = sum_deep(2, part_b)
        part_b[half(near), :] = dot_right_t(hidden_all[half(near), :], down_w[...])
        sum_pass(2, part_b, mlp_sems)
        sum_near(2, part_b, mlp_sems)
    with jax.named_scope("down_reduce2"):
        reduce_second(down_g, land_d, 0, down_g.shape[1], down_reduce)

    def head_half(side_at):
        side_rows = slice(side_at * pair, (side_at + 1) * pair)
        done = dot_plain(mid_all[side_rows, :], attn_w[:, win:]).astype(bf16)
        for image in range(2):
            to = slice(image * pair + side_at * rows, image * pair + (side_at + 1) * rows)
            for head in range(heads):
                lo = win_shift + head * HD
                head_grads[head, to, :HD] = done[image * rows : (image + 1) * rows, lo : lo + HD]

    with jax.named_scope("share_mid"):
        share_forward(mid_all, mid_sems)
        share_near(mid_all, mid_sems)
        share_deep(mid_all, mid_sems)
    with jax.named_scope("head_grad"):
        head_half(0)
        head_half(1)
    with jax.named_scope("out_grad"):
        skip = qkv_lanes - win
        outer(attn_g, mid_all, mixed_all[:, skip:], qkv_lanes, all_lanes)
        out_reduce = reduce_first(attn_g, land_o, qkv_lanes, all_lanes)

    def attend_back(step, carry):
        head, span = image_head(step)
        queries, keys_part = head_rows[head, span, :], head_rows[heads + head, span, :]
        values, grads = head_rows[2 * heads + head, span, :], head_grads[head, span, :]
        probs = probs_all[step]
        value_grad = dot_left_t(probs.astype(bf16), grads)
        prob_grad = dot_right_t(grads, values)
        row_dot = jnp.sum(probs * prob_grad, axis=1, keepdims=True)
        score_grad = (probs * (prob_grad - row_dot)).astype(bf16)
        query_grad = dot_plain(score_grad, keys_part) * scale
        key_grad = dot_left_t(score_grad, queries) * scale
        head_rows[head, span, :] = query_grad.astype(bf16)
        head_rows[heads + head, span, :] = key_grad.astype(bf16)
        head_rows[2 * heads + head, span, :] = value_grad.astype(bf16)
        return carry

    with jax.named_scope("attend_back"):
        lax.fori_loop(0, 2 * heads, attend_back, 0)
    with jax.named_scope("pack_back"):
        pack(qkv_grads, head_rows, 3 * heads, 0)
    with jax.named_scope("first_deep"):
        part_a[half(deep), :] = dot_right_t(
            qkv_grads[half(deep), :qkv_lanes], attn_w[:, :qkv_lanes]
        )
        first_sum_sems = sum_deep(3, part_a)
        part_a[half(near), :] = dot_right_t(
            qkv_grads[half(near), :qkv_lanes], attn_w[:, :qkv_lanes]
        )
        sum_pass(3, part_a, first_sum_sems)
        sum_near(3, part_a, first_sum_sems)
    with jax.named_scope("qkv_grad"):
        outer(attn_g, first_all, qkv_grads[:, :win], 0, win)
        outer(
            attn_g,
            first_all,
            qkv_grads[:, win:qkv_lanes],
            win,
            qkv_lanes,
            more=(mid_all, mixed_all[:, :skip]),
        )
        qkv_reduce = reduce_first(attn_g, land_q, 0, qkv_lanes)
        vec_send[0, 7:8, :] = jnp.sum(qkv_grads[...].astype(f32), axis=0, keepdims=True)
    with jax.named_scope("mlp_finish"):
        mlp_rows = sum_finish(2, part_b, mlp_sems)
        layer_ref[...] = (mid_rows[...] + mlp_rows + down_bias).astype(bf16)
    with jax.named_scope("reduce_tail"):
        reduce_third(down_g, land_d, 0, down_g.shape[1], down_reduce)
        reduce_second(up_g, land_u, 0, up_g.shape[1], up_reduce)
        reduce_second(attn_g, land_o, qkv_lanes, all_lanes, out_reduce)
    with jax.named_scope("first_finish"):
        first_grad = sum_finish(3, part_a, first_sum_sems)
        back, gain_sum, shift_sum = norm_back(
            first_grad, first_hat[...], row_scale[0][:, :1], first_gain
        )
        input_grad_ref[...] = mid_grad[...] + back
        vec_send[0, 0:1, :] = gain_sum[None, :]
        vec_send[0, 1:2, :] = shift_sum[None, :]

    def vector_step(step, device):
        sem = new_sem()
        remote(vec_send.at[step], vec_land.at[step], device, sem)
        return sem

    def vector_add(step, sem):
        arrived(vec_land.at[step], sem)
        vec_send[step + 1] = vec_send[step] + vec_land[step]

    with jax.named_scope("vec_x"):
        sem = vector_step(0, dev_x)
        reduce_second(attn_g, land_q, 0, qkv_lanes, qkv_reduce)
        vector_add(0, sem)
    with jax.named_scope("vec_y"):
        sem = vector_step(1, dev_y)
        reduce_third(up_g, land_u, 0, up_g.shape[1], up_reduce)
        reduce_third(attn_g, land_o, qkv_lanes, all_lanes, out_reduce)
        vector_add(1, sem)
    with jax.named_scope("vec_far"):
        sem = vector_step(2, dev_far)
        down_grad_ref[...] = reduce_finish(land_d, down_reduce)
        vector_add(2, sem)
    with jax.named_scope("vec_z"):
        sem = vector_step(3, dev_z)
        reduce_third(attn_g, land_q, 0, qkv_lanes, qkv_reduce)
        arrived(vec_land.at[3], sem)
        vec_send[4, 0:6, :] = vec_send[3, 0:6, :] + vec_land[3, 0:6, :]
        vec_send[4, 6:8, :] = vec_send[3, 6:8, :]
    with jax.named_scope("vec_c"):
        sem = vector_step(4, dev_c)
        up_grad_ref[...] = reduce_finish(land_u, up_reduce)
        attn_grad_ref[:, qkv_lanes:all_lanes] = reduce_finish(land_o, out_reduce)
        arrived(vec_land.at[4], sem)
        vector_grad_ref[0:6, :] = vec_send[4, 0:6, :] + vec_land[4, 0:6, :]
        vector_grad_ref[6:8, :] = jnp.where(home, vec_send[4, 6:8, :], vec_land[4, 6:8, :])
    with jax.named_scope("last"):
        attn_grad_ref[:, :qkv_lanes] = reduce_finish(land_q, qkv_reduce)

    with jax.named_scope("drain"):
        for copy, when in pending:
            if when is None:
                copy.wait_send()
            else:
                pl.when(when)(copy.wait_send)


def fused_step(
    tokens,
    cotangent,
    first_gain,
    first_shift,
    query_weight,
    key_weight,
    value_weight,
    query_bias,
    value_bias,
    out_weight,
    out_bias,
    second_gain,
    second_shift,
    up_weight,
    up_bias,
    down_weight,
    down_bias,
):
    bf16, f32 = jnp.bfloat16, jnp.float32
    rows, piece, width, units = (
        tokens.shape[0],
        query_weight.shape[0],
        query_weight.shape[1],
        up_weight.shape[1],
    )
    heads = width // HD
    group = 4 * rows
    qkv_lanes = round_up(3 * width, LANES)
    attn_lanes = round_up(4 * width, LANES)
    ff_lanes = round_up(units, LANES)
    win = 3 * width // LANES * LANES

    def padded(array, lanes):
        return jnp.pad(array, ((0, 0), (0, lanes - array.shape[1])))

    attn_piece = padded(
        jnp.concatenate((query_weight, key_weight, value_weight, out_weight.T), axis=1),
        attn_lanes,
    )
    up_piece = padded(up_weight, ff_lanes)
    down_piece = padded(down_weight.T, ff_lanes)
    qkv_bias = jnp.concatenate((query_bias, jnp.zeros_like(query_bias), value_bias))
    vectors = jnp.stack(
        (
            first_gain,
            first_shift,
            out_bias,
            second_gain,
            second_shift,
            down_bias,
            jnp.pad(qkv_bias, (0, D - 3 * width)),
            jnp.pad(up_bias, (0, D - units)),
        )
    )
    vmem = pl.BlockSpec(memory_space=pltpu.VMEM)
    place = pl.BlockSpec(memory_space=pl.ANY)
    sem_count = 128
    o_lanes = attn_lanes - qkv_lanes
    scratch = [
        pltpu.VMEM((D, attn_lanes), bf16),
        pltpu.VMEM((D, ff_lanes), bf16),
        pltpu.VMEM((D, ff_lanes), bf16),
        pltpu.VMEM((D, attn_lanes), bf16),
        pltpu.VMEM((D, ff_lanes), bf16),
        pltpu.VMEM((D, ff_lanes), bf16),
        pltpu.VMEM((8, piece, o_lanes), bf16),
        pltpu.VMEM((8, piece, qkv_lanes), bf16),
        pltpu.VMEM((8, piece, ff_lanes), bf16),
        pltpu.VMEM((8, piece, ff_lanes), bf16),
        pltpu.VMEM((group, D), bf16),
        pltpu.VMEM((group, D), bf16),
        pltpu.VMEM((group, D), bf16),
        pltpu.VMEM((group, D), bf16),
        pltpu.VMEM((3 * heads, group, LANES), bf16),
        pltpu.VMEM((heads, group, LANES), bf16),
        pltpu.VMEM((2 * heads, 2 * rows, 2 * rows), f32),
        pltpu.VMEM((heads, group, LANES), bf16),
        pltpu.VMEM((group, attn_lanes - win), bf16),
        pltpu.VMEM((group, ff_lanes), bf16),
        pltpu.VMEM((group, ff_lanes), f32),
        pltpu.VMEM((group, ff_lanes), bf16),
        pltpu.VMEM((group, attn_lanes), bf16),
        pltpu.VMEM((group, D), f32),
        pltpu.VMEM((group, D), f32),
        pltpu.VMEM((4, 2, rows, D), bf16),
        pltpu.VMEM((4, 2, rows, D), bf16),
        pltpu.VMEM((4, rows, D), bf16),
        pltpu.VMEM((4, rows, D), bf16),
        pltpu.VMEM((rows, D), f32),
        pltpu.VMEM((rows, D), f32),
        pltpu.VMEM((rows, D), f32),
        pltpu.VMEM((rows, D), f32),
        pltpu.VMEM((2, rows, LANES), f32),
        pltpu.VMEM((5, 8, D), f32),
        pltpu.VMEM((5, 8, D), f32),
        pltpu.VMEM((8, D), f32),
        pltpu.SemaphoreType.DMA((sem_count,)),
        pltpu.SemaphoreType.DMA((sem_count,)),
    ]
    shapes = (rows, heads, width, qkv_lanes, piece)

    def body(*refs):
        layer_kernel(shapes, *refs)

    layer_out, input_grad, attn_grad, up_grad, down_grad, vector_grad = pl.pallas_call(
        body,
        out_shape=(
            jax.ShapeDtypeStruct((rows, D), bf16),
            jax.ShapeDtypeStruct((rows, D), f32),
            jax.ShapeDtypeStruct((piece, attn_lanes), f32),
            jax.ShapeDtypeStruct((piece, ff_lanes), f32),
            jax.ShapeDtypeStruct((piece, ff_lanes), f32),
            jax.ShapeDtypeStruct((8, D), f32),
        ),
        in_specs=[vmem, vmem, vmem, place, place, place],
        out_specs=(vmem,) * 6,
        scratch_shapes=scratch,
        compiler_params=pltpu.CompilerParams(
            collective_id=0, has_side_effects=True, vmem_limit_bytes=67043328
        ),
        name="layer",
    )(tokens, cotangent, vectors, attn_piece, up_piece, down_piece)
    return (
        layer_out,
        input_grad,
        vector_grad[0],
        vector_grad[1],
        attn_grad[:, :width],
        attn_grad[:, width : 2 * width],
        attn_grad[:, 2 * width : 3 * width],
        vector_grad[7, :width],
        vector_grad[7, 2 * width : 3 * width],
        attn_grad[:, 3 * width : 4 * width].T,
        vector_grad[2],
        vector_grad[3],
        vector_grad[4],
        up_grad[:, :units],
        vector_grad[6, :units],
        down_grad[:, :units].T,
        vector_grad[5],
    )


def pick_step(mesh):
    if mesh.shape["fsdp"] == 8 and mesh.shape["tensor"] == 4:
        return fused_step
    return on_device


def solution(mesh):
    return jax.shard_map(
        pick_step(mesh),
        mesh=mesh,
        in_specs=(
            P(("fsdp", "tensor"), None),
            P(("fsdp", "tensor"), None),
            P(),
            P(),
            P("fsdp", "tensor"),
            P("fsdp", "tensor"),
            P("fsdp", "tensor"),
            P("tensor"),
            P("tensor"),
            P("tensor", "fsdp"),
            P(),
            P(),
            P(),
            P("fsdp", "tensor"),
            P("tensor"),
            P("tensor", "fsdp"),
            P(),
        ),
        out_specs=(
            P(("fsdp", "tensor"), None),
            P(("fsdp", "tensor"), None),
            P(),
            P(),
            P("fsdp", "tensor"),
            P("fsdp", "tensor"),
            P("fsdp", "tensor"),
            P("tensor"),
            P("tensor"),
            P("tensor", "fsdp"),
            P(),
            P(),
            P(),
            P("fsdp", "tensor"),
            P("tensor"),
            P("tensor", "fsdp"),
            P(),
        ),
        check_vma=False,
    )
```

```python
import math
from types import SimpleNamespace

import jax
import jax.numpy as jnp
from jax import lax
from jax.experimental import pallas as pl
from jax.experimental.pallas import tpu as pltpu
from jax.sharding import PartitionSpec as P

D = 1152
HD = 72
FF = 4304
SEQ = 256


norm_eps = 1e-06
gelu_coef = 0.7978845608028654
cubic_coef = 0.044715


def dot_plain(left, right):
    return jnp.dot(left, right, preferred_element_type=jnp.float32)


def dot_right_t(left, right):
    return lax.dot_general(
        left, right, (((1,), (1,)), ((), ())), preferred_element_type=jnp.float32
    )


def dot_left_t(left, right):
    return lax.dot_general(
        left, right, (((0,), (0,)), ((), ())), preferred_element_type=jnp.float32
    )


def norm_rows(values, gain, shift):
    row_mean = jnp.mean(values, axis=1, keepdims=True)
    centred = values - row_mean
    inv_scale = lax.rsqrt(jnp.mean(centred * centred, axis=1, keepdims=True) + norm_eps)
    normed = centred * inv_scale
    return (normed * gain + shift, normed, inv_scale)


def norm_back(out_grad, normed, inv_scale, gain):
    scaled_grad = out_grad * gain
    grad_mean = jnp.mean(scaled_grad, axis=1, keepdims=True)
    cross_mean = jnp.mean(scaled_grad * normed, axis=1, keepdims=True)
    in_grad = inv_scale * (scaled_grad - grad_mean - normed * cross_mean)
    return (in_grad, jnp.sum(out_grad * normed, axis=0), jnp.sum(out_grad, axis=0))


def gelu_pair(upper):
    tangent = jnp.tanh(gelu_coef * (upper + cubic_coef * upper * upper * upper))
    gelu_value = 0.5 * upper * (1.0 + tangent)
    gelu_slope = 0.5 * (1.0 + tangent) + 0.5 * upper * (1.0 - tangent * tangent) * gelu_coef * (
        1.0 + 3.0 * cubic_coef * upper * upper
    )
    return (gelu_value, gelu_slope)


def split_heads(block_rows, head_count):
    col_width = block_rows.shape[1] // 3
    img_count = block_rows.shape[0] // SEQ
    shape_four = (img_count, SEQ, head_count, HD)
    queries = block_rows[:, :col_width].reshape(shape_four)
    keys_part = block_rows[:, col_width : 2 * col_width].reshape(shape_four)
    values = block_rows[:, 2 * col_width :].reshape(shape_four)
    return (queries, keys_part, values, shape_four)


def attend_forward(block_rows, head_count):
    queries, keys_part, values, shape_four = split_heads(block_rows, head_count)
    scores = jnp.einsum(
        "nqhd,nkhd->nhqk", queries, keys_part, preferred_element_type=jnp.float32
    ) * HD ** (-0.5)
    peak = jnp.max(scores, axis=-1, keepdims=True)
    expo = jnp.exp(scores - peak)
    totals = jnp.sum(expo, axis=-1, keepdims=True)
    prob_low = (expo / totals).astype(jnp.bfloat16)
    mixed = jnp.einsum("nhqk,nkhd->nqhd", prob_low, values, preferred_element_type=jnp.float32)
    row_total = block_rows.shape[0]
    mixed = mixed.reshape(row_total, head_count * HD).astype(jnp.bfloat16)
    return (mixed, (peak + jnp.log(totals))[..., 0])


def attend_backward(inputs, head_count):
    block_rows, grad_block, log_total = inputs
    queries, keys_part, values, shape_four = split_heads(block_rows, head_count)
    grad_out = grad_block.reshape(shape_four)
    scores = jnp.einsum(
        "nqhd,nkhd->nhqk", queries, keys_part, preferred_element_type=jnp.float32
    ) * HD ** (-0.5)
    probs = jnp.exp(scores - log_total[..., None])
    prob_low = probs.astype(jnp.bfloat16)
    value_grad = jnp.einsum(
        "nhqk,nqhd->nkhd", prob_low, grad_out, preferred_element_type=jnp.float32
    )
    prob_grad = jnp.einsum("nqhd,nkhd->nhqk", grad_out, values, preferred_element_type=jnp.float32)
    row_dot = jnp.sum(probs * prob_grad, axis=-1, keepdims=True)
    score_grad = (probs * (prob_grad - row_dot)).astype(jnp.bfloat16)
    query_grad = jnp.einsum(
        "nhqk,nkhd->nqhd", score_grad, keys_part, preferred_element_type=jnp.float32
    ) * HD ** (-0.5)
    key_grad = jnp.einsum(
        "nhqk,nqhd->nkhd", score_grad, queries, preferred_element_type=jnp.float32
    ) * HD ** (-0.5)
    row_total = block_rows.shape[0]
    col_width = head_count * HD
    return jnp.concatenate(
        (
            query_grad.reshape(row_total, col_width),
            key_grad.reshape(row_total, col_width),
            value_grad.reshape(row_total, col_width),
        ),
        axis=1,
    ).astype(jnp.bfloat16)


def on_device(
    tokens,
    cotangent,
    first_gain,
    first_shift,
    query_weight,
    key_weight,
    value_weight,
    query_bias,
    value_bias,
    out_weight,
    out_bias,
    second_gain,
    second_shift,
    up_weight,
    up_bias,
    down_weight,
    down_bias,
):
    full_query, full_key, full_value, full_outp, full_up, full_down = (
        lax.all_gather(query_weight, "fsdp", axis=0, tiled=True),
        lax.all_gather(key_weight, "fsdp", axis=0, tiled=True),
        lax.all_gather(value_weight, "fsdp", axis=0, tiled=True),
        lax.all_gather(out_weight, "fsdp", axis=1, tiled=True),
        lax.all_gather(up_weight, "fsdp", axis=0, tiled=True),
        lax.all_gather(down_weight, "fsdp", axis=1, tiled=True),
    )
    qkv_weight = jnp.concatenate((full_query, full_key, full_value), axis=1)
    local_width = full_query.shape[1]
    ffn_width = full_up.shape[1]
    head_count = local_width // HD
    token_rows = tokens.astype(jnp.float32)
    first_out, first_hat, first_scale = norm_rows(token_rows, first_gain, first_shift)
    all_first = lax.all_gather(first_out.astype(jnp.bfloat16), "tensor", axis=0, tiled=True)
    qkv_bias = jnp.concatenate((query_bias, jnp.zeros_like(query_bias), value_bias))
    qkv_rows = (dot_plain(all_first, qkv_weight) + qkv_bias).astype(jnp.bfloat16)
    group_rows = qkv_rows.shape[0]
    images = group_rows // SEQ
    per_block = math.gcd(images, max(1, 512 // SEQ))
    blocks = images // per_block
    stacked = qkv_rows.reshape(blocks, per_block * SEQ, 3 * local_width)

    def forward_block(block_rows):
        return attend_forward(block_rows, head_count)

    head_out, log_total = lax.map(forward_block, stacked)
    head_out = head_out.reshape(group_rows, local_width)
    attn_rows = lax.psum_scatter(
        dot_plain(head_out, full_outp), "tensor", scatter_dimension=0, tiled=True
    )
    mid_rows = token_rows + attn_rows + out_bias
    second_out, second_hat, second_scale = norm_rows(mid_rows, second_gain, second_shift)
    all_second = lax.all_gather(second_out.astype(jnp.bfloat16), "tensor", axis=0, tiled=True)
    up_pre = dot_plain(all_second, full_up) + up_bias
    hidden_value, hidden_slope = gelu_pair(up_pre)
    hidden_low = hidden_value.astype(jnp.bfloat16)
    mlp_rows = lax.psum_scatter(
        dot_plain(hidden_low, full_down).astype(jnp.bfloat16),
        "tensor",
        scatter_dimension=0,
        tiled=True,
    ).astype(jnp.float32)
    layer_out = (mid_rows + mlp_rows + down_bias).astype(jnp.bfloat16)
    out_grad = cotangent.astype(jnp.float32)
    all_out_grad = lax.all_gather(cotangent, "tensor", axis=0, tiled=True)
    down_grad = dot_left_t(hidden_low, all_out_grad)
    hidden_grad = dot_right_t(all_out_grad, full_down)
    upper_low = (hidden_grad * hidden_slope).astype(jnp.bfloat16)
    up_bias_grad = jnp.sum(upper_low.astype(jnp.float32), axis=0)
    up_grad = dot_left_t(all_second, upper_low)
    second_grad = lax.psum_scatter(
        dot_right_t(upper_low, full_up), "tensor", scatter_dimension=0, tiled=True
    )
    back_second, second_gain_grad, second_shift_grad = norm_back(
        second_grad, second_hat, second_scale, second_gain
    )
    mid_grad = out_grad + back_second
    mid_low = mid_grad.astype(jnp.bfloat16)
    all_mid_grad = lax.all_gather(mid_low, "tensor", axis=0, tiled=True)
    outp_grad = dot_left_t(head_out, all_mid_grad)
    head_grad = dot_right_t(all_mid_grad, full_outp).astype(jnp.bfloat16)

    def backward_block(inputs):
        return attend_backward(inputs, head_count)

    qkv_grad = lax.map(
        backward_block,
        (stacked, head_grad.reshape(blocks, per_block * SEQ, local_width), log_total),
    )
    qkv_grad = qkv_grad.reshape(group_rows, 3 * local_width)
    qkv_weight_grad = dot_left_t(all_first, qkv_grad)
    qkv_bias_grad = jnp.sum(qkv_grad.astype(jnp.float32), axis=0)
    first_grad = lax.psum_scatter(
        dot_right_t(qkv_grad, qkv_weight).astype(jnp.bfloat16),
        "tensor",
        scatter_dimension=0,
        tiled=True,
    ).astype(jnp.float32)
    back_first, first_gain_grad, first_shift_grad = norm_back(
        first_grad, first_hat, first_scale, first_gain
    )
    input_grad = mid_grad + back_first
    out_bias_grad = jnp.sum(mid_low.astype(jnp.float32), axis=0)
    down_bias_grad = jnp.sum(out_grad, axis=0)
    small_terms = jnp.concatenate(
        (
            first_gain_grad,
            first_shift_grad,
            out_bias_grad,
            second_gain_grad,
            second_shift_grad,
            down_bias_grad,
        )
    )
    tensor_index = lax.axis_index("tensor")
    head_terms = jnp.zeros((2 * D + FF,), jnp.float32)
    head_terms = lax.dynamic_update_slice(
        head_terms, qkv_bias_grad[:local_width], (tensor_index * local_width,)
    )
    head_terms = lax.dynamic_update_slice(
        head_terms, qkv_bias_grad[2 * local_width :], (D + tensor_index * local_width,)
    )
    head_terms = lax.dynamic_update_slice(
        head_terms, up_bias_grad, (2 * D + tensor_index * ffn_width,)
    )
    small_sums, head_sums = lax.psum((small_terms, head_terms), ("fsdp", "tensor"))
    query_bias_total = lax.dynamic_slice(head_sums, (tensor_index * local_width,), (local_width,))
    value_bias_total = lax.dynamic_slice(
        head_sums, (D + tensor_index * local_width,), (local_width,)
    )
    up_bias_total = lax.dynamic_slice(head_sums, (2 * D + tensor_index * ffn_width,), (ffn_width,))
    query_part, key_part, value_part, outp_part, up_part, down_part = (
        lax.psum_scatter(qkv_weight_grad[:, :local_width], "fsdp", scatter_dimension=0, tiled=True),
        lax.psum_scatter(
            qkv_weight_grad[:, local_width : 2 * local_width],
            "fsdp",
            scatter_dimension=0,
            tiled=True,
        ),
        lax.psum_scatter(
            qkv_weight_grad[:, 2 * local_width :], "fsdp", scatter_dimension=0, tiled=True
        ),
        lax.psum_scatter(outp_grad, "fsdp", scatter_dimension=1, tiled=True),
        lax.psum_scatter(up_grad, "fsdp", scatter_dimension=0, tiled=True),
        lax.psum_scatter(down_grad, "fsdp", scatter_dimension=1, tiled=True),
    )
    return (
        layer_out,
        input_grad,
        small_sums[0:D],
        small_sums[D : 2 * D],
        query_part,
        key_part,
        value_part,
        query_bias_total,
        value_bias_total,
        outp_part,
        small_sums[2 * D : 3 * D],
        small_sums[3 * D : 4 * D],
        small_sums[4 * D : 5 * D],
        up_part,
        up_bias_total,
        down_part,
        small_sums[5 * D : 6 * D],
    )


MESH_IDS = pl.DeviceIdType.MESH
LANES = 128


def round_up(value, step):
    return -(-value // step) * step


def row_cuts(count, parts):
    edges = [min(count, round_up(count * at // parts, 16)) for at in range(parts + 1)]
    return list(zip(edges[:-1], edges[1:]))


class Remote:
    def __init__(self, send_sems, recv_sems):
        self.send_sems, self.recv_sems = send_sems, recv_sems
        self.used = 0
        self.pending = []

    def sem(self):
        self.used += 1
        return self.used - 1

    def sems(self, count):
        return [self.sem() for _ in range(count)]

    def send(self, src, dst, device, sem, recv=None, when=None):
        copy = pltpu.make_async_remote_copy(
            src_ref=src,
            dst_ref=dst,
            send_sem=self.send_sems.at[sem],
            recv_sem=self.recv_sems.at[sem if recv is None else recv],
            device_id=device,
            device_id_type=MESH_IDS,
        )
        if when is None:
            copy.start()
        else:
            pl.when(when)(copy.start)
        self.pending.append((copy, when))

    def local(self, src, dst, sem, when):
        copy = pltpu.make_async_copy(src, dst, self.recv_sems.at[sem])
        pl.when(when)(copy.start)

    def arrived(self, dst, sem):
        pltpu.make_async_copy(dst, dst, self.recv_sems.at[sem]).wait()

    def drain(self):
        for copy, when in self.pending:
            if when is None:
                copy.wait_send()
            else:
                pl.when(when)(copy.wait_send)


def layer_kernel(shapes, names, *refs):
    rows, heads, width, units, qkv_lanes, piece = shapes
    inputs, outputs, scratch = names
    hbm = SimpleNamespace(**dict(zip(inputs, refs[: len(inputs)], strict=True)))
    refs = refs[len(inputs) :]
    out = SimpleNamespace(**dict(zip(outputs, refs[: len(outputs)], strict=True)))
    refs = refs[len(outputs) :]
    held = SimpleNamespace(**dict(zip(inputs, refs[: len(inputs)], strict=True)))
    refs = refs[len(inputs) :]
    ref = SimpleNamespace(**dict(zip(scratch, refs, strict=True)))
    bf16, f32 = jnp.bfloat16, jnp.float32
    attn_w, up_w, down_w = ref.attn_w, ref.up_w, ref.down_w
    attn_g, up_g, down_g = ref.attn_g, ref.up_g, ref.down_g
    first_all, second_all = ref.first_all, ref.second_all
    dy_all, mid_all = ref.dy_all, ref.mid_all
    head_rows, head_grads = ref.head_rows, ref.head_grads
    mixed_all, hidden_all, upper_all = ref.mixed_all, ref.hidden_all, ref.upper_all
    slope_all, qkv_grads = ref.slope_all, ref.qkv_grads
    part_a, part_b, vectors = ref.part_a, ref.part_b, ref.vectors
    pair, fourth = 2 * rows, rows // 2
    out_base = 3 * width
    win = out_base // LANES * LANES
    win_shift = out_base - win
    skip = qkv_lanes - win
    all_lanes, ff_lanes = attn_w.shape[1], up_w.shape[1]

    f = lax.axis_index("fsdp")
    t = lax.axis_index("tensor")
    c, k = lax.rem(f, 2), lax.div(f, 2)
    kx, ky = lax.rem(k, 2), lax.div(k, 2)
    zl, zh = lax.rem(t, 2), lax.div(t, 2)
    oc, ox = 1 - c, 1 - kx
    k_x, k_y, k_d = ky * 2 + ox, (1 - ky) * 2 + kx, (1 - ky) * 2 + ox
    home = c == zh
    away = jnp.logical_not(home)
    stay = kx == zh
    outer = zl == zh
    inner = jnp.logical_not(outer)
    move = jnp.logical_not(stay)
    far_t = (1 - zh) * 2 + zl
    dev_x = {"fsdp": 2 * k_x + c, "tensor": t}
    dev_y = {"fsdp": 2 * k_y + c, "tensor": t}
    dev_c = {"fsdp": 2 * k + oc, "tensor": t}
    dev_z = {"fsdp": f, "tensor": zh * 2 + (1 - zl)}
    dev_far = {"fsdp": f, "tensor": far_t}
    dev_far_other = {"fsdp": 2 * k + oc, "tensor": far_t}
    net = Remote(ref.send_sems, ref.recv_sems)

    def aligned(start, size):
        return pl.ds(pl.multiple_of(start, math.gcd(size, LANES)), size)

    def piece_at(index):
        return pl.ds(pl.multiple_of(index * piece, piece), piece)

    def block(buf, index, lo=0, hi=None):
        return buf.at[piece_at(index), lo : buf.shape[1] if hi is None else hi]

    near, deep = zl * pair, (1 - zl) * pair

    def slot(side, place):
        return aligned(side + place * rows, rows)

    def spread_start(src, buf, lo, hi):
        base, other = net.sems(2)
        source, target = src.at[:, lo:hi], block(buf, f, lo, hi)
        net.local(source, target, base + c, home)
        to = {"fsdp": 2 * k + zh, "tensor": t}
        net.send(source, target, to, base, recv=base + c, when=away)
        to = {"fsdp": 2 * k + zh, "tensor": far_t}
        net.send(source, target, to, other, recv=base + c)
        return base

    def gather_start(buf, lo, hi, base):
        sems = net.sems(6)
        a_own, b_own = block(buf, 2 * k, lo, hi), block(buf, 2 * k + 1, lo, hi)
        net.arrived(a_own, base)
        net.send(a_own, a_own, dev_x, sems[0])
        net.arrived(b_own, base + 1)
        net.send(b_own, b_own, dev_y, sems[1])
        net.send(a_own, a_own, dev_y, sems[2])
        net.send(b_own, b_own, dev_x, sems[3])
        return sems

    def gather_forward(buf, lo, hi, sems):
        a_x, b_y = block(buf, 2 * k_x, lo, hi), block(buf, 2 * k_y + 1, lo, hi)
        net.arrived(a_x, sems[0])
        net.send(a_x, a_x, dev_y, sems[4])
        net.arrived(b_y, sems[1])
        net.send(b_y, b_y, dev_x, sems[5])

    def gather_finish(buf, lo, hi, sems):
        net.arrived(block(buf, 2 * k_y, lo, hi), sems[2])
        net.arrived(block(buf, 2 * k_x + 1, lo, hi), sems[3])
        net.arrived(block(buf, 2 * k_d, lo, hi), sems[4])
        net.arrived(block(buf, 2 * k_d + 1, lo, hi), sems[5])

    f_x, f_y, f_d = 2 * k_x + c, 2 * k_y + c, 2 * k_d + c

    class WideGather:
        def __init__(self, src, buf, wait_at, lo, hi):
            self.buf, self.lo, self.size = buf, lo, hi - lo
            self.src, self.wait_at = src.at[lo:hi, :], wait_at.at[lo:hi, :]
            self.sems = net.sems(9)

        def at(self, index):
            start = pl.multiple_of(index * piece + self.lo, 16)
            return self.buf.at[pl.ds(start, self.size), :]

        def start(self, when):
            own, sems = self.at(f), self.sems
            stay_now, move_now = jnp.logical_and(stay, when), jnp.logical_and(move, when)
            net.local(self.src, own, sems[8], stay_now)
            net.send(self.src, own, dev_far, sems[0], when=stay_now)
            net.send(self.src, self.wait_at, dev_far, sems[0], when=move_now)

        def beside(self):
            net.send(self.src, self.at(f), dev_x, self.sems[1], when=move)

        def second(self):
            own, sems = self.at(f), self.sems

            @pl.when(stay)
            def _():
                net.arrived(self.wait_at, sems[0])

            @pl.when(move)
            def _():
                net.arrived(own, sems[0])

            net.send(self.wait_at, own, dev_x, sems[1], when=stay)

            @pl.when(stay)
            def _():
                net.arrived(own, sems[8])

            net.send(own, own, dev_y, sems[2])
            net.send(own, own, dev_c, sems[4])

        def third(self):
            got = self.at(f_x)
            net.arrived(got, self.sems[1])
            net.send(got, got, dev_y, self.sems[3])
            net.send(got, got, dev_c, self.sems[5])

        def fourth(self):
            for index, sem, to in ((f_y, 2, 6), (f_d, 3, 7)):
                got = self.at(index)
                net.arrived(got, self.sems[sem])
                net.send(got, got, dev_c, self.sems[to])

        def finish(self):
            for index, sem in ((f, 4), (f_x, 5), (f_y, 6), (f_d, 7)):
                net.arrived(self.at(index + oc - c), self.sems[sem])

    def share_start(buf):
        sems = net.sems(3)
        own = buf.at[slot(near, c)]
        net.send(own, own, dev_z, sems[0])
        net.send(own, own, dev_c, sems[1])
        return sems

    def share_near(buf, sems):
        net.arrived(buf.at[slot(near, oc)], sems[1])

    def share_forward(buf, sems):
        got = buf.at[slot(deep, c)]
        net.arrived(got, sems[0])
        net.send(got, got, dev_c, sems[2])

    def share_deep(buf, sems):
        net.arrived(buf.at[slot(deep, oc)], sems[2])

    def sum_deep(which, part):
        sems = net.sems(3)
        send = ref.core_send.at[which, 0]
        send[...] = part[slot(deep, oc), :].astype(bf16)
        net.send(send, ref.core_land.at[which, 0], dev_c, sems[0])
        return sems

    def sum_pass(which, part, sems):
        land, send = ref.core_land.at[which, 0], ref.deep_send.at[which]
        net.arrived(land, sems[0])
        send[...] = (part[slot(deep, c), :] + land[...].astype(f32)).astype(bf16)
        net.send(send, ref.deep_land.at[which], dev_z, sems[1])

    def sum_near(which, part, sems):
        send = ref.core_send.at[which, 1]
        send[...] = part[slot(near, oc), :].astype(bf16)
        net.send(send, ref.core_land.at[which, 1], dev_c, sems[2])

    def sum_finish(which, part, sems):
        beside, across = ref.core_land.at[which, 1], ref.deep_land.at[which]
        net.arrived(beside, sems[2])
        total = part[slot(near, c), :] + beside[...].astype(f32)
        net.arrived(across, sems[1])
        return total + across[...].astype(f32)

    def quarter(side, place, which):
        return aligned(side + place * rows + which * fourth, fourth)

    def wide_share_start(buf):
        sems = net.sems(6)
        first, second = buf.at[quarter(near, kx, 0)], buf.at[quarter(near, kx, 1)]
        net.send(first, first, dev_z, sems[0])
        net.send(second, second, dev_x, sems[1])
        net.send(second, second, dev_z, sems[2])
        net.send(first, first, dev_x, sems[3])
        return sems

    def wide_share_forward(buf, sems):
        from_z, from_x = buf.at[quarter(deep, kx, 0)], buf.at[quarter(near, ox, 1)]
        net.arrived(from_z, sems[0])
        net.send(from_z, from_z, dev_x, sems[4])
        net.arrived(from_x, sems[1])
        net.send(from_x, from_x, dev_z, sems[5])

    def wide_share_near(buf, sems):
        net.arrived(buf.at[quarter(near, ox, 0)], sems[3])

    def wide_share_deep(buf, sems):
        net.arrived(buf.at[quarter(deep, kx, 1)], sems[2])
        net.arrived(buf.at[quarter(deep, ox, 0)], sems[4])
        net.arrived(buf.at[quarter(deep, ox, 1)], sems[5])

    def plain_share_z(buf):
        sems = net.sems(3)
        own = buf.at[slot(near, kx)]
        net.send(own, own, dev_z, sems[0])
        return sems

    def plain_share_x(buf, sems):
        own = buf.at[slot(near, kx)]
        net.send(own, own, dev_x, sems[1])

    def plain_share_forward(buf, sems):
        got = buf.at[slot(near, ox)]
        net.arrived(got, sems[1])
        net.send(got, got, dev_z, sems[2])

    def plain_share_finish(buf, sems):
        net.arrived(buf.at[slot(deep, kx)], sems[0])
        net.arrived(buf.at[slot(deep, ox)], sems[2])

    def wide_send(which, number):
        return ref.wide_send.at[which, number]

    def wide_land(which, number):
        return ref.wide_land.at[which, number]

    def wide_push(which, number, value, device, sem):
        wide_send(which, number)[...] = value.astype(bf16)
        net.send(wide_send(which, number), wide_land(which, number), device, sem)

    def wide_sum_deep(which, part):
        sems = net.sems(6)
        wide_push(which, 0, part[quarter(deep, ox, 0), :], dev_x, sems[0])
        wide_push(which, 1, part[quarter(deep, ox, 1), :], dev_z, sems[1])
        wide_push(which, 2, part[quarter(deep, kx, 1), :], dev_z, sems[2])
        return sems

    def wide_sum_near(which, part, sems):
        wide_push(which, 3, part[quarter(near, ox, 0), :], dev_x, sems[3])

    def wide_sum_pass(which, part, sems):
        net.arrived(wide_land(which, 0), sems[0])
        total = part[quarter(deep, kx, 0), :] + wide_land(which, 0)[...].astype(f32)
        wide_push(which, 4, total, dev_z, sems[4])
        net.arrived(wide_land(which, 1), sems[1])
        total = part[quarter(near, ox, 1), :] + wide_land(which, 1)[...].astype(f32)
        wide_push(which, 5, total, dev_x, sems[5])

    def wide_sum_finish(which, part, sems):
        halves = []
        for half_at, (by_z, by_x) in enumerate(((4, 3), (2, 5))):
            net.arrived(wide_land(which, by_z), sems[by_z])
            net.arrived(wide_land(which, by_x), sems[by_x])
            halves.append(
                part[quarter(near, kx, half_at), :]
                + wide_land(which, by_z)[...].astype(f32)
                + wide_land(which, by_x)[...].astype(f32)
            )
        return jnp.concatenate(halves, axis=0)

    def add_into(grad, index, lo, hi, land):
        at = piece_at(index)
        total = grad[at, lo:hi].astype(f32) + land[...].astype(f32)
        grad[at, lo:hi] = total.astype(bf16)

    def guarded(when, action):
        if when is None:
            action()
        else:
            pl.when(when)(action)

    def reduce_route(core, by_y):
        if core == 0 or by_y:
            return dev_y, 2 * k_y + core, 2 * k_x + core, dev_x
        return dev_x, 2 * k_x + core, 2 * k_y + core, dev_y

    def reduce_first(grad, land, lo, hi, sems, by_y=False, when=None):
        for distant in (True, False):
            for core in range(2):
                device, index, _, _ = reduce_route(core, by_y)
                index, number = (2 * k_d + core, 1 + 2 * core) if distant else (index, 2 * core)
                source = block(grad, index, lo, hi)
                net.send(source, land.at[number], device, sems[number], when=when)

    def reduce_second(grad, land, lo, hi, sems, by_y=False, when=None):
        def collect(index, number):
            def action():
                net.arrived(land.at[number], sems[number])
                add_into(grad, index, lo, hi, land.at[number])

            guarded(when, action)

        for core in range(2):
            _, _, index, device = reduce_route(core, by_y)
            collect(index, 1 + 2 * core)
            source = block(grad, index, lo, hi)
            net.send(source, land.at[4 + core], device, sems[4 + core], when=when)
        for core in range(2):
            collect(2 * k + core, 2 * core)

    def reduce_third(grad, land, lo, hi, sems):
        for core in range(2):
            net.arrived(land.at[4 + core], sems[4 + core])
            add_into(grad, 2 * k + core, lo, hi, land.at[4 + core])
            source = block(grad, 2 * k + core, lo, hi)
            mine, other = jnp.logical_and(home, c == core), jnp.logical_and(home, c != core)
            net.local(source, land.at[6], sems[6], mine)
            to = {"fsdp": 2 * k + core, "tensor": t}
            net.send(source, land.at[6], to, sems[8], recv=sems[6], when=other)
            to = {"fsdp": 2 * k + core, "tensor": far_t}
            net.send(source, land.at[7], to, sems[6 + core], recv=sems[7], when=away)

    def reduce_finish(land, sems):
        net.arrived(land.at[6], sems[6])
        net.arrived(land.at[7], sems[7])
        return land[6].astype(f32) + land[7].astype(f32)

    def wide_reduce_first(grad, land):
        sems = net.sems(8)
        for number, index in enumerate((f_y, f_d, f, f_x)):
            net.send(block(grad, index + oc - c), land.at[number], dev_c, sems[number])
        return sems

    def wide_reduce_second(grad, land, sems):
        for number, index in enumerate((f_y, f_d)):
            net.arrived(land.at[number], sems[number])
            add_into(grad, index, 0, ff_lanes, land.at[number])
            net.send(block(grad, index), land.at[4 + number], dev_y, sems[4 + number])
        for number, index in ((2, f), (3, f_x)):
            net.arrived(land.at[number], sems[number])
            add_into(grad, index, 0, ff_lanes, land.at[number])

    def wide_reduce_third(grad, land, sems):
        net.arrived(land.at[5], sems[5])
        add_into(grad, f_x, 0, ff_lanes, land.at[5])
        net.send(block(grad, f_x), land.at[6], dev_x, sems[6])
        net.arrived(land.at[4], sems[4])
        add_into(grad, f, 0, ff_lanes, land.at[4])

    def wide_reduce_cross(grad, land, sems):
        net.send(block(grad, f), land.at[7], dev_far, sems[7], when=move)

    def wide_reduce_fourth(grad, land, sems):
        net.arrived(land.at[6], sems[6])
        net.send(land.at[6], land.at[7], dev_far, sems[7], when=stay)

    def wide_reduce_finish(grad, land, sems):
        kept = jnp.where(stay, grad[piece_at(f), :].astype(f32), land[6].astype(f32))
        net.arrived(land.at[7], sems[7])
        return kept + land[7].astype(f32)

    vec_own, by_plane, by_chip = ref.vec_own, ref.by_plane, ref.by_chip
    plane_peers = [lax.rem(t + step, 4) for step in range(1, 4)]
    chip_peers = [lax.rem(k + step, 4) for step in range(1, 4)]

    def vector_planes():
        by_plane[t] = vec_own[...]
        sems = net.sems(3)
        for sem, plane in zip(sems, plane_peers, strict=True):
            net.send(vec_own, by_plane.at[t], {"fsdp": f, "tensor": plane}, sem)
        return sems

    def vector_chips(sems):
        for sem, step in zip(sems, range(3, 0, -1), strict=True):
            net.arrived(by_plane.at[lax.rem(t + step, 4)], sem)
        both = ref.vec_chip
        total = by_plane[0] + by_plane[1] + by_plane[2] + by_plane[3]
        shard = by_plane[zl] + by_plane[2 + zl]
        both[0:6, :] = total[0:6, :]
        both[6:8, :] = shard[6:8, :]
        by_chip[k] = both[...]
        sems = net.sems(3)
        for sem, chip in zip(sems, chip_peers, strict=True):
            net.send(both, by_chip.at[k], {"fsdp": 2 * chip + c, "tensor": t}, sem)
        return sems

    def vector_core(sems):
        for sem, step in zip(sems, range(3, 0, -1), strict=True):
            net.arrived(by_chip.at[lax.rem(k + step, 4)], sem)
        held = ref.vec_core
        total = by_chip[0] + by_chip[1] + by_chip[2] + by_chip[3]
        units_total = by_chip[zh] + by_chip[2 + zh]
        held[0:6, :] = total[0:6, :]
        held[6:7, :] = units_total[6:7, :]
        held[7:8, :] = total[7:8, :]
        sem = net.sem()
        net.send(held, ref.vec_core_land, dev_c, sem)
        return sem

    def vector_finish(sem):
        held, land, done = ref.vec_core, ref.vec_core_land, ref.vec_done
        net.arrived(land, sem)
        done[0:7, :] = held[0:7, :] + land[0:7, :]
        done[7:8, :] = jnp.where(home, held[7:8, :], land[7:8, :])

    barrier = pltpu.get_barrier_semaphore()
    dev_d = {"fsdp": 2 * k_d + c, "tensor": t}
    dev_last = {"fsdp": f, "tensor": (1 - zh) * 2 + (1 - zl)}
    peers = (dev_x, dev_y, dev_d, dev_c, dev_z, dev_far, dev_last, dev_far_other)
    for peer in peers:
        pl.semaphore_signal(barrier, inc=1, device_id=peer, device_id_type=MESH_IDS)

    coming = {}
    for number, name in enumerate(inputs):
        copy = pltpu.make_async_copy(
            getattr(hbm, name), getattr(held, name), ref.load_sems.at[number]
        )
        copy.start()
        coming[name] = copy
    coming = SimpleNamespace(**coming)
    stores = []

    def store(source, target):
        sem = ref.load_sems.at[len(inputs) + len(stores)]
        copy = pltpu.make_async_copy(source, target, sem)
        copy.start()
        stores.append(copy)

    attn_piece = ref.attn_piece
    if all_lanes > 4 * width:
        attn_piece[:, 4 * width :] = jnp.zeros((piece, all_lanes - 4 * width), bf16)
    for number, (copy, raw) in enumerate(
        (
            (coming.query_w, held.query_w),
            (coming.key_w, held.key_w),
            (coming.value_w, held.value_w),
            (coming.out_w, held.out_w),
        )
    ):
        copy.wait()
        attn_piece[:, number * width : (number + 1) * width] = raw[...]
    vectors[...] = jnp.zeros_like(vectors)
    for number, (copy, raw) in enumerate(
        (
            (coming.first_gain, held.first_gain),
            (coming.first_shift, held.first_shift),
            (coming.out_bias, held.out_bias),
            (coming.second_gain, held.second_gain),
            (coming.second_shift, held.second_shift),
            (coming.down_bias, held.down_bias),
        )
    ):
        copy.wait()
        vectors[number : number + 1, :] = raw[...].reshape(1, D)
    coming.up_bias.wait()
    vectors[6:7, :units] = held.up_bias[...].reshape(1, units)
    coming.query_bias.wait()
    vectors[7:8, :width] = held.query_bias[...].reshape(1, width)
    coming.value_bias.wait()
    vectors[7:8, 2 * width : 3 * width] = held.value_bias[...].reshape(1, width)
    first_gain, first_shift = vectors[0:1, :], vectors[1:2, :]
    out_bias, second_gain = vectors[2:3, :], vectors[3:4, :]
    second_shift, down_bias = vectors[4:5, :], vectors[5:6, :]
    tokens_ref, cotangent_ref = held.tokens, held.cotangent
    coming.tokens.wait()
    coming.cotangent.wait()
    token_rows = tokens_ref[...].astype(f32)
    normed, hat, inv_scale = norm_rows(token_rows, first_gain, first_shift)
    first_all[slot(near, c), :] = normed.astype(bf16)
    ref.first_hat[...] = hat
    ref.row_scale[0] = jnp.broadcast_to(inv_scale, (rows, LANES))

    pl.semaphore_wait(barrier, len(peers))

    first_sems = share_start(first_all)
    lane_cut = round_up(qkv_lanes // 2, LANES)
    q_parts = [(attn_w, 0, lane_cut), (attn_w, lane_cut, qkv_lanes)]
    o_part = (attn_w, qkv_lanes, all_lanes)
    q_base = [spread_start(attn_piece, *part) for part in q_parts]
    o_base = spread_start(attn_piece, *o_part)
    vec_sem = net.sem()
    net.send(vectors, ref.far_vectors, dev_far, vec_sem)
    up_parts = [
        WideGather(ref.up_piece, up_w, ref.up_wait, lo, hi)
        for lo, hi in row_cuts(piece, 2)
    ]
    down_parts = [
        WideGather(ref.down_piece, down_w, ref.down_wait, lo, hi)
        for lo, hi in row_cuts(piece, 3)
    ]

    for padded, copy, raw in (
        (ref.up_piece, coming.up_w, held.up_w),
        (ref.down_piece, coming.down_w, held.down_w),
    ):
        copy.wait()
        padded[...] = jnp.zeros((piece, ff_lanes), bf16)
        padded[:, :units] = raw[...]
    dy_all[slot(near, kx), :] = cotangent_ref[...]
    vec_own[5:6, :] = jnp.sum(cotangent_ref[...].astype(f32), axis=0, keepdims=True)
    head_rows[...] = jnp.zeros_like(head_rows)
    head_grads[...] = jnp.zeros_like(head_grads)
    mixed_all[...] = jnp.zeros_like(mixed_all)
    qkv_grads[...] = jnp.zeros_like(qkv_grads)

    for part in up_parts:
        part.start(inner)
    dy_sems = plain_share_z(dy_all)
    q_sems = [gather_start(*part, base) for part, base in zip(q_parts, q_base)]
    for part in up_parts:
        part.start(jnp.logical_and(outer, away))
    for part, sems in zip(q_parts, q_sems):
        gather_forward(*part, sems)
    for part in up_parts:
        part.start(jnp.logical_and(outer, home))
    o_sems = gather_start(*o_part, o_base)
    share_forward(first_all, first_sems)
    net.arrived(ref.far_vectors, vec_sem)
    share_near(first_all, first_sems)
    share_deep(first_all, first_sems)
    for part, sems in zip(q_parts, q_sems):
        gather_finish(*part, sems)
    down_parts[0].start(jnp.logical_or(inner, outer))
    for part in down_parts[1:]:
        part.start(inner)
    gather_forward(*o_part, o_sems)
    plain_share_x(dy_all, dy_sems)
    for part in up_parts:
        part.beside()
    for part in down_parts:
        part.beside()

    def shard_vector(row, own):
        return jnp.where(own, vectors[row : row + 1, :], ref.far_vectors[row : row + 1, :])

    qkv_bias = shard_vector(7, home)[:, :qkv_lanes]
    for side_at in range(2):
        side_rows = slice(side_at * pair, (side_at + 1) * pair)
        done = dot_plain(first_all[side_rows, :], attn_w[:, :qkv_lanes])
        done = (done + qkv_bias).astype(bf16)
        for image in range(2):
            to = slice(image * pair + side_at * rows, image * pair + (side_at + 1) * rows)
            for head in range(3 * heads):
                head_rows[head, to, :HD] = done[
                    image * rows : (image + 1) * rows, head * HD : (head + 1) * HD
                ]
    scale = HD ** (-0.5)

    def image_head(step):
        head, image = lax.rem(step, heads), lax.div(step, heads)
        return head, aligned(image * pair, pair)

    def attend(step, carry):
        head, span = image_head(step)
        queries, keys_part = head_rows[head, span, :], head_rows[heads + head, span, :]
        values = head_rows[2 * heads + head, span, :]
        scores = dot_right_t(queries, keys_part) * scale
        expo = jnp.exp(scores - jnp.max(scores, axis=1, keepdims=True))
        probs = expo / jnp.sum(expo, axis=1, keepdims=True)
        ref.probs_all[step] = probs
        mixed = dot_plain(probs.astype(bf16), values)
        ref.mixed_heads[head, span, :] = mixed.astype(bf16)
        return carry

    lax.fori_loop(0, 2 * heads, attend, 0, unroll=2)

    def pack(target, source, count, base):
        for side_at in range(2):
            for image in range(2):
                at = slice(side_at * pair + image * rows, side_at * pair + (image + 1) * rows)
                take = slice(image * pair + side_at * rows, image * pair + (side_at + 1) * rows)
                for head in range(count):
                    lo = base + head * HD
                    target[at, lo : lo + HD] = source[head, take, :HD]

    pack(mixed_all, ref.mixed_heads, heads, win_shift)

    def half(side):
        return aligned(side, pair)

    gather_finish(*o_part, o_sems)
    part_a[half(deep), :] = dot_right_t(mixed_all[half(deep), :], attn_w[:, win:])
    out_sems = sum_deep(0, part_a)
    part_a[half(near), :] = dot_right_t(mixed_all[half(near), :], attn_w[:, win:])
    sum_pass(0, part_a, out_sems)
    sum_near(0, part_a, out_sems)
    for part in down_parts[1:]:
        part.start(outer)
    for part in up_parts:
        part.second()
    up_parts[0].third()
    attn_rows = sum_finish(0, part_a, out_sems)
    middle = tokens_ref[...].astype(f32) + attn_rows + out_bias
    ref.mid_rows[...] = middle
    normed, hat, inv_scale = norm_rows(middle, second_gain, second_shift)
    second_all[slot(near, kx), :] = normed.astype(bf16)
    ref.second_hat[...] = hat
    ref.row_scale[1] = jnp.broadcast_to(inv_scale, (rows, LANES))
    second_sems = wide_share_start(second_all)
    up_parts[1].third()
    wide_share_forward(second_all, second_sems)
    for part in down_parts:
        part.second()
    plain_share_forward(dy_all, dy_sems)
    for part in up_parts:
        part.fourth()
    down_parts[0].third()
    for part in up_parts:
        part.finish()
    wide_share_near(second_all, second_sems)

    up_bias = shard_vector(6, stay)
    chunk = 32

    def raise_half(side):
        part_b[half(side), :] = dot_plain(second_all[half(side), :], up_w[...])

        def gelu_rows(step, carry):
            at = aligned(side + step * chunk, chunk)
            value, slope = gelu_pair(part_b[at, :] + up_bias)
            hidden_all[at, :] = value.astype(bf16)
            slope_all[at, :] = slope
            return carry

        lax.fori_loop(0, pair // chunk, gelu_rows, 0)

    raise_half(near)
    down_parts[1].third()
    wide_share_deep(second_all, second_sems)
    raise_half(deep)

    tile = 3 * LANES

    def outer_product(grad, left, right, lo, hi):
        def rows_of(step, carry):
            at = aligned(step * tile, tile)
            grad[at, lo:hi] = dot_left_t(left[:, at], right).astype(bf16)
            return carry

        lax.fori_loop(0, D // tile, rows_of, 0)

    down_parts[2].third()
    down_parts[0].fourth()
    plain_share_finish(dy_all, dy_sems)
    outer_product(down_g, dy_all, hidden_all[...], 0, ff_lanes)
    down_reduce = wide_reduce_first(down_g, ref.land_d)
    down_parts[1].fourth()
    wide_reduce_second(down_g, ref.land_d, down_reduce)
    down_parts[2].fourth()
    for part in down_parts:
        part.finish()

    def lower_half(side):
        part_b[half(side), :] = dot_plain(dy_all[half(side), :], down_w[...])

        def slope_rows(step, total):
            at = aligned(side + step * chunk, chunk)
            low = (part_b[at, :] * slope_all[at, :]).astype(bf16)
            upper_all[at, :] = low
            return total + jnp.sum(low.astype(f32), axis=0, keepdims=True)

        return lax.fori_loop(0, pair // chunk, slope_rows, jnp.zeros((1, ff_lanes), f32))

    up_bias_sum = lower_half(deep)
    part_a[half(deep), :] = dot_right_t(upper_all[half(deep), :], up_w[...])
    second_sum_sems = wide_sum_deep(0, part_a)
    up_bias_sum = up_bias_sum + lower_half(near)
    vec_own[6:7, :] = up_bias_sum
    part_a[half(near), :] = dot_right_t(upper_all[half(near), :], up_w[...])
    wide_sum_near(0, part_a, second_sum_sems)
    outer_product(up_g, second_all, upper_all[...], 0, ff_lanes)
    up_reduce = wide_reduce_first(up_g, ref.land_u)
    wide_sum_pass(0, part_a, second_sum_sems)
    wide_reduce_second(up_g, ref.land_u, up_reduce)
    wide_reduce_third(down_g, ref.land_d, down_reduce)
    second_grad = wide_sum_finish(0, part_a, second_sum_sems)
    back, gain_sum, shift_sum = norm_back(
        second_grad, ref.second_hat[...], ref.row_scale[1][:, :1], second_gain
    )
    vec_own[3:4, :] = gain_sum[None, :]
    vec_own[4:5, :] = shift_sum[None, :]
    total = cotangent_ref[...].astype(f32) + back
    ref.mid_grad[...] = total
    low = total.astype(bf16)
    mid_all[slot(near, c), :] = low
    vec_own[2:3, :] = jnp.sum(low.astype(f32), axis=0, keepdims=True)
    mid_sems = share_start(mid_all)
    part_b[half(deep), :] = dot_right_t(hidden_all[half(deep), :], down_w[...])
    mlp_sems = wide_sum_deep(1, part_b)
    part_b[half(near), :] = dot_right_t(hidden_all[half(near), :], down_w[...])
    wide_sum_near(1, part_b, mlp_sems)
    def head_half(side_at):
        side_rows = slice(side_at * pair, (side_at + 1) * pair)
        done = dot_plain(mid_all[side_rows, :], attn_w[:, win:]).astype(bf16)
        for image in range(2):
            to = slice(image * pair + side_at * rows, image * pair + (side_at + 1) * rows)
            for head in range(heads):
                lo = win_shift + head * HD
                head_grads[head, to, :HD] = done[image * rows : (image + 1) * rows, lo : lo + HD]

    share_forward(mid_all, mid_sems)
    share_near(mid_all, mid_sems)
    wide_reduce_cross(down_g, ref.land_d, down_reduce)
    wide_reduce_fourth(down_g, ref.land_d, down_reduce)
    share_deep(mid_all, mid_sems)
    head_half(0)
    head_half(1)
    wide_reduce_third(up_g, ref.land_u, up_reduce)
    wide_reduce_cross(up_g, ref.land_u, up_reduce)

    cut = round_up(2 * width, LANES)

    def value_back(step, carry):
        head, span = image_head(step)
        low = ref.probs_all[step].astype(bf16)
        value_grad = dot_left_t(low, head_grads[head, span, :])
        ref.mixed_heads[head, span, :] = value_grad.astype(bf16)
        return carry

    def value_out_rows(step, carry):
        at = aligned(step * tile, tile)
        by_value = dot_left_t(first_all[:, at], qkv_grads[:, cut:qkv_lanes])
        by_out = dot_left_t(mid_all[:, at], mixed_all[...])
        both = by_value[:, win - cut :] + by_out[:, :skip]
        attn_g[at, cut:win] = by_value[:, : win - cut].astype(bf16)
        attn_g[at, win:qkv_lanes] = both.astype(bf16)
        attn_g[at, qkv_lanes:] = by_out[:, skip:].astype(bf16)
        return carry

    lax.fori_loop(0, 2 * heads, value_back, 0, unroll=2)
    pack(qkv_grads, ref.mixed_heads, heads, 2 * width)
    lax.fori_loop(0, D // tile, value_out_rows, 0)
    vo_args = attn_g, ref.land_vo, cut, all_lanes, net.sems(10)
    reduce_first(*vo_args)

    def attend_back(step, carry):
        head, span = image_head(step)
        queries, keys_part = head_rows[head, span, :], head_rows[heads + head, span, :]
        values, grads = head_rows[2 * heads + head, span, :], head_grads[head, span, :]
        probs = ref.probs_all[step]
        prob_grad = dot_right_t(grads, values)
        row_dot = jnp.sum(probs * prob_grad, axis=1, keepdims=True)
        score_grad = (probs * (prob_grad - row_dot)).astype(bf16)
        query_grad = dot_plain(score_grad, keys_part) * scale
        key_grad = dot_left_t(score_grad, queries) * scale
        head_rows[head, span, :] = query_grad.astype(bf16)
        head_rows[heads + head, span, :] = key_grad.astype(bf16)
        return carry

    lax.fori_loop(0, 2 * heads, attend_back, 0, unroll=2)
    pack(qkv_grads, head_rows, 2 * heads, 0)
    wide_reduce_fourth(up_g, ref.land_u, up_reduce)
    outer_product(attn_g, first_all, qkv_grads[:, :cut], 0, cut)
    qk_args = attn_g, ref.land_qk, 0, cut, net.sems(10)
    reduce_first(*qk_args, when=away)
    part_a[half(deep), :] = dot_right_t(
        qkv_grads[half(deep), :qkv_lanes], attn_w[:, :qkv_lanes]
    )
    first_sum_sems = sum_deep(1, part_a)
    part_a[half(near), :] = dot_right_t(
        qkv_grads[half(near), :qkv_lanes], attn_w[:, :qkv_lanes]
    )
    sum_pass(1, part_a, first_sum_sems)
    sum_near(1, part_a, first_sum_sems)
    reduce_first(*qk_args, when=home)
    vec_own[7:8, :] = jnp.sum(qkv_grads[...].astype(f32), axis=0, keepdims=True)
    reduce_second(*vo_args)
    wide_sum_pass(1, part_b, mlp_sems)
    reduce_second(*qk_args, when=away)
    first_grad = sum_finish(1, part_a, first_sum_sems)
    back, gain_sum, shift_sum = norm_back(
        first_grad, ref.first_hat[...], ref.row_scale[0][:, :1], first_gain
    )
    vec_own[0:1, :] = gain_sum[None, :]
    vec_own[1:2, :] = shift_sum[None, :]
    vec_sems = vector_planes()
    ref.mid_grad[...] = ref.mid_grad[...] + back
    store(ref.mid_grad, out.input_grad)
    reduce_third(*vo_args)
    reduce_second(*qk_args, when=home)
    reduce_third(*qk_args)
    vec_sems = vector_chips(vec_sems)
    ref.down_buf[...] = wide_reduce_finish(down_g, ref.land_d, down_reduce)
    store(ref.down_buf, out.down_grad)
    vec_sems = vector_core(vec_sems)
    mlp_rows = wide_sum_finish(1, part_b, mlp_sems)
    ref.layer_buf[...] = (ref.mid_rows[...] + mlp_rows + down_bias).astype(bf16)
    store(ref.layer_buf, out.layer_out)
    vector_finish(vec_sems)
    store(ref.vec_done, out.vector_grad)
    ref.up_buf[...] = wide_reduce_finish(up_g, ref.land_u, up_reduce)
    store(ref.up_buf, out.up_grad)
    ref.attn_buf[:, cut:] = reduce_finish(ref.land_vo, vo_args[4])
    ref.attn_buf[:, :cut] = reduce_finish(ref.land_qk, qk_args[4])
    store(ref.attn_buf, out.attn_grad)
    net.drain()
    assert net.used <= ref.send_sems.shape[0]
    for copy in stores:
        copy.wait()


def format_kernel(shapes, *refs):
    width, units = shapes
    inputs, refs = refs[:6], refs[6:]
    outs, refs = refs[:17], refs[17:]
    held, refs = refs[:6], refs[6:]
    shaped, sems = refs[:-1], refs[-1]
    copies = [
        pltpu.make_async_copy(source, target, sems.at[number])
        for number, (source, target) in enumerate(zip(inputs, held, strict=True))
    ]
    for copy in copies:
        copy.start()
    going = []

    def put(source, number):
        copy = pltpu.make_async_copy(source, outs[number], sems.at[6 + number])
        copy.start()
        going.append(copy)

    def put_shaped(number, value):
        shaped[number - 2][...] = value
        put(shaped[number - 2], number)

    copies[0].wait()
    put(held[0], 0)
    copies[1].wait()
    put(held[1], 1)
    copies[2].wait()
    for number, place in ((4, 0), (5, 1), (6, 2), (9, 3)):
        put_shaped(number, held[2][:, place * width : (place + 1) * width])
    copies[3].wait()
    put_shaped(13, held[3][:, :units])
    copies[4].wait()
    put_shaped(15, held[4][:, :units])
    copies[5].wait()
    for number, row, lo, size in (
        (2, 0, 0, D),
        (3, 1, 0, D),
        (10, 2, 0, D),
        (11, 3, 0, D),
        (12, 4, 0, D),
        (16, 5, 0, D),
        (14, 6, 0, units),
        (7, 7, 0, width),
        (8, 7, 2 * width, width),
    ):
        put_shaped(number, held[5][row, lo : lo + size])
    for copy in going:
        copy.wait()


def fused_step(
    tokens,
    cotangent,
    first_gain,
    first_shift,
    query_weight,
    key_weight,
    value_weight,
    query_bias,
    value_bias,
    out_weight,
    out_bias,
    second_gain,
    second_shift,
    up_weight,
    up_bias,
    down_weight,
    down_bias,
):
    bf16, f32 = jnp.bfloat16, jnp.float32
    rows, piece, width, units = (
        tokens.shape[0],
        query_weight.shape[0],
        query_weight.shape[1],
        up_weight.shape[1],
    )
    heads = width // HD
    group = 4 * rows
    qkv_lanes = round_up(3 * width, LANES)
    attn_lanes = round_up(4 * width, LANES)
    ff_lanes = round_up(units, LANES)
    win = 3 * width // LANES * LANES
    given = dict(
        query_w=query_weight,
        key_w=key_weight,
        value_w=value_weight,
        out_w=out_weight.T,
        first_gain=first_gain,
        first_shift=first_shift,
        out_bias=out_bias,
        second_gain=second_gain,
        second_shift=second_shift,
        down_bias=down_bias,
        up_bias=up_bias,
        query_bias=query_bias,
        value_bias=value_bias,
        tokens=tokens,
        cotangent=cotangent,
        up_w=up_weight,
        down_w=down_weight.T,
    )
    place = pl.BlockSpec(memory_space=pl.ANY)
    sem_count = 148
    cut = round_up(2 * width, LANES)
    raw_outs = dict(
        layer_out=jax.ShapeDtypeStruct((rows, D), bf16),
        input_grad=jax.ShapeDtypeStruct((rows, D), f32),
        attn_grad=jax.ShapeDtypeStruct((piece, attn_lanes), f32),
        up_grad=jax.ShapeDtypeStruct((piece, ff_lanes), f32),
        down_grad=jax.ShapeDtypeStruct((piece, ff_lanes), f32),
        vector_grad=jax.ShapeDtypeStruct((8, D), f32),
    )
    scratch = dict(
        attn_piece=pltpu.VMEM((piece, attn_lanes), bf16),
        up_piece=pltpu.VMEM((piece, ff_lanes), bf16),
        down_piece=pltpu.VMEM((piece, ff_lanes), bf16),
        up_wait=pltpu.VMEM((piece, ff_lanes), bf16),
        down_wait=pltpu.VMEM((piece, ff_lanes), bf16),
        attn_w=pltpu.VMEM((D, attn_lanes), bf16),
        up_w=pltpu.VMEM((D, ff_lanes), bf16),
        down_w=pltpu.VMEM((D, ff_lanes), bf16),
        attn_g=pltpu.VMEM((D, attn_lanes), bf16),
        up_g=pltpu.VMEM((D, ff_lanes), bf16),
        down_g=pltpu.VMEM((D, ff_lanes), bf16),
        land_vo=pltpu.VMEM((8, piece, attn_lanes - cut), bf16),
        land_qk=pltpu.VMEM((8, piece, cut), bf16),
        land_u=pltpu.VMEM((8, piece, ff_lanes), bf16),
        land_d=pltpu.VMEM((8, piece, ff_lanes), bf16),
        first_all=pltpu.VMEM((group, D), bf16),
        second_all=pltpu.VMEM((group, D), bf16),
        dy_all=pltpu.VMEM((group, D), bf16),
        mid_all=pltpu.VMEM((group, D), bf16),
        head_rows=pltpu.VMEM((3 * heads, group, LANES), bf16),
        head_grads=pltpu.VMEM((heads, group, LANES), bf16),
        probs_all=pltpu.VMEM((2 * heads, 2 * rows, 2 * rows), f32),
        mixed_heads=pltpu.VMEM((heads, group, LANES), bf16),
        mixed_all=pltpu.VMEM((group, attn_lanes - win), bf16),
        hidden_all=pltpu.VMEM((group, ff_lanes), bf16),
        slope_all=pltpu.VMEM((group, ff_lanes), f32),
        upper_all=pltpu.VMEM((group, ff_lanes), bf16),
        qkv_grads=pltpu.VMEM((group, attn_lanes), bf16),
        part_a=pltpu.VMEM((group, D), f32),
        part_b=pltpu.VMEM((group, D), f32),
        core_send=pltpu.VMEM((2, 2, rows, D), bf16),
        core_land=pltpu.VMEM((2, 2, rows, D), bf16),
        deep_send=pltpu.VMEM((2, rows, D), bf16),
        deep_land=pltpu.VMEM((2, rows, D), bf16),
        wide_send=pltpu.VMEM((2, 6, rows // 2, D), bf16),
        wide_land=pltpu.VMEM((2, 6, rows // 2, D), bf16),
        first_hat=pltpu.VMEM((rows, D), f32),
        second_hat=pltpu.VMEM((rows, D), f32),
        mid_rows=pltpu.VMEM((rows, D), f32),
        mid_grad=pltpu.VMEM((rows, D), f32),
        row_scale=pltpu.VMEM((2, rows, LANES), f32),
        vectors=pltpu.VMEM((8, D), f32),
        far_vectors=pltpu.VMEM((8, D), f32),
        vec_own=pltpu.VMEM((8, D), f32),
        by_plane=pltpu.VMEM((4, 8, D), f32),
        vec_chip=pltpu.VMEM((8, D), f32),
        by_chip=pltpu.VMEM((4, 8, D), f32),
        vec_core=pltpu.VMEM((8, D), f32),
        vec_core_land=pltpu.VMEM((8, D), f32),
        vec_done=pltpu.VMEM((8, D), f32),
        layer_buf=pltpu.VMEM((rows, D), bf16),
        attn_buf=pltpu.VMEM((piece, attn_lanes), f32),
        up_buf=pltpu.VMEM((piece, ff_lanes), f32),
        down_buf=pltpu.VMEM((piece, ff_lanes), f32),
        load_sems=pltpu.SemaphoreType.DMA((len(given) + len(raw_outs),)),
        send_sems=pltpu.SemaphoreType.DMA((sem_count,)),
        recv_sems=pltpu.SemaphoreType.DMA((sem_count,)),
    )
    shapes = (rows, heads, width, units, qkv_lanes, piece)
    names = tuple(given), tuple(raw_outs), tuple(scratch)

    def body(*refs):
        layer_kernel(shapes, names, *refs)

    raw = pl.pallas_call(
        body,
        out_shape=tuple(raw_outs.values()),
        in_specs=[place] * len(given),
        out_specs=(place,) * len(raw_outs),
        scratch_shapes=[
            *(pltpu.VMEM(array.shape, array.dtype) for array in given.values()),
            *scratch.values(),
        ],
        compiler_params=pltpu.CompilerParams(
            collective_id=0, has_side_effects=True, vmem_limit_bytes=67043328
        ),
        name="layer",
    )(*given.values())
    raw_outs = tuple(raw_outs.values())

    vector, narrow = jax.ShapeDtypeStruct((D,), f32), jax.ShapeDtypeStruct((width,), f32)
    attn_out = jax.ShapeDtypeStruct((piece, width), f32)
    ff_out = jax.ShapeDtypeStruct((piece, units), f32)
    outs = (
        *raw_outs[:2],
        vector,
        vector,
        attn_out,
        attn_out,
        attn_out,
        narrow,
        narrow,
        attn_out,
        vector,
        vector,
        vector,
        ff_out,
        jax.ShapeDtypeStruct((units,), f32),
        ff_out,
        vector,
    )

    def format_body(*refs):
        format_kernel((width, units), *refs)

    done = pl.pallas_call(
        format_body,
        out_shape=outs,
        in_specs=[place] * 6,
        out_specs=(place,) * 17,
        scratch_shapes=[
            *(pltpu.VMEM(item.shape, item.dtype) for item in raw_outs),
            *(pltpu.VMEM(item.shape, item.dtype) for item in outs[2:]),
            pltpu.SemaphoreType.DMA((6 + 17,)),
        ],
        compiler_params=pltpu.CompilerParams(vmem_limit_bytes=67043328),
        name="outputs",
    )(*raw)
    done = list(done)
    done[9], done[15] = done[9].T, done[15].T
    return tuple(done)


def pick_step(mesh):
    if mesh.shape["fsdp"] == 8 and mesh.shape["tensor"] == 4:
        return fused_step
    return on_device


def solution(mesh):
    return jax.shard_map(
        pick_step(mesh),
        mesh=mesh,
        in_specs=(
            P(("fsdp", "tensor"), None),
            P(("fsdp", "tensor"), None),
            P(),
            P(),
            P("fsdp", "tensor"),
            P("fsdp", "tensor"),
            P("fsdp", "tensor"),
            P("tensor"),
            P("tensor"),
            P("tensor", "fsdp"),
            P(),
            P(),
            P(),
            P("fsdp", "tensor"),
            P("tensor"),
            P("tensor", "fsdp"),
            P(),
        ),
        out_specs=(
            P(("fsdp", "tensor"), None),
            P(("fsdp", "tensor"), None),
            P(),
            P(),
            P("fsdp", "tensor"),
            P("fsdp", "tensor"),
            P("fsdp", "tensor"),
            P("tensor"),
            P("tensor"),
            P("tensor", "fsdp"),
            P(),
            P(),
            P(),
            P("fsdp", "tensor"),
            P("tensor"),
            P("tensor", "fsdp"),
            P(),
        ),
        check_vma=False,
    )
```

```python
import math
from types import SimpleNamespace

import jax
import jax.numpy as jnp
from jax import lax
from jax.experimental import pallas as pl
from jax.experimental.pallas import tpu as pltpu
from jax.sharding import PartitionSpec as P

D = 1152
HD = 72
FF = 4304
SEQ = 256


norm_eps = 1e-06
gelu_coef = 0.7978845608028654
cubic_coef = 0.044715


def dot_plain(left, right):
    return jnp.dot(left, right, preferred_element_type=jnp.float32)


def dot_right_t(left, right):
    return lax.dot_general(
        left, right, (((1,), (1,)), ((), ())), preferred_element_type=jnp.float32
    )


def dot_left_t(left, right):
    return lax.dot_general(
        left, right, (((0,), (0,)), ((), ())), preferred_element_type=jnp.float32
    )


def norm_rows(values, gain, shift):
    row_mean = jnp.mean(values, axis=1, keepdims=True)
    centred = values - row_mean
    inv_scale = lax.rsqrt(jnp.mean(centred * centred, axis=1, keepdims=True) + norm_eps)
    normed = centred * inv_scale
    return (normed * gain + shift, normed, inv_scale)


def norm_back(out_grad, normed, inv_scale, gain):
    scaled_grad = out_grad * gain
    grad_mean = jnp.mean(scaled_grad, axis=1, keepdims=True)
    cross_mean = jnp.mean(scaled_grad * normed, axis=1, keepdims=True)
    in_grad = inv_scale * (scaled_grad - grad_mean - normed * cross_mean)
    return (in_grad, jnp.sum(out_grad * normed, axis=0), jnp.sum(out_grad, axis=0))


def gelu_pair(upper):
    tangent = jnp.tanh(gelu_coef * (upper + cubic_coef * upper * upper * upper))
    gelu_value = 0.5 * upper * (1.0 + tangent)
    gelu_slope = 0.5 * (1.0 + tangent) + 0.5 * upper * (1.0 - tangent * tangent) * gelu_coef * (
        1.0 + 3.0 * cubic_coef * upper * upper
    )
    return (gelu_value, gelu_slope)


def split_heads(block_rows, head_count):
    col_width = block_rows.shape[1] // 3
    img_count = block_rows.shape[0] // SEQ
    shape_four = (img_count, SEQ, head_count, HD)
    queries = block_rows[:, :col_width].reshape(shape_four)
    keys_part = block_rows[:, col_width : 2 * col_width].reshape(shape_four)
    values = block_rows[:, 2 * col_width :].reshape(shape_four)
    return (queries, keys_part, values, shape_four)


def attend_forward(block_rows, head_count):
    queries, keys_part, values, shape_four = split_heads(block_rows, head_count)
    scores = jnp.einsum(
        "nqhd,nkhd->nhqk", queries, keys_part, preferred_element_type=jnp.float32
    ) * HD ** (-0.5)
    peak = jnp.max(scores, axis=-1, keepdims=True)
    expo = jnp.exp(scores - peak)
    totals = jnp.sum(expo, axis=-1, keepdims=True)
    prob_low = (expo / totals).astype(jnp.bfloat16)
    mixed = jnp.einsum("nhqk,nkhd->nqhd", prob_low, values, preferred_element_type=jnp.float32)
    row_total = block_rows.shape[0]
    mixed = mixed.reshape(row_total, head_count * HD).astype(jnp.bfloat16)
    return (mixed, (peak + jnp.log(totals))[..., 0])


def attend_backward(inputs, head_count):
    block_rows, grad_block, log_total = inputs
    queries, keys_part, values, shape_four = split_heads(block_rows, head_count)
    grad_out = grad_block.reshape(shape_four)
    scores = jnp.einsum(
        "nqhd,nkhd->nhqk", queries, keys_part, preferred_element_type=jnp.float32
    ) * HD ** (-0.5)
    probs = jnp.exp(scores - log_total[..., None])
    prob_low = probs.astype(jnp.bfloat16)
    value_grad = jnp.einsum(
        "nhqk,nqhd->nkhd", prob_low, grad_out, preferred_element_type=jnp.float32
    )
    prob_grad = jnp.einsum("nqhd,nkhd->nhqk", grad_out, values, preferred_element_type=jnp.float32)
    row_dot = jnp.sum(probs * prob_grad, axis=-1, keepdims=True)
    score_grad = (probs * (prob_grad - row_dot)).astype(jnp.bfloat16)
    query_grad = jnp.einsum(
        "nhqk,nkhd->nqhd", score_grad, keys_part, preferred_element_type=jnp.float32
    ) * HD ** (-0.5)
    key_grad = jnp.einsum(
        "nhqk,nqhd->nkhd", score_grad, queries, preferred_element_type=jnp.float32
    ) * HD ** (-0.5)
    row_total = block_rows.shape[0]
    col_width = head_count * HD
    return jnp.concatenate(
        (
            query_grad.reshape(row_total, col_width),
            key_grad.reshape(row_total, col_width),
            value_grad.reshape(row_total, col_width),
        ),
        axis=1,
    ).astype(jnp.bfloat16)


def on_device(
    tokens,
    cotangent,
    first_gain,
    first_shift,
    query_weight,
    key_weight,
    value_weight,
    query_bias,
    value_bias,
    out_weight,
    out_bias,
    second_gain,
    second_shift,
    up_weight,
    up_bias,
    down_weight,
    down_bias,
):
    full_query, full_key, full_value, full_outp, full_up, full_down = (
        lax.all_gather(query_weight, "fsdp", axis=0, tiled=True),
        lax.all_gather(key_weight, "fsdp", axis=0, tiled=True),
        lax.all_gather(value_weight, "fsdp", axis=0, tiled=True),
        lax.all_gather(out_weight, "fsdp", axis=1, tiled=True),
        lax.all_gather(up_weight, "fsdp", axis=0, tiled=True),
        lax.all_gather(down_weight, "fsdp", axis=1, tiled=True),
    )
    qkv_weight = jnp.concatenate((full_query, full_key, full_value), axis=1)
    local_width = full_query.shape[1]
    ffn_width = full_up.shape[1]
    head_count = local_width // HD
    token_rows = tokens.astype(jnp.float32)
    first_out, first_hat, first_scale = norm_rows(token_rows, first_gain, first_shift)
    all_first = lax.all_gather(first_out.astype(jnp.bfloat16), "tensor", axis=0, tiled=True)
    qkv_bias = jnp.concatenate((query_bias, jnp.zeros_like(query_bias), value_bias))
    qkv_rows = (dot_plain(all_first, qkv_weight) + qkv_bias).astype(jnp.bfloat16)
    group_rows = qkv_rows.shape[0]
    images = group_rows // SEQ
    per_block = math.gcd(images, max(1, 512 // SEQ))
    blocks = images // per_block
    stacked = qkv_rows.reshape(blocks, per_block * SEQ, 3 * local_width)

    def forward_block(block_rows):
        return attend_forward(block_rows, head_count)

    head_out, log_total = lax.map(forward_block, stacked)
    head_out = head_out.reshape(group_rows, local_width)
    attn_rows = lax.psum_scatter(
        dot_plain(head_out, full_outp), "tensor", scatter_dimension=0, tiled=True
    )
    mid_rows = token_rows + attn_rows + out_bias
    second_out, second_hat, second_scale = norm_rows(mid_rows, second_gain, second_shift)
    all_second = lax.all_gather(second_out.astype(jnp.bfloat16), "tensor", axis=0, tiled=True)
    up_pre = dot_plain(all_second, full_up) + up_bias
    hidden_value, hidden_slope = gelu_pair(up_pre)
    hidden_low = hidden_value.astype(jnp.bfloat16)
    mlp_rows = lax.psum_scatter(
        dot_plain(hidden_low, full_down).astype(jnp.bfloat16),
        "tensor",
        scatter_dimension=0,
        tiled=True,
    ).astype(jnp.float32)
    layer_out = (mid_rows + mlp_rows + down_bias).astype(jnp.bfloat16)
    out_grad = cotangent.astype(jnp.float32)
    all_out_grad = lax.all_gather(cotangent, "tensor", axis=0, tiled=True)
    down_grad = dot_left_t(hidden_low, all_out_grad)
    hidden_grad = dot_right_t(all_out_grad, full_down)
    upper_low = (hidden_grad * hidden_slope).astype(jnp.bfloat16)
    up_bias_grad = jnp.sum(upper_low.astype(jnp.float32), axis=0)
    up_grad = dot_left_t(all_second, upper_low)
    second_grad = lax.psum_scatter(
        dot_right_t(upper_low, full_up), "tensor", scatter_dimension=0, tiled=True
    )
    back_second, second_gain_grad, second_shift_grad = norm_back(
        second_grad, second_hat, second_scale, second_gain
    )
    mid_grad = out_grad + back_second
    mid_low = mid_grad.astype(jnp.bfloat16)
    all_mid_grad = lax.all_gather(mid_low, "tensor", axis=0, tiled=True)
    outp_grad = dot_left_t(head_out, all_mid_grad)
    head_grad = dot_right_t(all_mid_grad, full_outp).astype(jnp.bfloat16)

    def backward_block(inputs):
        return attend_backward(inputs, head_count)

    qkv_grad = lax.map(
        backward_block,
        (stacked, head_grad.reshape(blocks, per_block * SEQ, local_width), log_total),
    )
    qkv_grad = qkv_grad.reshape(group_rows, 3 * local_width)
    qkv_weight_grad = dot_left_t(all_first, qkv_grad)
    qkv_bias_grad = jnp.sum(qkv_grad.astype(jnp.float32), axis=0)
    first_grad = lax.psum_scatter(
        dot_right_t(qkv_grad, qkv_weight).astype(jnp.bfloat16),
        "tensor",
        scatter_dimension=0,
        tiled=True,
    ).astype(jnp.float32)
    back_first, first_gain_grad, first_shift_grad = norm_back(
        first_grad, first_hat, first_scale, first_gain
    )
    input_grad = mid_grad + back_first
    out_bias_grad = jnp.sum(mid_low.astype(jnp.float32), axis=0)
    down_bias_grad = jnp.sum(out_grad, axis=0)
    small_terms = jnp.concatenate(
        (
            first_gain_grad,
            first_shift_grad,
            out_bias_grad,
            second_gain_grad,
            second_shift_grad,
            down_bias_grad,
        )
    )
    tensor_index = lax.axis_index("tensor")
    head_terms = jnp.zeros((2 * D + FF,), jnp.float32)
    head_terms = lax.dynamic_update_slice(
        head_terms, qkv_bias_grad[:local_width], (tensor_index * local_width,)
    )
    head_terms = lax.dynamic_update_slice(
        head_terms, qkv_bias_grad[2 * local_width :], (D + tensor_index * local_width,)
    )
    head_terms = lax.dynamic_update_slice(
        head_terms, up_bias_grad, (2 * D + tensor_index * ffn_width,)
    )
    small_sums, head_sums = lax.psum((small_terms, head_terms), ("fsdp", "tensor"))
    query_bias_total = lax.dynamic_slice(head_sums, (tensor_index * local_width,), (local_width,))
    value_bias_total = lax.dynamic_slice(
        head_sums, (D + tensor_index * local_width,), (local_width,)
    )
    up_bias_total = lax.dynamic_slice(head_sums, (2 * D + tensor_index * ffn_width,), (ffn_width,))
    query_part, key_part, value_part, outp_part, up_part, down_part = (
        lax.psum_scatter(qkv_weight_grad[:, :local_width], "fsdp", scatter_dimension=0, tiled=True),
        lax.psum_scatter(
            qkv_weight_grad[:, local_width : 2 * local_width],
            "fsdp",
            scatter_dimension=0,
            tiled=True,
        ),
        lax.psum_scatter(
            qkv_weight_grad[:, 2 * local_width :], "fsdp", scatter_dimension=0, tiled=True
        ),
        lax.psum_scatter(outp_grad, "fsdp", scatter_dimension=1, tiled=True),
        lax.psum_scatter(up_grad, "fsdp", scatter_dimension=0, tiled=True),
        lax.psum_scatter(down_grad, "fsdp", scatter_dimension=1, tiled=True),
    )
    return (
        layer_out,
        input_grad,
        small_sums[0:D],
        small_sums[D : 2 * D],
        query_part,
        key_part,
        value_part,
        query_bias_total,
        value_bias_total,
        outp_part,
        small_sums[2 * D : 3 * D],
        small_sums[3 * D : 4 * D],
        small_sums[4 * D : 5 * D],
        up_part,
        up_bias_total,
        down_part,
        small_sums[5 * D : 6 * D],
    )


MESH_IDS = pl.DeviceIdType.MESH
LANES = 128


def round_up(value, step):
    return -(-value // step) * step


def row_cuts(count, parts):
    edges = [min(count, round_up(count * at // parts, 16)) for at in range(parts + 1)]
    return list(zip(edges[:-1], edges[1:]))


class Remote:
    def __init__(self, send_sems, recv_sems):
        self.send_sems, self.recv_sems = send_sems, recv_sems
        self.used = 0
        self.sent = 0
        self.slots = [None] * send_sems.shape[0]

    def sem(self):
        self.used += 1
        return self.used - 1

    def sems(self, count):
        return [self.sem() for _ in range(count)]

    def release(self, slot):
        if self.slots[slot] is not None:
            copy, when = self.slots[slot]
            guarded(when, copy.wait_send)

    def send(self, src, dst, device, recv, when=None):
        slot = self.sent % len(self.slots)
        self.sent += 1
        self.release(slot)
        copy = pltpu.make_async_remote_copy(
            src_ref=src,
            dst_ref=dst,
            send_sem=self.send_sems.at[slot],
            recv_sem=self.recv_sems.at[recv],
            device_id=device,
            device_id_type=MESH_IDS,
        )
        guarded(when, copy.start)
        self.slots[slot] = copy, when

    def local(self, src, dst, sem, when):
        copy = pltpu.make_async_copy(src, dst, self.recv_sems.at[sem])
        guarded(when, copy.start)

    def arrived(self, dst, sem):
        pltpu.make_async_copy(dst, dst, self.recv_sems.at[sem]).wait()

    def drain(self):
        for slot in range(len(self.slots)):
            self.release(slot)


def guarded(when, action):
    if when is None:
        action()
    else:
        pl.when(when)(action)


def layer_kernel(shapes, names, *refs):
    rows, heads, width, units, qkv_lanes, piece = shapes
    inputs, outputs, scratch = names
    hbm = SimpleNamespace(**dict(zip(inputs, refs[: len(inputs)], strict=True)))
    refs = refs[len(inputs) :]
    out = SimpleNamespace(**dict(zip(outputs, refs[: len(outputs)], strict=True)))
    refs = refs[len(outputs) :]
    held = SimpleNamespace(**dict(zip(inputs, refs[: len(inputs)], strict=True)))
    refs = refs[len(inputs) :]
    ref = SimpleNamespace(**dict(zip(scratch, refs, strict=True)))
    bf16, f32 = jnp.bfloat16, jnp.float32
    attn_w, up_w, down_w = ref.attn_w, ref.up_w, ref.down_w
    attn_g, up_g, down_g = ref.attn_g, ref.up_g, ref.down_g
    first_all, second_all = ref.first_all, ref.second_all
    dy_all, mid_all = ref.dy_all, ref.mid_all
    head_rows, head_grads = ref.head_rows, ref.head_grads
    mixed_all, hidden_all, upper_all = ref.mixed_all, ref.hidden_all, ref.upper_all
    slope_all, qkv_grads = ref.slope_all, ref.qkv_grads
    part_a, part_b, vectors = ref.part_a, ref.part_b, ref.vectors
    pair, fourth = 2 * rows, rows // 2
    out_base = 3 * width
    win = out_base // LANES * LANES
    win_shift = out_base - win
    skip = qkv_lanes - win
    all_lanes, ff_lanes = attn_w.shape[1], up_w.shape[1]
    main = units // LANES * LANES
    rest = units - main

    f = lax.axis_index("fsdp")
    t = lax.axis_index("tensor")
    c, k = lax.rem(f, 2), lax.div(f, 2)
    kx, ky = lax.rem(k, 2), lax.div(k, 2)
    zl, zh = lax.rem(t, 2), lax.div(t, 2)
    oc, ox = 1 - c, 1 - kx
    k_x, k_y, k_d = ky * 2 + ox, (1 - ky) * 2 + kx, (1 - ky) * 2 + ox
    home = c == zh
    away = jnp.logical_not(home)
    stay = kx == zh
    outer = zl == zh
    inner = jnp.logical_not(outer)
    move = jnp.logical_not(stay)
    far_t = (1 - zh) * 2 + zl
    dev_x = {"fsdp": 2 * k_x + c, "tensor": t}
    dev_y = {"fsdp": 2 * k_y + c, "tensor": t}
    dev_c = {"fsdp": 2 * k + oc, "tensor": t}
    dev_z = {"fsdp": f, "tensor": zh * 2 + (1 - zl)}
    dev_far = {"fsdp": f, "tensor": far_t}
    dev_far_other = {"fsdp": 2 * k + oc, "tensor": far_t}
    net = Remote(ref.send_sems, ref.recv_sems)

    def aligned(start, size):
        return pl.ds(pl.multiple_of(start, math.gcd(size, LANES)), size)

    def piece_at(index):
        return pl.ds(pl.multiple_of(index * piece, piece), piece)

    def block(buf, index, lo=0, hi=None):
        return buf.at[piece_at(index), lo : buf.shape[1] if hi is None else hi]

    near, deep = zl * pair, (1 - zl) * pair

    def slot(side, place):
        return aligned(side + place * rows, rows)

    def spread_start(src, buf, lo, hi):
        base, _ = net.sems(2)
        source, target = src.at[:, lo:hi], block(buf, f, lo, hi)
        net.local(source, target, base + c, home)
        to = {"fsdp": 2 * k + zh, "tensor": t}
        net.send(source, target, to, base + c, when=away)
        to = {"fsdp": 2 * k + zh, "tensor": far_t}
        net.send(source, target, to, base + c)
        return base

    def gather_start(buf, lo, hi, base):
        sems = net.sems(3)
        a_own, b_own = block(buf, 2 * k, lo, hi), block(buf, 2 * k + 1, lo, hi)
        net.arrived(a_own, base)
        net.send(a_own, a_own, dev_x, sems[0])
        net.arrived(b_own, base + 1)
        net.send(b_own, b_own, dev_y, sems[1])
        net.send(a_own, a_own, dev_y, sems[2])
        net.send(b_own, b_own, dev_x, sems[2])
        return sems

    def gather_forward(buf, lo, hi, sems):
        a_x, b_y = block(buf, 2 * k_x, lo, hi), block(buf, 2 * k_y + 1, lo, hi)
        net.arrived(a_x, sems[0])
        net.send(a_x, a_x, dev_y, sems[2])
        net.arrived(b_y, sems[1])
        net.send(b_y, b_y, dev_x, sems[2])

    def gather_finish(buf, lo, hi, sems):
        net.arrived(buf.at[0 : 4 * piece, lo:hi], sems[2])

    f_x, f_y, f_d = 2 * k_x + c, 2 * k_y + c, 2 * k_d + c

    class WideGather:
        def __init__(self, src, buf, wait_at, lo, hi):
            self.buf, self.lo, self.size = buf, lo, hi - lo
            self.src, self.wait_at = src.at[lo:hi, :], wait_at.at[lo:hi, :]
            self.sems = net.sems(6)

        def at(self, index):
            start = pl.multiple_of(index * piece + self.lo, 16)
            return self.buf.at[pl.ds(start, self.size), :]

        def start(self, when):
            own, sems = self.at(f), self.sems
            stay_now, move_now = jnp.logical_and(stay, when), jnp.logical_and(move, when)
            net.local(self.src, own, sems[4], stay_now)
            net.send(self.src, own, dev_far, sems[0], when=stay_now)
            net.send(self.src, self.wait_at, dev_far, sems[0], when=move_now)

        def beside(self):
            net.send(self.src, self.at(f), dev_x, self.sems[1], when=move)

        def second(self):
            own, sems = self.at(f), self.sems

            @pl.when(stay)
            def _():
                net.arrived(self.wait_at, sems[0])

            @pl.when(move)
            def _():
                net.arrived(own, sems[0])

            net.send(self.wait_at, own, dev_x, sems[1], when=stay)

            @pl.when(stay)
            def _():
                net.arrived(own, sems[4])

            net.send(own, own, dev_y, sems[2])
            net.send(own, own, dev_c, sems[3])

        def third(self):
            got = self.at(f_x)
            net.arrived(got, self.sems[1])
            net.send(got, got, dev_y, self.sems[5])
            net.send(got, got, dev_c, self.sems[3])

        def fourth(self):
            for index, sem in ((f_y, 2), (f_d, 5)):
                got = self.at(index)
                net.arrived(got, self.sems[sem])
                net.send(got, got, dev_c, self.sems[3])

        def finish(self):
            net.arrived(self.buf.at[0 : 4 * self.size, :], self.sems[3])

    def share_start(buf):
        sems = net.sems(3)
        own = buf.at[slot(near, c)]
        net.send(own, own, dev_z, sems[0])
        net.send(own, own, dev_c, sems[1])
        return sems

    def share_near(buf, sems):
        net.arrived(buf.at[slot(near, oc)], sems[1])

    def share_forward(buf, sems):
        got = buf.at[slot(deep, c)]
        net.arrived(got, sems[0])
        net.send(got, got, dev_c, sems[2])

    def share_deep(buf, sems):
        net.arrived(buf.at[slot(deep, oc)], sems[2])

    def sum_deep(which, part):
        sems = net.sems(3)
        send = ref.core_send.at[which, 0]
        send[...] = part[slot(deep, oc), :].astype(bf16)
        net.send(send, ref.core_land.at[which, 0], dev_c, sems[0])
        return sems

    def sum_pass(which, part, sems):
        land, send = ref.core_land.at[which, 0], ref.deep_send.at[which]
        net.arrived(land, sems[0])
        send[...] = (part[slot(deep, c), :] + land[...].astype(f32)).astype(bf16)
        net.send(send, ref.deep_land.at[which], dev_z, sems[1])

    def sum_near(which, part, sems):
        send = ref.core_send.at[which, 1]
        send[...] = part[slot(near, oc), :].astype(bf16)
        net.send(send, ref.core_land.at[which, 1], dev_c, sems[2])

    def sum_finish(which, part, sems):
        beside, across = ref.core_land.at[which, 1], ref.deep_land.at[which]
        net.arrived(beside, sems[2])
        total = part[slot(near, c), :] + beside[...].astype(f32)
        net.arrived(across, sems[1])
        return total + across[...].astype(f32)

    def quarter(side, place, which):
        return aligned(side + place * rows + which * fourth, fourth)

    def wide_share_start(buf):
        sems = net.sems(4)
        first, second = buf.at[quarter(near, kx, 0)], buf.at[quarter(near, kx, 1)]
        net.send(first, first, dev_z, sems[0])
        net.send(second, second, dev_x, sems[1])
        net.send(second, second, dev_z, sems[3])
        net.send(first, first, dev_x, sems[2])
        return sems

    def wide_share_forward(buf, sems):
        from_z, from_x = buf.at[quarter(deep, kx, 0)], buf.at[quarter(near, ox, 1)]
        net.arrived(from_z, sems[0])
        net.send(from_z, from_z, dev_x, sems[3])
        net.arrived(from_x, sems[1])
        net.send(from_x, from_x, dev_z, sems[3])

    def wide_share_near(buf, sems):
        net.arrived(buf.at[quarter(near, ox, 0)], sems[2])

    def wide_share_deep(buf, sems):
        net.arrived(buf.at[0 : 3 * fourth, :], sems[3])

    def plain_share_z(buf):
        sems = net.sems(3)
        own = buf.at[slot(near, kx)]
        net.send(own, own, dev_z, sems[0])
        return sems

    def plain_share_x(buf, sems):
        own = buf.at[slot(near, kx)]
        net.send(own, own, dev_x, sems[1])

    def plain_share_forward(buf, sems):
        got = buf.at[slot(near, ox)]
        net.arrived(got, sems[1])
        net.send(got, got, dev_z, sems[2])

    def plain_share_finish(buf, sems):
        net.arrived(buf.at[slot(deep, kx)], sems[0])
        net.arrived(buf.at[slot(deep, ox)], sems[2])

    def wide_send(which, number):
        return ref.wide_send.at[which, number]

    def wide_land(which, number):
        return ref.wide_land.at[which, number]

    def wide_push(which, number, value, device, sem):
        wide_send(which, number)[...] = value.astype(bf16)
        net.send(wide_send(which, number), wide_land(which, number), device, sem)

    def wide_sum_deep(which, part):
        sems = net.sems(6)
        wide_push(which, 0, part[quarter(deep, ox, 0), :], dev_x, sems[0])
        wide_push(which, 1, part[quarter(deep, ox, 1), :], dev_z, sems[1])
        wide_push(which, 2, part[quarter(deep, kx, 1), :], dev_z, sems[2])
        return sems

    def wide_sum_near(which, part, sems):
        wide_push(which, 3, part[quarter(near, ox, 0), :], dev_x, sems[3])

    def wide_sum_pass(which, part, sems):
        net.arrived(wide_land(which, 0), sems[0])
        total = part[quarter(deep, kx, 0), :] + wide_land(which, 0)[...].astype(f32)
        wide_push(which, 4, total, dev_z, sems[4])
        net.arrived(wide_land(which, 1), sems[1])
        total = part[quarter(near, ox, 1), :] + wide_land(which, 1)[...].astype(f32)
        wide_push(which, 5, total, dev_x, sems[5])

    def wide_sum_finish(which, part, sems):
        halves = []
        for half_at, (by_z, by_x) in enumerate(((4, 3), (2, 5))):
            net.arrived(wide_land(which, by_z), sems[by_z])
            net.arrived(wide_land(which, by_x), sems[by_x])
            halves.append(
                part[quarter(near, kx, half_at), :]
                + wide_land(which, by_z)[...].astype(f32)
                + wide_land(which, by_x)[...].astype(f32)
            )
        return jnp.concatenate(halves, axis=0)

    def add_into(grad, index, lo, hi, land):
        at = piece_at(index)
        total = grad[at, lo:hi].astype(f32) + land[...].astype(f32)
        grad[at, lo:hi] = total.astype(bf16)

    def reduce_route(core, by_y):
        if core == 0 or by_y:
            return dev_y, 2 * k_y + core, 2 * k_x + core, dev_x
        return dev_x, 2 * k_x + core, 2 * k_y + core, dev_y

    def reduce_first(grad, land, lo, hi, sems, by_y=False, when=None):
        for distant in (True, False):
            for core in range(2):
                device, index, _, _ = reduce_route(core, by_y)
                index, number = (2 * k_d + core, 1 + 2 * core) if distant else (index, 2 * core)
                source = block(grad, index, lo, hi)
                net.send(source, land.at[number], device, sems[number], when=when)

    def reduce_second(grad, land, lo, hi, sems, by_y=False, when=None):
        def collect(index, number):
            def action():
                net.arrived(land.at[number], sems[number])
                add_into(grad, index, lo, hi, land.at[number])

            guarded(when, action)

        for core in range(2):
            _, _, index, device = reduce_route(core, by_y)
            collect(index, 1 + 2 * core)
            source = block(grad, index, lo, hi)
            net.send(source, land.at[4 + core], device, sems[4 + core], when=when)
        for core in range(2):
            collect(2 * k + core, 2 * core)

    def reduce_third(grad, land, lo, hi, sems, when=None):
        def here(condition):
            return condition if when is None else jnp.logical_and(when, condition)

        for core in range(2):

            def collect(core=core):
                net.arrived(land.at[4 + core], sems[4 + core])
                add_into(grad, 2 * k + core, lo, hi, land.at[4 + core])

            guarded(when, collect)
            source = block(grad, 2 * k + core, lo, hi)
            mine, other = jnp.logical_and(home, c == core), jnp.logical_and(home, c != core)
            net.local(source, land.at[6], sems[6], here(mine))
            to = {"fsdp": 2 * k + core, "tensor": t}
            net.send(source, land.at[6], to, sems[6], when=here(other))
            to = {"fsdp": 2 * k + core, "tensor": far_t}
            net.send(source, land.at[7], to, sems[7], when=here(away))

    def reduce_finish(land, sems):
        net.arrived(land.at[6], sems[6])
        net.arrived(land.at[7], sems[7])
        return land[6].astype(f32) + land[7].astype(f32)

    def wide_reduce_first(grad, land):
        sems = net.sems(6)
        for number, index in enumerate((f_d, f_y, f, f_x)):
            sem = sems[0] if number < 2 else sems[1]
            net.send(block(grad, index + oc - c), land.at[number], dev_c, sem)
        return sems

    def wide_reduce_second(grad, land, sems):
        net.arrived(land.at[0:2], sems[0])
        for number, index in enumerate((f_d, f_y)):
            add_into(grad, index, 0, grad.shape[1], land.at[number])
            net.send(block(grad, index), land.at[4 + number], dev_y, sems[4 + number])
        net.arrived(land.at[2:4], sems[1])
        for number, index in ((2, f), (3, f_x)):
            add_into(grad, index, 0, grad.shape[1], land.at[number])

    def wide_reduce_third(grad, land, sems):
        net.arrived(land.at[4], sems[4])
        add_into(grad, f_x, 0, grad.shape[1], land.at[4])
        net.send(block(grad, f_x), land.at[6], dev_x, sems[2])
        net.arrived(land.at[5], sems[5])
        add_into(grad, f, 0, grad.shape[1], land.at[5])

    def wide_reduce_cross(grad, land, sems, when):
        now = jnp.logical_and(move, when)
        net.send(block(grad, f), land.at[7], dev_far, sems[3], when=now)

    def wide_reduce_fourth(grad, land, sems, when):
        guarded(when, lambda: net.arrived(land.at[6], sems[2]))
        now = jnp.logical_and(stay, when)
        net.send(land.at[6], land.at[7], dev_far, sems[3], when=now)

    def wide_reduce_finish(grad, land, sems):
        kept = jnp.where(stay, grad[piece_at(f), :].astype(f32), land[6].astype(f32))
        net.arrived(land.at[7], sems[3])
        return kept + land[7].astype(f32)

    vec_own, by_plane, by_chip = ref.vec_own, ref.by_plane, ref.by_chip
    plane_peers = [lax.rem(t + step, 4) for step in range(1, 4)]
    chip_peers = [lax.rem(k + step, 4) for step in range(1, 4)]

    def vector_planes():
        by_plane[t] = vec_own[...]
        sem = net.sem()
        for plane in plane_peers:
            net.send(vec_own, by_plane.at[t], {"fsdp": f, "tensor": plane}, sem)
        return sem

    def vector_chips(sem):
        net.arrived(by_plane.at[0:3], sem)
        both = ref.vec_chip
        total = by_plane[0] + by_plane[1] + by_plane[2] + by_plane[3]
        shard = by_plane[zl] + by_plane[2 + zl]
        both[0:6, :] = total[0:6, :]
        both[6:8, :] = shard[6:8, :]
        by_chip[k] = both[...]
        sem = net.sem()
        for chip in chip_peers:
            net.send(both, by_chip.at[k], {"fsdp": 2 * chip + c, "tensor": t}, sem)
        return sem

    def vector_core(sem):
        net.arrived(by_chip.at[0:3], sem)
        held = ref.vec_core
        total = by_chip[0] + by_chip[1] + by_chip[2] + by_chip[3]
        units_total = by_chip[zh] + by_chip[2 + zh]
        held[0:6, :] = total[0:6, :]
        held[6:7, :] = units_total[6:7, :]
        held[7:8, :] = total[7:8, :]
        sem = net.sem()
        net.send(held, ref.vec_core_land, dev_c, sem)
        return sem

    def vector_finish(sem):
        held, land, done = ref.vec_core, ref.vec_core_land, ref.vec_done
        net.arrived(land, sem)
        done[0:7, :] = held[0:7, :] + land[0:7, :]
        done[7:8, :] = jnp.where(home, held[7:8, :], land[7:8, :])

    barrier = pltpu.get_barrier_semaphore()
    peers = (dev_x, dev_y, dev_c, dev_z, dev_far, dev_far_other)
    for peer in peers:
        pl.semaphore_signal(barrier, inc=1, device_id=peer, device_id_type=MESH_IDS)

    coming = {}
    for number, name in enumerate(inputs):
        copy = pltpu.make_async_copy(
            getattr(hbm, name), getattr(held, name), ref.load_sems.at[number]
        )
        copy.start()
        coming[name] = copy
    coming = SimpleNamespace(**coming)
    stores = []

    def store(source, target):
        sem = ref.load_sems.at[len(inputs) + len(stores)]
        copy = pltpu.make_async_copy(source, target, sem)
        copy.start()
        stores.append(copy)

    attn_piece = ref.attn_piece
    if all_lanes > 4 * width:
        attn_piece[:, 4 * width :] = jnp.zeros((piece, all_lanes - 4 * width), bf16)
    for number, (copy, raw) in enumerate(
        (
            (coming.query_w, held.query_w),
            (coming.key_w, held.key_w),
            (coming.value_w, held.value_w),
            (coming.out_w, held.out_w),
        )
    ):
        copy.wait()
        attn_piece[:, number * width : (number + 1) * width] = raw[...]
    vectors[...] = jnp.zeros_like(vectors)
    for number, (copy, raw) in enumerate(
        (
            (coming.first_gain, held.first_gain),
            (coming.first_shift, held.first_shift),
            (coming.out_bias, held.out_bias),
            (coming.second_gain, held.second_gain),
            (coming.second_shift, held.second_shift),
            (coming.down_bias, held.down_bias),
        )
    ):
        copy.wait()
        vectors[number : number + 1, :] = raw[...].reshape(1, D)
    coming.up_bias.wait()
    vectors[6:7, :units] = held.up_bias[...].reshape(1, units)
    coming.query_bias.wait()
    vectors[7:8, :width] = held.query_bias[...].reshape(1, width)
    coming.value_bias.wait()
    vectors[7:8, 2 * width : 3 * width] = held.value_bias[...].reshape(1, width)
    first_gain, first_shift = vectors[0:1, :], vectors[1:2, :]
    out_bias, second_gain = vectors[2:3, :], vectors[3:4, :]
    second_shift, down_bias = vectors[4:5, :], vectors[5:6, :]
    tokens_ref, cotangent_ref = held.tokens, held.cotangent
    coming.tokens.wait()
    coming.cotangent.wait()
    token_rows = tokens_ref[...].astype(f32)
    normed, hat, inv_scale = norm_rows(token_rows, first_gain, first_shift)
    first_all[slot(near, c), :] = normed.astype(bf16)
    ref.first_hat[...] = hat
    ref.row_scale[0] = jnp.broadcast_to(inv_scale, (rows, LANES))

    pl.semaphore_wait(barrier, len(peers))

    first_sems = share_start(first_all)
    lane_cut = round_up(qkv_lanes // 2, LANES)
    q_parts = [(attn_w, 0, lane_cut), (attn_w, lane_cut, qkv_lanes)]
    o_part = (attn_w, qkv_lanes, all_lanes)
    q_base = [spread_start(attn_piece, *part) for part in q_parts]
    o_base = spread_start(attn_piece, *o_part)
    vec_sem = net.sem()
    net.send(vectors, ref.far_vectors, dev_far, vec_sem)
    up_parts = [
        WideGather(ref.up_piece, up_w, ref.up_wait, lo, hi)
        for lo, hi in row_cuts(piece, 2)
    ]
    down_parts = [
        WideGather(ref.down_piece, down_w, ref.down_wait, lo, hi)
        for lo, hi in row_cuts(piece, 3)
    ]

    coming.up_w.wait()
    coming.down_w.wait()
    ref.up_piece[:, main:] = jnp.zeros((piece, LANES), bf16)
    ref.up_piece[:, :units] = held.up_w[...]
    ref.up_piece[:, units : units + rest] = held.down_w[:, main:]
    ref.down_piece[...] = held.down_w[:, :main]
    dy_all[slot(near, kx), :] = cotangent_ref[...]
    vec_own[5:6, :] = jnp.sum(cotangent_ref[...].astype(f32), axis=0, keepdims=True)
    head_rows[...] = jnp.zeros_like(head_rows)
    head_grads[...] = jnp.zeros_like(head_grads)
    mixed_all[...] = jnp.zeros_like(mixed_all)
    qkv_grads[...] = jnp.zeros_like(qkv_grads)

    for part in up_parts:
        part.start(inner)
    dy_sems = plain_share_z(dy_all)
    q_sems = [gather_start(*part, base) for part, base in zip(q_parts, q_base)]
    for part in up_parts:
        part.start(jnp.logical_and(outer, away))
    for part, sems in zip(q_parts, q_sems):
        gather_forward(*part, sems)
    for part in up_parts:
        part.start(jnp.logical_and(outer, home))
    o_sems = gather_start(*o_part, o_base)
    share_forward(first_all, first_sems)
    net.arrived(ref.far_vectors, vec_sem)
    share_near(first_all, first_sems)
    share_deep(first_all, first_sems)
    for part, sems in zip(q_parts, q_sems):
        gather_finish(*part, sems)
    for part in down_parts:
        part.start(outer)
    gather_forward(*o_part, o_sems)
    plain_share_x(dy_all, dy_sems)
    for part in up_parts:
        part.beside()
    for part in down_parts:
        part.beside()

    def shard_vector(row, own):
        return jnp.where(own, vectors[row : row + 1, :], ref.far_vectors[row : row + 1, :])

    qkv_bias = shard_vector(7, home)[:, :qkv_lanes]
    for side_at in range(2):
        side_rows = slice(side_at * pair, (side_at + 1) * pair)
        done = dot_plain(first_all[side_rows, :], attn_w[:, :qkv_lanes])
        done = (done + qkv_bias).astype(bf16)
        for image in range(2):
            to = slice(image * pair + side_at * rows, image * pair + (side_at + 1) * rows)
            for head in range(3 * heads):
                head_rows[head, to, :HD] = done[
                    image * rows : (image + 1) * rows, head * HD : (head + 1) * HD
                ]
    scale = HD ** (-0.5)

    def image_head(step):
        head, image = lax.rem(step, heads), lax.div(step, heads)
        return head, aligned(image * pair, pair)

    def attend(step, carry):
        head, span = image_head(step)
        queries, keys_part = head_rows[head, span, :], head_rows[heads + head, span, :]
        values = head_rows[2 * heads + head, span, :]
        scores = dot_right_t(queries, keys_part) * scale
        expo = jnp.exp(scores - jnp.max(scores, axis=1, keepdims=True))
        probs = expo / jnp.sum(expo, axis=1, keepdims=True)
        ref.probs_all[step] = probs
        mixed = dot_plain(probs.astype(bf16), values)
        ref.mixed_heads[head, span, :] = mixed.astype(bf16)
        return carry

    lax.fori_loop(0, 2 * heads, attend, 0, unroll=2)

    def pack(target, source, count, base):
        for side_at in range(2):
            for image in range(2):
                at = slice(side_at * pair + image * rows, side_at * pair + (image + 1) * rows)
                take = slice(image * pair + side_at * rows, image * pair + (side_at + 1) * rows)
                for head in range(count):
                    lo = base + head * HD
                    target[at, lo : lo + HD] = source[head, take, :HD]

    pack(mixed_all, ref.mixed_heads, heads, win_shift)

    def half(side):
        return aligned(side, pair)

    gather_finish(*o_part, o_sems)
    part_a[half(deep), :] = dot_right_t(mixed_all[half(deep), :], attn_w[:, win:])
    out_sems = sum_deep(0, part_a)
    part_a[half(near), :] = dot_right_t(mixed_all[half(near), :], attn_w[:, win:])
    sum_pass(0, part_a, out_sems)
    sum_near(0, part_a, out_sems)
    for part in up_parts:
        part.second()
    up_parts[0].third()
    attn_rows = sum_finish(0, part_a, out_sems)
    middle = tokens_ref[...].astype(f32) + attn_rows + out_bias
    ref.mid_rows[...] = middle
    normed, hat, inv_scale = norm_rows(middle, second_gain, second_shift)
    second_all[slot(near, kx), :] = normed.astype(bf16)
    ref.second_hat[...] = hat
    ref.row_scale[1] = jnp.broadcast_to(inv_scale, (rows, LANES))
    second_sems = wide_share_start(second_all)
    for part in down_parts:
        part.start(inner)
    up_parts[1].third()
    wide_share_forward(second_all, second_sems)
    for part in down_parts:
        part.second()
    plain_share_forward(dy_all, dy_sems)
    for part in up_parts:
        part.fourth()
    down_parts[0].third()
    for part in up_parts:
        part.finish()
    wide_share_near(second_all, second_sems)

    up_bias = shard_vector(6, stay)
    chunk = 32

    in_rest = lax.broadcasted_iota(jnp.int32, (chunk, LANES), 1) < rest
    hidden_rest = ref.hidden_rest

    def raise_half(side):
        part_b[half(side), :] = dot_plain(second_all[half(side), :], up_w[...])

        def gelu_rows(step, carry):
            at = aligned(side + step * chunk, chunk)
            value, slope = gelu_pair(part_b[at, :] + up_bias)
            last = jnp.where(in_rest, value[:, main:], 0.0)
            hidden_all[at, :main] = value[:, :main].astype(bf16)
            hidden_all[at, main:] = last.astype(bf16)
            hidden_rest[at, :] = pltpu.roll(last, rest, 1).astype(bf16)
            slope_all[at, :] = slope
            return carry

        lax.fori_loop(0, pair // chunk, gelu_rows, 0)

    raise_half(near)
    down_parts[1].third()
    wide_share_deep(second_all, second_sems)
    raise_half(deep)

    tile = 3 * LANES

    def outer_product(grad, left, right, lo, hi):
        def rows_of(step, carry):
            at = aligned(step * tile, tile)
            grad[at, lo:hi] = dot_left_t(left[:, at], right).astype(bf16)
            return carry

        lax.fori_loop(0, D // tile, rows_of, 0)

    down_parts[2].third()
    down_parts[0].fourth()
    plain_share_finish(dy_all, dy_sems)
    outer_product(down_g, dy_all, hidden_all[:, :main], 0, main)
    down_reduce = wide_reduce_first(down_g, ref.land_d)
    down_parts[1].fourth()
    wide_reduce_second(down_g, ref.land_d, down_reduce)
    down_parts[2].fourth()
    for part in down_parts:
        part.finish()

    def lower_half(side):
        part_b[half(side), :main] = dot_plain(dy_all[half(side), :], down_w[...])
        part_b[half(side), main:] = dot_plain(dy_all[half(side), :], up_w[:, main:])

        def slope_rows(step, totals):
            at = aligned(side + step * chunk, chunk)
            last = pltpu.roll(part_b[at, main:], LANES - rest, 1)
            last = jnp.where(in_rest, last * slope_all[at, main:], 0.0).astype(bf16)
            low = (part_b[at, :main] * slope_all[at, :main]).astype(bf16)
            upper_all[at, :main] = low
            upper_all[at, main:] = last
            return (
                totals[0] + jnp.sum(low.astype(f32), axis=0, keepdims=True),
                totals[1] + jnp.sum(last.astype(f32), axis=0, keepdims=True),
            )

        start = jnp.zeros((1, main), f32), jnp.zeros((1, LANES), f32)
        return lax.fori_loop(0, pair // chunk, slope_rows, start)

    def up_rows(step, carry):
        at = aligned(step * tile, tile)
        by_row = second_all[:, at]
        up_g[at, :main] = dot_left_t(by_row, upper_all[:, :main]).astype(bf16)
        last = dot_left_t(by_row, upper_all[:, main:])
        last = last + dot_left_t(dy_all[:, at], hidden_rest[...])
        up_g[at, main:] = last.astype(bf16)
        return carry

    up_bias_sum = lower_half(deep)
    part_a[half(deep), :] = dot_right_t(upper_all[half(deep), :], up_w[...])
    second_sum_sems = wide_sum_deep(0, part_a)
    more_sum = lower_half(near)
    vec_own[6:7, :main] = up_bias_sum[0] + more_sum[0]
    vec_own[6:7, main:] = up_bias_sum[1] + more_sum[1]
    part_a[half(near), :] = dot_right_t(upper_all[half(near), :], up_w[...])
    wide_sum_near(0, part_a, second_sum_sems)
    lax.fori_loop(0, D // tile, up_rows, 0)
    up_reduce = wide_reduce_first(up_g, ref.land_u)
    wide_sum_pass(0, part_a, second_sum_sems)
    wide_reduce_second(up_g, ref.land_u, up_reduce)
    wide_reduce_third(down_g, ref.land_d, down_reduce)
    second_grad = wide_sum_finish(0, part_a, second_sum_sems)
    back, gain_sum, shift_sum = norm_back(
        second_grad, ref.second_hat[...], ref.row_scale[1][:, :1], second_gain
    )
    vec_own[3:4, :] = gain_sum[None, :]
    vec_own[4:5, :] = shift_sum[None, :]
    total = cotangent_ref[...].astype(f32) + back
    ref.mid_grad[...] = total
    low = total.astype(bf16)
    mid_all[slot(near, c), :] = low
    vec_own[2:3, :] = jnp.sum(low.astype(f32), axis=0, keepdims=True)
    mid_sems = share_start(mid_all)

    def lower_product(side):
        total = dot_right_t(hidden_all[half(side), :main], down_w[...])
        return total + dot_right_t(hidden_rest[half(side), :], up_w[:, main:])

    part_b[half(deep), :] = lower_product(deep)
    mlp_sems = wide_sum_deep(1, part_b)
    part_b[half(near), :] = lower_product(near)
    wide_sum_near(1, part_b, mlp_sems)
    def head_half(side_at):
        side_rows = slice(side_at * pair, (side_at + 1) * pair)
        done = dot_plain(mid_all[side_rows, :], attn_w[:, win:]).astype(bf16)
        for image in range(2):
            to = slice(image * pair + side_at * rows, image * pair + (side_at + 1) * rows)
            for head in range(heads):
                lo = win_shift + head * HD
                head_grads[head, to, :HD] = done[image * rows : (image + 1) * rows, lo : lo + HD]

    share_forward(mid_all, mid_sems)
    share_near(mid_all, mid_sems)
    wide_reduce_cross(down_g, ref.land_d, down_reduce, when=outer)
    wide_reduce_fourth(down_g, ref.land_d, down_reduce, when=outer)
    share_deep(mid_all, mid_sems)
    head_half(0)
    head_half(1)
    wide_reduce_third(up_g, ref.land_u, up_reduce)
    wide_reduce_cross(down_g, ref.land_d, down_reduce, when=inner)
    wide_reduce_fourth(down_g, ref.land_d, down_reduce, when=inner)

    cut = round_up(2 * width, LANES)

    def value_back(step, carry):
        head, span = image_head(step)
        low = ref.probs_all[step].astype(bf16)
        value_grad = dot_left_t(low, head_grads[head, span, :])
        ref.mixed_heads[head, span, :] = value_grad.astype(bf16)
        return carry

    def value_out_rows(step, carry):
        at = aligned(step * tile, tile)
        by_value = dot_left_t(first_all[:, at], qkv_grads[:, cut:qkv_lanes])
        by_out = dot_left_t(mid_all[:, at], mixed_all[...])
        both = by_value[:, win - cut :] + by_out[:, :skip]
        attn_g[at, cut:win] = by_value[:, : win - cut].astype(bf16)
        attn_g[at, win:qkv_lanes] = both.astype(bf16)
        attn_g[at, qkv_lanes:] = by_out[:, skip:].astype(bf16)
        return carry

    lax.fori_loop(0, 2 * heads, value_back, 0, unroll=2)
    pack(qkv_grads, ref.mixed_heads, heads, 2 * width)
    lax.fori_loop(0, D // tile, value_out_rows, 0)
    vo_args = attn_g, ref.land_vo, cut, all_lanes, net.sems(8)
    reduce_first(*vo_args)

    wide_sum_pass(1, part_b, mlp_sems)

    def attend_back(step, carry):
        head, span = image_head(step)
        queries, keys_part = head_rows[head, span, :], head_rows[heads + head, span, :]
        values, grads = head_rows[2 * heads + head, span, :], head_grads[head, span, :]
        probs = ref.probs_all[step]
        prob_grad = dot_right_t(grads, values)
        row_dot = jnp.sum(probs * prob_grad, axis=1, keepdims=True)
        score_grad = (probs * (prob_grad - row_dot)).astype(bf16)
        query_grad = dot_plain(score_grad, keys_part) * scale
        key_grad = dot_left_t(score_grad, queries) * scale
        head_rows[head, span, :] = query_grad.astype(bf16)
        head_rows[heads + head, span, :] = key_grad.astype(bf16)
        return carry

    lax.fori_loop(0, 2 * heads, attend_back, 0, unroll=2)
    pack(qkv_grads, head_rows, 2 * heads, 0)
    wide_reduce_cross(up_g, ref.land_u, up_reduce, when=outer)
    wide_reduce_fourth(up_g, ref.land_u, up_reduce, when=outer)
    part_a[half(deep), :] = dot_right_t(
        qkv_grads[half(deep), :qkv_lanes], attn_w[:, :qkv_lanes]
    )
    first_sum_sems = sum_deep(1, part_a)
    part_a[half(near), :] = dot_right_t(
        qkv_grads[half(near), :qkv_lanes], attn_w[:, :qkv_lanes]
    )
    sum_pass(1, part_a, first_sum_sems)
    sum_near(1, part_a, first_sum_sems)
    vec_own[7:8, :] = jnp.sum(qkv_grads[...].astype(f32), axis=0, keepdims=True)
    outer_product(attn_g, first_all, qkv_grads[:, :cut], 0, cut)
    qk_args = attn_g, ref.land_qk, 0, cut, net.sems(8)
    reduce_first(*qk_args, when=away)
    reduce_second(*vo_args)
    wide_reduce_cross(up_g, ref.land_u, up_reduce, when=inner)
    wide_reduce_fourth(up_g, ref.land_u, up_reduce, when=inner)
    reduce_second(*qk_args, when=away)
    first_grad = sum_finish(1, part_a, first_sum_sems)
    back, gain_sum, shift_sum = norm_back(
        first_grad, ref.first_hat[...], ref.row_scale[0][:, :1], first_gain
    )
    vec_own[0:1, :] = gain_sum[None, :]
    vec_own[1:2, :] = shift_sum[None, :]
    vec_sem = vector_planes()
    ref.mid_grad[...] = ref.mid_grad[...] + back
    store(ref.mid_grad, out.input_grad)
    reduce_first(*qk_args, when=home)
    reduce_third(*vo_args)
    reduce_third(*qk_args, when=away)
    vec_sem = vector_chips(vec_sem)
    vec_sem = vector_core(vec_sem)
    reduce_second(*qk_args, when=home)
    vector_finish(vec_sem)
    store(ref.vec_done, out.vector_grad)
    reduce_third(*qk_args, when=home)
    ref.down_buf[...] = wide_reduce_finish(down_g, ref.land_d, down_reduce)
    store(ref.down_buf, out.down_grad)
    mlp_rows = wide_sum_finish(1, part_b, mlp_sems)
    ref.layer_buf[...] = (ref.mid_rows[...] + mlp_rows + down_bias).astype(bf16)
    store(ref.layer_buf, out.layer_out)
    ref.up_buf[...] = wide_reduce_finish(up_g, ref.land_u, up_reduce)
    store(ref.up_buf, out.up_grad)
    ref.attn_buf[:, cut:] = reduce_finish(ref.land_vo, vo_args[4])
    store(ref.attn_buf.at[:, cut:], out.attn_grad.at[:, cut:])
    ref.attn_buf[:, :cut] = reduce_finish(ref.land_qk, qk_args[4])
    store(ref.attn_buf.at[:, :cut], out.attn_grad.at[:, :cut])
    net.drain()
    assert net.used <= ref.recv_sems.shape[0]
    for copy in stores:
        copy.wait()


def format_kernel(shapes, *refs):
    width, units = shapes
    inputs, refs = refs[:6], refs[6:]
    outs, refs = refs[:17], refs[17:]
    held, refs = refs[:6], refs[6:]
    shaped, sems = refs[:-1], refs[-1]
    copies = [
        pltpu.make_async_copy(source, target, sems.at[number])
        for number, (source, target) in enumerate(zip(inputs, held, strict=True))
    ]
    for copy in copies:
        copy.start()
    going = []

    def put(source, number):
        copy = pltpu.make_async_copy(source, outs[number], sems.at[6 + number])
        copy.start()
        going.append(copy)

    def put_shaped(number, value):
        shaped[number - 2][...] = value
        put(shaped[number - 2], number)

    copies[0].wait()
    put(held[0], 0)
    copies[1].wait()
    put(held[1], 1)
    copies[2].wait()
    for number, place in ((4, 0), (5, 1), (6, 2), (9, 3)):
        put_shaped(number, held[2][:, place * width : (place + 1) * width])
    copies[3].wait()
    put_shaped(13, held[3][:, :units])
    copies[4].wait()
    main = held[4].shape[1]
    shaped[13][:, :main] = held[4][...]
    shaped[13][:, main:] = held[3][:, units : 2 * units - main]
    put(shaped[13], 15)
    copies[5].wait()
    for number, row, lo, size in (
        (2, 0, 0, D),
        (3, 1, 0, D),
        (10, 2, 0, D),
        (11, 3, 0, D),
        (12, 4, 0, D),
        (16, 5, 0, D),
        (14, 6, 0, units),
        (7, 7, 0, width),
        (8, 7, 2 * width, width),
    ):
        put_shaped(number, held[5][row, lo : lo + size])
    for copy in going:
        copy.wait()


def fused_step(
    tokens,
    cotangent,
    first_gain,
    first_shift,
    query_weight,
    key_weight,
    value_weight,
    query_bias,
    value_bias,
    out_weight,
    out_bias,
    second_gain,
    second_shift,
    up_weight,
    up_bias,
    down_weight,
    down_bias,
):
    bf16, f32 = jnp.bfloat16, jnp.float32
    rows, piece, width, units = (
        tokens.shape[0],
        query_weight.shape[0],
        query_weight.shape[1],
        up_weight.shape[1],
    )
    heads = width // HD
    group = 4 * rows
    qkv_lanes = round_up(3 * width, LANES)
    attn_lanes = round_up(4 * width, LANES)
    ff_lanes = round_up(units, LANES)
    main = units // LANES * LANES
    assert 2 * (units - main) <= LANES < ff_lanes - main + 1
    win = 3 * width // LANES * LANES
    given = dict(
        query_w=query_weight,
        key_w=key_weight,
        value_w=value_weight,
        out_w=out_weight.T,
        first_gain=first_gain,
        first_shift=first_shift,
        out_bias=out_bias,
        second_gain=second_gain,
        second_shift=second_shift,
        down_bias=down_bias,
        up_bias=up_bias,
        query_bias=query_bias,
        value_bias=value_bias,
        tokens=tokens,
        cotangent=cotangent,
        up_w=up_weight,
        down_w=down_weight.T,
    )
    place = pl.BlockSpec(memory_space=pl.ANY)
    cut = round_up(2 * width, LANES)
    raw_outs = dict(
        layer_out=jax.ShapeDtypeStruct((rows, D), bf16),
        input_grad=jax.ShapeDtypeStruct((rows, D), f32),
        attn_grad=jax.ShapeDtypeStruct((piece, attn_lanes), f32),
        up_grad=jax.ShapeDtypeStruct((piece, ff_lanes), f32),
        down_grad=jax.ShapeDtypeStruct((piece, main), f32),
        vector_grad=jax.ShapeDtypeStruct((8, D), f32),
    )
    scratch = dict(
        attn_piece=pltpu.VMEM((piece, attn_lanes), bf16),
        up_piece=pltpu.VMEM((piece, ff_lanes), bf16),
        down_piece=pltpu.VMEM((piece, main), bf16),
        up_wait=pltpu.VMEM((piece, ff_lanes), bf16),
        down_wait=pltpu.VMEM((piece, main), bf16),
        attn_w=pltpu.VMEM((D, attn_lanes), bf16),
        up_w=pltpu.VMEM((D, ff_lanes), bf16),
        down_w=pltpu.VMEM((D, main), bf16),
        attn_g=pltpu.VMEM((D, attn_lanes), bf16),
        up_g=pltpu.VMEM((D, ff_lanes), bf16),
        down_g=pltpu.VMEM((D, main), bf16),
        land_vo=pltpu.VMEM((8, piece, attn_lanes - cut), bf16),
        land_qk=pltpu.VMEM((8, piece, cut), bf16),
        land_u=pltpu.VMEM((8, piece, ff_lanes), bf16),
        land_d=pltpu.VMEM((8, piece, main), bf16),
        first_all=pltpu.VMEM((group, D), bf16),
        second_all=pltpu.VMEM((group, D), bf16),
        dy_all=pltpu.VMEM((group, D), bf16),
        mid_all=pltpu.VMEM((group, D), bf16),
        head_rows=pltpu.VMEM((3 * heads, group, LANES), bf16),
        head_grads=pltpu.VMEM((heads, group, LANES), bf16),
        probs_all=pltpu.VMEM((2 * heads, 2 * rows, 2 * rows), f32),
        mixed_heads=pltpu.VMEM((heads, group, LANES), bf16),
        mixed_all=pltpu.VMEM((group, attn_lanes - win), bf16),
        hidden_all=pltpu.VMEM((group, ff_lanes), bf16),
        hidden_rest=pltpu.VMEM((group, LANES), bf16),
        slope_all=pltpu.VMEM((group, ff_lanes), f32),
        upper_all=pltpu.VMEM((group, ff_lanes), bf16),
        qkv_grads=pltpu.VMEM((group, attn_lanes), bf16),
        part_a=pltpu.VMEM((group, D), f32),
        part_b=pltpu.VMEM((group, D), f32),
        core_send=pltpu.VMEM((2, 2, rows, D), bf16),
        core_land=pltpu.VMEM((2, 2, rows, D), bf16),
        deep_send=pltpu.VMEM((2, rows, D), bf16),
        deep_land=pltpu.VMEM((2, rows, D), bf16),
        wide_send=pltpu.VMEM((2, 6, rows // 2, D), bf16),
        wide_land=pltpu.VMEM((2, 6, rows // 2, D), bf16),
        first_hat=pltpu.VMEM((rows, D), f32),
        second_hat=pltpu.VMEM((rows, D), f32),
        mid_rows=pltpu.VMEM((rows, D), f32),
        mid_grad=pltpu.VMEM((rows, D), f32),
        row_scale=pltpu.VMEM((2, rows, LANES), f32),
        vectors=pltpu.VMEM((8, D), f32),
        far_vectors=pltpu.VMEM((8, D), f32),
        vec_own=pltpu.VMEM((8, D), f32),
        by_plane=pltpu.VMEM((4, 8, D), f32),
        vec_chip=pltpu.VMEM((8, D), f32),
        by_chip=pltpu.VMEM((4, 8, D), f32),
        vec_core=pltpu.VMEM((8, D), f32),
        vec_core_land=pltpu.VMEM((8, D), f32),
        vec_done=pltpu.VMEM((8, D), f32),
        layer_buf=pltpu.VMEM((rows, D), bf16),
        attn_buf=pltpu.VMEM((piece, attn_lanes), f32),
        up_buf=pltpu.VMEM((piece, ff_lanes), f32),
        down_buf=pltpu.VMEM((piece, main), f32),
        load_sems=pltpu.SemaphoreType.DMA((len(given) + len(raw_outs) + 1,)),
        send_sems=pltpu.SemaphoreType.DMA((64,)),
        recv_sems=pltpu.SemaphoreType.DMA((112,)),
    )
    shapes = (rows, heads, width, units, qkv_lanes, piece)
    names = tuple(given), tuple(raw_outs), tuple(scratch)

    def body(*refs):
        layer_kernel(shapes, names, *refs)

    raw = pl.pallas_call(
        body,
        out_shape=tuple(raw_outs.values()),
        in_specs=[place] * len(given),
        out_specs=(place,) * len(raw_outs),
        scratch_shapes=[
            *(pltpu.VMEM(array.shape, array.dtype) for array in given.values()),
            *scratch.values(),
        ],
        compiler_params=pltpu.CompilerParams(
            collective_id=0, has_side_effects=True, vmem_limit_bytes=67043328
        ),
        name="layer",
    )(*given.values())
    raw_outs = tuple(raw_outs.values())

    vector, narrow = jax.ShapeDtypeStruct((D,), f32), jax.ShapeDtypeStruct((width,), f32)
    attn_out = jax.ShapeDtypeStruct((piece, width), f32)
    ff_out = jax.ShapeDtypeStruct((piece, units), f32)
    outs = (
        *raw_outs[:2],
        vector,
        vector,
        attn_out,
        attn_out,
        attn_out,
        narrow,
        narrow,
        attn_out,
        vector,
        vector,
        vector,
        ff_out,
        jax.ShapeDtypeStruct((units,), f32),
        ff_out,
        vector,
    )

    def format_body(*refs):
        format_kernel((width, units), *refs)

    done = pl.pallas_call(
        format_body,
        out_shape=outs,
        in_specs=[place] * 6,
        out_specs=(place,) * 17,
        scratch_shapes=[
            *(pltpu.VMEM(item.shape, item.dtype) for item in raw_outs),
            *(pltpu.VMEM(item.shape, item.dtype) for item in outs[2:]),
            pltpu.SemaphoreType.DMA((6 + 17,)),
        ],
        compiler_params=pltpu.CompilerParams(vmem_limit_bytes=67043328),
        name="outputs",
    )(*raw)
    done = list(done)
    done[9], done[15] = done[9].T, done[15].T
    return tuple(done)


def pick_step(mesh):
    if mesh.shape["fsdp"] == 8 and mesh.shape["tensor"] == 4:
        return fused_step
    return on_device


def solution(mesh):
    return jax.shard_map(
        pick_step(mesh),
        mesh=mesh,
        in_specs=(
            P(("fsdp", "tensor"), None),
            P(("fsdp", "tensor"), None),
            P(),
            P(),
            P("fsdp", "tensor"),
            P("fsdp", "tensor"),
            P("fsdp", "tensor"),
            P("tensor"),
            P("tensor"),
            P("tensor", "fsdp"),
            P(),
            P(),
            P(),
            P("fsdp", "tensor"),
            P("tensor"),
            P("tensor", "fsdp"),
            P(),
        ),
        out_specs=(
            P(("fsdp", "tensor"), None),
            P(("fsdp", "tensor"), None),
            P(),
            P(),
            P("fsdp", "tensor"),
            P("fsdp", "tensor"),
            P("fsdp", "tensor"),
            P("tensor"),
            P("tensor"),
            P("tensor", "fsdp"),
            P(),
            P(),
            P(),
            P("fsdp", "tensor"),
            P("tensor"),
            P("tensor", "fsdp"),
            P(),
        ),
        check_vma=False,
    )
```

```python
import math
from types import SimpleNamespace

import jax
import jax.numpy as jnp
from jax import lax
from jax.experimental import pallas as pl
from jax.experimental.pallas import tpu as pltpu
from jax.sharding import PartitionSpec as P

D = 1152
HD = 72
FF = 4304
SEQ = 256


norm_eps = 1e-06
gelu_coef = 0.7978845608028654
cubic_coef = 0.044715


def dot_plain(left, right):
    return jnp.dot(left, right, preferred_element_type=jnp.float32)


def dot_right_t(left, right):
    return lax.dot_general(
        left, right, (((1,), (1,)), ((), ())), preferred_element_type=jnp.float32
    )


def dot_left_t(left, right):
    return lax.dot_general(
        left, right, (((0,), (0,)), ((), ())), preferred_element_type=jnp.float32
    )


def norm_rows(values, gain, shift):
    row_mean = jnp.mean(values, axis=1, keepdims=True)
    centred = values - row_mean
    inv_scale = lax.rsqrt(jnp.mean(centred * centred, axis=1, keepdims=True) + norm_eps)
    normed = centred * inv_scale
    return (normed * gain + shift, normed, inv_scale)


def norm_back(out_grad, normed, inv_scale, gain):
    scaled_grad = out_grad * gain
    grad_mean = jnp.mean(scaled_grad, axis=1, keepdims=True)
    cross_mean = jnp.mean(scaled_grad * normed, axis=1, keepdims=True)
    in_grad = inv_scale * (scaled_grad - grad_mean - normed * cross_mean)
    return (in_grad, jnp.sum(out_grad * normed, axis=0), jnp.sum(out_grad, axis=0))


def gelu_pair(upper):
    tangent = jnp.tanh(gelu_coef * (upper + cubic_coef * upper * upper * upper))
    gelu_value = 0.5 * upper * (1.0 + tangent)
    gelu_slope = 0.5 * (1.0 + tangent) + 0.5 * upper * (1.0 - tangent * tangent) * gelu_coef * (
        1.0 + 3.0 * cubic_coef * upper * upper
    )
    return (gelu_value, gelu_slope)


def split_heads(block_rows, head_count):
    col_width = block_rows.shape[1] // 3
    img_count = block_rows.shape[0] // SEQ
    shape_four = (img_count, SEQ, head_count, HD)
    queries = block_rows[:, :col_width].reshape(shape_four)
    keys_part = block_rows[:, col_width : 2 * col_width].reshape(shape_four)
    values = block_rows[:, 2 * col_width :].reshape(shape_four)
    return (queries, keys_part, values, shape_four)


def attend_forward(block_rows, head_count):
    queries, keys_part, values, shape_four = split_heads(block_rows, head_count)
    scores = jnp.einsum(
        "nqhd,nkhd->nhqk", queries, keys_part, preferred_element_type=jnp.float32
    ) * HD ** (-0.5)
    peak = jnp.max(scores, axis=-1, keepdims=True)
    expo = jnp.exp(scores - peak)
    totals = jnp.sum(expo, axis=-1, keepdims=True)
    prob_low = (expo / totals).astype(jnp.bfloat16)
    mixed = jnp.einsum("nhqk,nkhd->nqhd", prob_low, values, preferred_element_type=jnp.float32)
    row_total = block_rows.shape[0]
    mixed = mixed.reshape(row_total, head_count * HD).astype(jnp.bfloat16)
    return (mixed, (peak + jnp.log(totals))[..., 0])


def attend_backward(inputs, head_count):
    block_rows, grad_block, log_total = inputs
    queries, keys_part, values, shape_four = split_heads(block_rows, head_count)
    grad_out = grad_block.reshape(shape_four)
    scores = jnp.einsum(
        "nqhd,nkhd->nhqk", queries, keys_part, preferred_element_type=jnp.float32
    ) * HD ** (-0.5)
    probs = jnp.exp(scores - log_total[..., None])
    prob_low = probs.astype(jnp.bfloat16)
    value_grad = jnp.einsum(
        "nhqk,nqhd->nkhd", prob_low, grad_out, preferred_element_type=jnp.float32
    )
    prob_grad = jnp.einsum("nqhd,nkhd->nhqk", grad_out, values, preferred_element_type=jnp.float32)
    row_dot = jnp.sum(probs * prob_grad, axis=-1, keepdims=True)
    score_grad = (probs * (prob_grad - row_dot)).astype(jnp.bfloat16)
    query_grad = jnp.einsum(
        "nhqk,nkhd->nqhd", score_grad, keys_part, preferred_element_type=jnp.float32
    ) * HD ** (-0.5)
    key_grad = jnp.einsum(
        "nhqk,nqhd->nkhd", score_grad, queries, preferred_element_type=jnp.float32
    ) * HD ** (-0.5)
    row_total = block_rows.shape[0]
    col_width = head_count * HD
    return jnp.concatenate(
        (
            query_grad.reshape(row_total, col_width),
            key_grad.reshape(row_total, col_width),
            value_grad.reshape(row_total, col_width),
        ),
        axis=1,
    ).astype(jnp.bfloat16)


def on_device(
    tokens,
    cotangent,
    first_gain,
    first_shift,
    query_weight,
    key_weight,
    value_weight,
    query_bias,
    value_bias,
    out_weight,
    out_bias,
    second_gain,
    second_shift,
    up_weight,
    up_bias,
    down_weight,
    down_bias,
):
    full_query, full_key, full_value, full_outp, full_up, full_down = (
        lax.all_gather(query_weight, "fsdp", axis=0, tiled=True),
        lax.all_gather(key_weight, "fsdp", axis=0, tiled=True),
        lax.all_gather(value_weight, "fsdp", axis=0, tiled=True),
        lax.all_gather(out_weight, "fsdp", axis=1, tiled=True),
        lax.all_gather(up_weight, "fsdp", axis=0, tiled=True),
        lax.all_gather(down_weight, "fsdp", axis=1, tiled=True),
    )
    qkv_weight = jnp.concatenate((full_query, full_key, full_value), axis=1)
    local_width = full_query.shape[1]
    ffn_width = full_up.shape[1]
    head_count = local_width // HD
    token_rows = tokens.astype(jnp.float32)
    first_out, first_hat, first_scale = norm_rows(token_rows, first_gain, first_shift)
    all_first = lax.all_gather(first_out.astype(jnp.bfloat16), "tensor", axis=0, tiled=True)
    qkv_bias = jnp.concatenate((query_bias, jnp.zeros_like(query_bias), value_bias))
    qkv_rows = (dot_plain(all_first, qkv_weight) + qkv_bias).astype(jnp.bfloat16)
    group_rows = qkv_rows.shape[0]
    images = group_rows // SEQ
    per_block = math.gcd(images, max(1, 512 // SEQ))
    blocks = images // per_block
    stacked = qkv_rows.reshape(blocks, per_block * SEQ, 3 * local_width)

    def forward_block(block_rows):
        return attend_forward(block_rows, head_count)

    head_out, log_total = lax.map(forward_block, stacked)
    head_out = head_out.reshape(group_rows, local_width)
    attn_rows = lax.psum_scatter(
        dot_plain(head_out, full_outp), "tensor", scatter_dimension=0, tiled=True
    )
    mid_rows = token_rows + attn_rows + out_bias
    second_out, second_hat, second_scale = norm_rows(mid_rows, second_gain, second_shift)
    all_second = lax.all_gather(second_out.astype(jnp.bfloat16), "tensor", axis=0, tiled=True)
    up_pre = dot_plain(all_second, full_up) + up_bias
    hidden_value, hidden_slope = gelu_pair(up_pre)
    hidden_low = hidden_value.astype(jnp.bfloat16)
    mlp_rows = lax.psum_scatter(
        dot_plain(hidden_low, full_down).astype(jnp.bfloat16),
        "tensor",
        scatter_dimension=0,
        tiled=True,
    ).astype(jnp.float32)
    layer_out = (mid_rows + mlp_rows + down_bias).astype(jnp.bfloat16)
    out_grad = cotangent.astype(jnp.float32)
    all_out_grad = lax.all_gather(cotangent, "tensor", axis=0, tiled=True)
    down_grad = dot_left_t(hidden_low, all_out_grad)
    hidden_grad = dot_right_t(all_out_grad, full_down)
    upper_low = (hidden_grad * hidden_slope).astype(jnp.bfloat16)
    up_bias_grad = jnp.sum(upper_low.astype(jnp.float32), axis=0)
    up_grad = dot_left_t(all_second, upper_low)
    second_grad = lax.psum_scatter(
        dot_right_t(upper_low, full_up), "tensor", scatter_dimension=0, tiled=True
    )
    back_second, second_gain_grad, second_shift_grad = norm_back(
        second_grad, second_hat, second_scale, second_gain
    )
    mid_grad = out_grad + back_second
    mid_low = mid_grad.astype(jnp.bfloat16)
    all_mid_grad = lax.all_gather(mid_low, "tensor", axis=0, tiled=True)
    outp_grad = dot_left_t(head_out, all_mid_grad)
    head_grad = dot_right_t(all_mid_grad, full_outp).astype(jnp.bfloat16)

    def backward_block(inputs):
        return attend_backward(inputs, head_count)

    qkv_grad = lax.map(
        backward_block,
        (stacked, head_grad.reshape(blocks, per_block * SEQ, local_width), log_total),
    )
    qkv_grad = qkv_grad.reshape(group_rows, 3 * local_width)
    qkv_weight_grad = dot_left_t(all_first, qkv_grad)
    qkv_bias_grad = jnp.sum(qkv_grad.astype(jnp.float32), axis=0)
    first_grad = lax.psum_scatter(
        dot_right_t(qkv_grad, qkv_weight).astype(jnp.bfloat16),
        "tensor",
        scatter_dimension=0,
        tiled=True,
    ).astype(jnp.float32)
    back_first, first_gain_grad, first_shift_grad = norm_back(
        first_grad, first_hat, first_scale, first_gain
    )
    input_grad = mid_grad + back_first
    out_bias_grad = jnp.sum(mid_low.astype(jnp.float32), axis=0)
    down_bias_grad = jnp.sum(out_grad, axis=0)
    small_terms = jnp.concatenate(
        (
            first_gain_grad,
            first_shift_grad,
            out_bias_grad,
            second_gain_grad,
            second_shift_grad,
            down_bias_grad,
        )
    )
    tensor_index = lax.axis_index("tensor")
    head_terms = jnp.zeros((2 * D + FF,), jnp.float32)
    head_terms = lax.dynamic_update_slice(
        head_terms, qkv_bias_grad[:local_width], (tensor_index * local_width,)
    )
    head_terms = lax.dynamic_update_slice(
        head_terms, qkv_bias_grad[2 * local_width :], (D + tensor_index * local_width,)
    )
    head_terms = lax.dynamic_update_slice(
        head_terms, up_bias_grad, (2 * D + tensor_index * ffn_width,)
    )
    small_sums, head_sums = lax.psum((small_terms, head_terms), ("fsdp", "tensor"))
    query_bias_total = lax.dynamic_slice(head_sums, (tensor_index * local_width,), (local_width,))
    value_bias_total = lax.dynamic_slice(
        head_sums, (D + tensor_index * local_width,), (local_width,)
    )
    up_bias_total = lax.dynamic_slice(head_sums, (2 * D + tensor_index * ffn_width,), (ffn_width,))
    query_part, key_part, value_part, outp_part, up_part, down_part = (
        lax.psum_scatter(qkv_weight_grad[:, :local_width], "fsdp", scatter_dimension=0, tiled=True),
        lax.psum_scatter(
            qkv_weight_grad[:, local_width : 2 * local_width],
            "fsdp",
            scatter_dimension=0,
            tiled=True,
        ),
        lax.psum_scatter(
            qkv_weight_grad[:, 2 * local_width :], "fsdp", scatter_dimension=0, tiled=True
        ),
        lax.psum_scatter(outp_grad, "fsdp", scatter_dimension=1, tiled=True),
        lax.psum_scatter(up_grad, "fsdp", scatter_dimension=0, tiled=True),
        lax.psum_scatter(down_grad, "fsdp", scatter_dimension=1, tiled=True),
    )
    return (
        layer_out,
        input_grad,
        small_sums[0:D],
        small_sums[D : 2 * D],
        query_part,
        key_part,
        value_part,
        query_bias_total,
        value_bias_total,
        outp_part,
        small_sums[2 * D : 3 * D],
        small_sums[3 * D : 4 * D],
        small_sums[4 * D : 5 * D],
        up_part,
        up_bias_total,
        down_part,
        small_sums[5 * D : 6 * D],
    )


MESH_IDS = pl.DeviceIdType.MESH
LANES = 128


def round_up(value, step):
    return -(-value // step) * step


def row_cuts(count, parts):
    edges = [min(count, round_up(count * at // parts, 16)) for at in range(parts + 1)]
    return list(zip(edges[:-1], edges[1:]))


class Remote:
    def __init__(self, send_sems, recv_sems):
        self.send_sems, self.recv_sems = send_sems, recv_sems
        self.used = 0
        self.sent = 0
        self.slots = [None] * send_sems.shape[0]

    def sem(self):
        self.used += 1
        return self.used - 1

    def sems(self, count):
        return [self.sem() for _ in range(count)]

    def release(self, slot):
        if self.slots[slot] is not None:
            copy, when = self.slots[slot]
            guarded(when, copy.wait_send)

    def send(self, src, dst, device, recv, when=None):
        slot = self.sent % len(self.slots)
        self.sent += 1
        self.release(slot)
        copy = pltpu.make_async_remote_copy(
            src_ref=src,
            dst_ref=dst,
            send_sem=self.send_sems.at[slot],
            recv_sem=self.recv_sems.at[recv],
            device_id=device,
            device_id_type=MESH_IDS,
        )
        guarded(when, copy.start)
        self.slots[slot] = copy, when

    def local(self, src, dst, sem, when):
        copy = pltpu.make_async_copy(src, dst, self.recv_sems.at[sem])
        guarded(when, copy.start)

    def arrived(self, dst, sem):
        pltpu.make_async_copy(dst, dst, self.recv_sems.at[sem]).wait()

    def drain(self):
        for slot in range(len(self.slots)):
            self.release(slot)


def guarded(when, action):
    if when is None:
        action()
    else:
        pl.when(when)(action)


def layer_kernel(shapes, names, *refs):
    rows, heads, width, units, qkv_lanes, piece = shapes
    inputs, outputs, scratch = names
    hbm = SimpleNamespace(**dict(zip(inputs, refs[: len(inputs)], strict=True)))
    refs = refs[len(inputs) :]
    out = SimpleNamespace(**dict(zip(outputs, refs[: len(outputs)], strict=True)))
    refs = refs[len(outputs) :]
    held = SimpleNamespace(**dict(zip(inputs, refs[: len(inputs)], strict=True)))
    refs = refs[len(inputs) :]
    ref = SimpleNamespace(**dict(zip(scratch, refs, strict=True)))
    bf16, f32 = jnp.bfloat16, jnp.float32
    attn_w, up_w, down_w = ref.attn_w, ref.up_w, ref.down_w
    attn_g, up_g, down_g = ref.attn_g, ref.up_g, ref.down_g
    first_all, second_all = ref.first_all, ref.second_all
    dy_all, mid_all = ref.dy_all, ref.mid_all
    head_rows, head_grads = ref.head_rows, ref.head_grads
    mixed_all, hidden_all, upper_all = ref.mixed_all, ref.hidden_all, ref.upper_all
    slope_all, qkv_grads = ref.slope_all, ref.qkv_grads
    part_a, part_b, vectors = ref.part_a, ref.part_b, ref.vectors
    pair, fourth = 2 * rows, rows // 2
    out_base = 3 * width
    win = out_base // LANES * LANES
    win_shift = out_base - win
    skip = qkv_lanes - win
    all_lanes, ff_lanes = attn_w.shape[1], up_w.shape[1]
    main = units // LANES * LANES
    rest = units - main

    f = lax.axis_index("fsdp")
    t = lax.axis_index("tensor")
    c, k = lax.rem(f, 2), lax.div(f, 2)
    kx, ky = lax.rem(k, 2), lax.div(k, 2)
    zl, zh = lax.rem(t, 2), lax.div(t, 2)
    oc, ox = 1 - c, 1 - kx
    k_x, k_y, k_d = ky * 2 + ox, (1 - ky) * 2 + kx, (1 - ky) * 2 + ox
    home = c == zh
    away = jnp.logical_not(home)
    stay = kx == zh
    outer = zl == zh
    inner = jnp.logical_not(outer)
    move = jnp.logical_not(stay)
    far_t = (1 - zh) * 2 + zl
    dev_x = {"fsdp": 2 * k_x + c, "tensor": t}
    dev_y = {"fsdp": 2 * k_y + c, "tensor": t}
    dev_c = {"fsdp": 2 * k + oc, "tensor": t}
    dev_z = {"fsdp": f, "tensor": zh * 2 + (1 - zl)}
    dev_far = {"fsdp": f, "tensor": far_t}
    dev_far_other = {"fsdp": 2 * k + oc, "tensor": far_t}
    net = Remote(ref.send_sems, ref.recv_sems)

    def aligned(start, size):
        return pl.ds(pl.multiple_of(start, math.gcd(size, LANES)), size)

    def piece_at(index):
        return pl.ds(pl.multiple_of(index * piece, piece), piece)

    def block(buf, index, lo=0, hi=None):
        return buf.at[piece_at(index), lo : buf.shape[1] if hi is None else hi]

    near, deep = zl * pair, (1 - zl) * pair

    def slot(side, place):
        return aligned(side + place * rows, rows)

    def spread_start(src, buf, lo, hi):
        base, _ = net.sems(2)
        source, target = src.at[:, lo:hi], block(buf, f, lo, hi)
        net.local(source, target, base + c, home)
        to = {"fsdp": 2 * k + zh, "tensor": t}
        net.send(source, target, to, base + c, when=away)
        to = {"fsdp": 2 * k + zh, "tensor": far_t}
        net.send(source, target, to, base + c)
        return base

    def gather_start(buf, lo, hi, base):
        sems = net.sems(3)
        a_own, b_own = block(buf, 2 * k, lo, hi), block(buf, 2 * k + 1, lo, hi)
        net.arrived(a_own, base)
        net.send(a_own, a_own, dev_x, sems[0])
        net.arrived(b_own, base + 1)
        net.send(b_own, b_own, dev_y, sems[1])
        net.send(a_own, a_own, dev_y, sems[2])
        net.send(b_own, b_own, dev_x, sems[2])
        return sems

    def gather_forward(buf, lo, hi, sems):
        a_x, b_y = block(buf, 2 * k_x, lo, hi), block(buf, 2 * k_y + 1, lo, hi)
        net.arrived(a_x, sems[0])
        net.send(a_x, a_x, dev_y, sems[2])
        net.arrived(b_y, sems[1])
        net.send(b_y, b_y, dev_x, sems[2])

    def gather_finish(buf, lo, hi, sems):
        net.arrived(buf.at[0 : 4 * piece, lo:hi], sems[2])

    f_x, f_y, f_d = 2 * k_x + c, 2 * k_y + c, 2 * k_d + c

    class WideGather:
        def __init__(self, src, buf, wait_at, lo, hi):
            self.buf, self.lo, self.size = buf, lo, hi - lo
            self.src, self.wait_at = src.at[lo:hi, :], wait_at.at[lo:hi, :]
            self.sems = net.sems(6)

        def at(self, index):
            start = pl.multiple_of(index * piece + self.lo, 16)
            return self.buf.at[pl.ds(start, self.size), :]

        def start(self, when):
            own, sems = self.at(f), self.sems
            stay_now, move_now = jnp.logical_and(stay, when), jnp.logical_and(move, when)
            net.local(self.src, own, sems[4], stay_now)
            net.send(self.src, own, dev_far, sems[0], when=stay_now)
            net.send(self.src, self.wait_at, dev_far, sems[0], when=move_now)

        def beside(self):
            net.send(self.src, self.at(f), dev_x, self.sems[1], when=move)

        def second(self):
            own, sems = self.at(f), self.sems

            @pl.when(stay)
            def _():
                net.arrived(self.wait_at, sems[0])

            @pl.when(move)
            def _():
                net.arrived(own, sems[0])

            net.send(self.wait_at, own, dev_x, sems[1], when=stay)

            @pl.when(stay)
            def _():
                net.arrived(own, sems[4])

            net.send(own, own, dev_y, sems[2])
            net.send(own, own, dev_c, sems[3])

        def third(self):
            got = self.at(f_x)
            net.arrived(got, self.sems[1])
            net.send(got, got, dev_y, self.sems[5])
            net.send(got, got, dev_c, self.sems[3])

        def fourth(self):
            for index, sem in ((f_y, 2), (f_d, 5)):
                got = self.at(index)
                net.arrived(got, self.sems[sem])
                net.send(got, got, dev_c, self.sems[3])

        def finish(self):
            net.arrived(self.buf.at[0 : 4 * self.size, :], self.sems[3])

    def share_start(buf):
        sems = net.sems(3)
        own = buf.at[slot(near, c)]
        net.send(own, own, dev_z, sems[0])
        net.send(own, own, dev_c, sems[1])
        return sems

    def share_near(buf, sems):
        net.arrived(buf.at[slot(near, oc)], sems[1])

    def share_forward(buf, sems):
        got = buf.at[slot(deep, c)]
        net.arrived(got, sems[0])
        net.send(got, got, dev_c, sems[2])

    def share_deep(buf, sems):
        net.arrived(buf.at[slot(deep, oc)], sems[2])

    def sum_deep(which, part):
        sems = net.sems(3)
        send = ref.core_send.at[which, 0]
        send[...] = part[slot(deep, oc), :].astype(bf16)
        net.send(send, ref.core_land.at[which, 0], dev_c, sems[0])
        return sems

    def sum_pass(which, part, sems):
        land, send = ref.core_land.at[which, 0], ref.deep_send.at[which]
        net.arrived(land, sems[0])
        send[...] = (part[slot(deep, c), :] + land[...].astype(f32)).astype(bf16)
        net.send(send, ref.deep_land.at[which], dev_z, sems[1])

    def sum_near(which, part, sems):
        send = ref.core_send.at[which, 1]
        send[...] = part[slot(near, oc), :].astype(bf16)
        net.send(send, ref.core_land.at[which, 1], dev_c, sems[2])

    def sum_finish(which, part, sems):
        beside, across = ref.core_land.at[which, 1], ref.deep_land.at[which]
        net.arrived(beside, sems[2])
        total = part[slot(near, c), :] + beside[...].astype(f32)
        net.arrived(across, sems[1])
        return total + across[...].astype(f32)

    def quarter(side, place, which):
        return aligned(side + place * rows + which * fourth, fourth)

    def wide_share_start(buf):
        sems = net.sems(4)
        first, second = buf.at[quarter(near, kx, 0)], buf.at[quarter(near, kx, 1)]
        net.send(first, first, dev_z, sems[0])
        net.send(second, second, dev_x, sems[1])
        net.send(second, second, dev_z, sems[3])
        net.send(first, first, dev_x, sems[2])
        return sems

    def wide_share_forward(buf, sems):
        from_z, from_x = buf.at[quarter(deep, kx, 0)], buf.at[quarter(near, ox, 1)]
        net.arrived(from_z, sems[0])
        net.send(from_z, from_z, dev_x, sems[3])
        net.arrived(from_x, sems[1])
        net.send(from_x, from_x, dev_z, sems[3])

    def wide_share_near(buf, sems):
        net.arrived(buf.at[quarter(near, ox, 0)], sems[2])

    def wide_share_deep(buf, sems):
        net.arrived(buf.at[0 : 3 * fourth, :], sems[3])

    def plain_share_z(buf):
        sems = net.sems(3)
        own = buf.at[slot(near, kx)]
        net.send(own, own, dev_z, sems[0])
        return sems

    def plain_share_x(buf, sems):
        own = buf.at[slot(near, kx)]
        net.send(own, own, dev_x, sems[1])

    def plain_share_forward(buf, sems):
        got = buf.at[slot(near, ox)]
        net.arrived(got, sems[1])
        net.send(got, got, dev_z, sems[2])

    def plain_share_finish(buf, sems):
        net.arrived(buf.at[slot(deep, kx)], sems[0])
        net.arrived(buf.at[slot(deep, ox)], sems[2])

    def wide_send(which, number):
        return ref.wide_send.at[which, number]

    def wide_land(which, number):
        return ref.wide_land.at[which, number]

    def wide_push(which, number, value, device, sem):
        wide_send(which, number)[...] = value.astype(bf16)
        net.send(wide_send(which, number), wide_land(which, number), device, sem)

    def wide_sum_deep(which, part):
        sems = net.sems(6)
        wide_push(which, 0, part[quarter(deep, ox, 0), :], dev_x, sems[0])
        wide_push(which, 1, part[quarter(deep, ox, 1), :], dev_z, sems[1])
        wide_push(which, 2, part[quarter(deep, kx, 1), :], dev_z, sems[2])
        return sems

    def wide_sum_near(which, part, sems):
        wide_push(which, 3, part[quarter(near, ox, 0), :], dev_x, sems[3])

    def wide_sum_pass(which, part, sems):
        net.arrived(wide_land(which, 0), sems[0])
        total = part[quarter(deep, kx, 0), :] + wide_land(which, 0)[...].astype(f32)
        wide_push(which, 4, total, dev_z, sems[4])
        net.arrived(wide_land(which, 1), sems[1])
        total = part[quarter(near, ox, 1), :] + wide_land(which, 1)[...].astype(f32)
        wide_push(which, 5, total, dev_x, sems[5])

    def wide_sum_finish(which, part, sems):
        halves = []
        for half_at, (by_z, by_x) in enumerate(((4, 3), (2, 5))):
            net.arrived(wide_land(which, by_z), sems[by_z])
            net.arrived(wide_land(which, by_x), sems[by_x])
            halves.append(
                part[quarter(near, kx, half_at), :]
                + wide_land(which, by_z)[...].astype(f32)
                + wide_land(which, by_x)[...].astype(f32)
            )
        return jnp.concatenate(halves, axis=0)

    def add_into(grad, index, lo, hi, land):
        at = piece_at(index)
        total = grad[at, lo:hi].astype(f32) + land[...].astype(f32)
        grad[at, lo:hi] = total.astype(bf16)

    def reduce_route(core, by_y):
        if core == 0 or by_y:
            return dev_y, 2 * k_y + core, 2 * k_x + core, dev_x
        return dev_x, 2 * k_x + core, 2 * k_y + core, dev_y

    def reduce_first(grad, land, lo, hi, sems, by_y=False, when=None):
        for distant in (True, False):
            for core in range(2):
                device, index, _, _ = reduce_route(core, by_y)
                index, number = (2 * k_d + core, 1 + 2 * core) if distant else (index, 2 * core)
                source = block(grad, index, lo, hi)
                net.send(source, land.at[number], device, sems[number], when=when)

    def reduce_second(grad, land, lo, hi, sems, by_y=False, when=None):
        def collect(index, number):
            def action():
                net.arrived(land.at[number], sems[number])
                add_into(grad, index, lo, hi, land.at[number])

            guarded(when, action)

        for core in range(2):
            _, _, index, device = reduce_route(core, by_y)
            collect(index, 1 + 2 * core)
            source = block(grad, index, lo, hi)
            net.send(source, land.at[4 + core], device, sems[4 + core], when=when)
        for core in range(2):
            collect(2 * k + core, 2 * core)

    def reduce_third(grad, land, lo, hi, sems, when=None):
        def here(condition):
            return condition if when is None else jnp.logical_and(when, condition)

        for core in range(2):

            def collect(core=core):
                net.arrived(land.at[4 + core], sems[4 + core])
                add_into(grad, 2 * k + core, lo, hi, land.at[4 + core])

            guarded(when, collect)
            source = block(grad, 2 * k + core, lo, hi)
            mine, other = jnp.logical_and(home, c == core), jnp.logical_and(home, c != core)
            net.local(source, land.at[6], sems[6], here(mine))
            to = {"fsdp": 2 * k + core, "tensor": t}
            net.send(source, land.at[6], to, sems[6], when=here(other))
            to = {"fsdp": 2 * k + core, "tensor": far_t}
            net.send(source, land.at[7], to, sems[7], when=here(away))

    def reduce_finish(land, sems):
        net.arrived(land.at[6], sems[6])
        net.arrived(land.at[7], sems[7])
        return land[6].astype(f32) + land[7].astype(f32)

    def wide_reduce_first(grad, land):
        sems = net.sems(6)
        for number, index in enumerate((f_d, f_y, f, f_x)):
            sem = sems[0] if number < 2 else sems[1]
            net.send(block(grad, index + oc - c), land.at[number], dev_c, sem)
        return sems

    def wide_reduce_second(grad, land, sems):
        net.arrived(land.at[0:2], sems[0])
        for number, index in enumerate((f_d, f_y)):
            add_into(grad, index, 0, grad.shape[1], land.at[number])
            net.send(block(grad, index), land.at[4 + number], dev_y, sems[4 + number])
        net.arrived(land.at[2:4], sems[1])
        for number, index in ((2, f), (3, f_x)):
            add_into(grad, index, 0, grad.shape[1], land.at[number])

    def wide_reduce_third(grad, land, sems):
        net.arrived(land.at[4], sems[4])
        add_into(grad, f_x, 0, grad.shape[1], land.at[4])
        net.send(block(grad, f_x), land.at[6], dev_x, sems[2])
        net.arrived(land.at[5], sems[5])
        add_into(grad, f, 0, grad.shape[1], land.at[5])

    def wide_reduce_cross(grad, land, sems, when):
        now = jnp.logical_and(move, when)
        net.send(block(grad, f), land.at[7], dev_far, sems[3], when=now)

    def wide_reduce_fourth(grad, land, sems, when):
        guarded(when, lambda: net.arrived(land.at[6], sems[2]))
        now = jnp.logical_and(stay, when)
        net.send(land.at[6], land.at[7], dev_far, sems[3], when=now)

    def wide_reduce_finish(grad, land, sems):
        kept = jnp.where(stay, grad[piece_at(f), :].astype(f32), land[6].astype(f32))
        net.arrived(land.at[7], sems[3])
        return kept + land[7].astype(f32)

    vec_own, by_plane, by_chip = ref.vec_own, ref.by_plane, ref.by_chip
    plane_peers = [lax.rem(t + step, 4) for step in range(1, 4)]
    chip_peers = [lax.rem(k + step, 4) for step in range(1, 4)]

    def vector_planes():
        by_plane[t] = vec_own[...]
        sem = net.sem()
        for plane in plane_peers:
            net.send(vec_own, by_plane.at[t], {"fsdp": f, "tensor": plane}, sem)
        return sem

    def vector_chips(sem):
        net.arrived(by_plane.at[0:3], sem)
        both = ref.vec_chip
        total = by_plane[0] + by_plane[1] + by_plane[2] + by_plane[3]
        shard = by_plane[zl] + by_plane[2 + zl]
        both[0:6, :] = total[0:6, :]
        both[6:8, :] = shard[6:8, :]
        by_chip[k] = both[...]
        sem = net.sem()
        for chip in chip_peers:
            net.send(both, by_chip.at[k], {"fsdp": 2 * chip + c, "tensor": t}, sem)
        return sem

    def vector_core(sem):
        net.arrived(by_chip.at[0:3], sem)
        held = ref.vec_core
        total = by_chip[0] + by_chip[1] + by_chip[2] + by_chip[3]
        units_total = by_chip[zh] + by_chip[2 + zh]
        held[0:6, :] = total[0:6, :]
        held[6:7, :] = units_total[6:7, :]
        held[7:8, :] = total[7:8, :]
        sem = net.sem()
        net.send(held, ref.vec_core_land, dev_c, sem)
        return sem

    def vector_finish(sem):
        held, land, done = ref.vec_core, ref.vec_core_land, ref.vec_done
        net.arrived(land, sem)
        done[0:7, :] = held[0:7, :] + land[0:7, :]
        done[7:8, :] = jnp.where(home, held[7:8, :], land[7:8, :])

    barrier = pltpu.get_barrier_semaphore()
    peers = (dev_x, dev_y, dev_c, dev_z, dev_far, dev_far_other)
    for peer in peers:
        pl.semaphore_signal(barrier, inc=1, device_id=peer, device_id_type=MESH_IDS)

    coming = {}
    for number, name in enumerate(inputs):
        copy = pltpu.make_async_copy(
            getattr(hbm, name), getattr(held, name), ref.load_sems.at[number]
        )
        copy.start()
        coming[name] = copy
    coming = SimpleNamespace(**coming)
    stores = []

    def store(source, target):
        sem = ref.load_sems.at[len(inputs) + len(stores)]
        copy = pltpu.make_async_copy(source, target, sem)
        copy.start()
        stores.append(copy)

    attn_piece = ref.attn_piece
    if all_lanes > 4 * width:
        attn_piece[:, 4 * width :] = jnp.zeros((piece, all_lanes - 4 * width), bf16)
    for number, (copy, raw) in enumerate(
        (
            (coming.query_w, held.query_w),
            (coming.key_w, held.key_w),
            (coming.value_w, held.value_w),
            (coming.out_w, held.out_w),
        )
    ):
        copy.wait()
        attn_piece[:, number * width : (number + 1) * width] = raw[...]
    vectors[...] = jnp.zeros_like(vectors)
    for number, (copy, raw) in enumerate(
        (
            (coming.first_gain, held.first_gain),
            (coming.first_shift, held.first_shift),
            (coming.out_bias, held.out_bias),
            (coming.second_gain, held.second_gain),
            (coming.second_shift, held.second_shift),
            (coming.down_bias, held.down_bias),
        )
    ):
        copy.wait()
        vectors[number : number + 1, :] = raw[...].reshape(1, D)
    coming.up_bias.wait()
    vectors[6:7, :units] = held.up_bias[...].reshape(1, units)
    coming.query_bias.wait()
    vectors[7:8, :width] = held.query_bias[...].reshape(1, width)
    coming.value_bias.wait()
    vectors[7:8, 2 * width : 3 * width] = held.value_bias[...].reshape(1, width)
    first_gain, first_shift = vectors[0:1, :], vectors[1:2, :]
    out_bias, second_gain = vectors[2:3, :], vectors[3:4, :]
    second_shift, down_bias = vectors[4:5, :], vectors[5:6, :]
    tokens_ref, cotangent_ref = held.tokens, held.cotangent
    coming.tokens.wait()
    coming.cotangent.wait()
    token_rows = tokens_ref[...].astype(f32)
    normed, hat, inv_scale = norm_rows(token_rows, first_gain, first_shift)
    first_all[slot(near, c), :] = normed.astype(bf16)
    ref.first_hat[...] = hat
    ref.row_scale[0] = jnp.broadcast_to(inv_scale, (rows, LANES))

    pl.semaphore_wait(barrier, len(peers))

    first_sems = share_start(first_all)
    lane_cut = round_up(qkv_lanes // 2, LANES)
    q_parts = [(attn_w, 0, lane_cut), (attn_w, lane_cut, qkv_lanes)]
    o_part = (attn_w, qkv_lanes, all_lanes)
    q_base = [spread_start(attn_piece, *part) for part in q_parts]
    o_base = spread_start(attn_piece, *o_part)
    vec_sem = net.sem()
    net.send(vectors, ref.far_vectors, dev_far, vec_sem)
    up_parts = [
        WideGather(ref.up_piece, up_w, ref.up_wait, lo, hi)
        for lo, hi in row_cuts(piece, 2)
    ]
    down_parts = [
        WideGather(ref.down_piece, down_w, ref.down_wait, lo, hi)
        for lo, hi in row_cuts(piece, 3)
    ]

    coming.up_w.wait()
    coming.down_w.wait()
    ref.up_piece[:, main:] = jnp.zeros((piece, LANES), bf16)
    ref.up_piece[:, :units] = held.up_w[...]
    ref.up_piece[:, units : units + rest] = held.down_w[:, main:]
    ref.down_piece[...] = held.down_w[:, :main]
    dy_all[slot(near, kx), :] = cotangent_ref[...]
    vec_own[5:6, :] = jnp.sum(cotangent_ref[...].astype(f32), axis=0, keepdims=True)
    head_rows[...] = jnp.zeros_like(head_rows)
    head_grads[...] = jnp.zeros_like(head_grads)
    mixed_all[...] = jnp.zeros_like(mixed_all)
    qkv_grads[...] = jnp.zeros_like(qkv_grads)

    def shard_vector(row, own):
        return jnp.where(own, vectors[row : row + 1, :], ref.far_vectors[row : row + 1, :])

    scale = HD ** (-0.5)

    def image_head(step):
        head, image = lax.rem(step, heads), lax.div(step, heads)
        return head, aligned(image * pair, pair)

    def attend(step, carry):
        head, span = image_head(step)
        queries, keys_part = head_rows[head, span, :], head_rows[heads + head, span, :]
        values = head_rows[2 * heads + head, span, :]
        scores = dot_right_t(queries, keys_part) * scale
        expo = jnp.exp(scores - jnp.max(scores, axis=1, keepdims=True))
        probs = expo / jnp.sum(expo, axis=1, keepdims=True)
        ref.probs_all[step] = probs
        mixed = dot_plain(probs.astype(bf16), values)
        ref.mixed_heads[head, span, :] = mixed.astype(bf16)
        return carry

    def pack(target, source, count, base):
        for side_at in range(2):
            for image in range(2):
                at = slice(side_at * pair + image * rows, side_at * pair + (image + 1) * rows)
                take = slice(image * pair + side_at * rows, image * pair + (side_at + 1) * rows)
                for head in range(count):
                    lo = base + head * HD
                    target[at, lo : lo + HD] = source[head, take, :HD]

    def half(side):
        return aligned(side, pair)

    chunk = 32

    in_rest = lax.broadcasted_iota(jnp.int32, (chunk, LANES), 1) < rest

    hidden_rest = ref.hidden_rest

    def raise_half(side):
        part_b[half(side), :] = dot_plain(second_all[half(side), :], up_w[...])

        def gelu_rows(step, carry):
            at = aligned(side + step * chunk, chunk)
            value, slope = gelu_pair(part_b[at, :] + up_bias)
            last = jnp.where(in_rest, value[:, main:], 0.0)
            hidden_all[at, :main] = value[:, :main].astype(bf16)
            hidden_all[at, main:] = last.astype(bf16)
            hidden_rest[at, :] = pltpu.roll(last, rest, 1).astype(bf16)
            slope_all[at, :] = slope
            return carry

        lax.fori_loop(0, pair // chunk, gelu_rows, 0)

    tile = 3 * LANES

    def outer_product(grad, left, right, lo, hi):
        def rows_of(step, carry):
            at = aligned(step * tile, tile)
            grad[at, lo:hi] = dot_left_t(left[:, at], right).astype(bf16)
            return carry

        lax.fori_loop(0, D // tile, rows_of, 0, unroll=True)

    def lower_half(side):
        part_b[half(side), :main] = dot_plain(dy_all[half(side), :], down_w[...])
        part_b[half(side), main:] = dot_plain(dy_all[half(side), :], up_w[:, main:])

        def slope_rows(step, totals):
            at = aligned(side + step * chunk, chunk)
            last = pltpu.roll(part_b[at, main:], LANES - rest, 1)
            last = jnp.where(in_rest, last * slope_all[at, main:], 0.0).astype(bf16)
            low = (part_b[at, :main] * slope_all[at, :main]).astype(bf16)
            upper_all[at, :main] = low
            upper_all[at, main:] = last
            return (
                totals[0] + jnp.sum(low.astype(f32), axis=0, keepdims=True),
                totals[1] + jnp.sum(last.astype(f32), axis=0, keepdims=True),
            )

        start = jnp.zeros((1, main), f32), jnp.zeros((1, LANES), f32)
        return lax.fori_loop(0, pair // chunk, slope_rows, start)

    def up_rows(step, carry):
        at = aligned(step * tile, tile)
        by_row = second_all[:, at]
        up_g[at, :main] = dot_left_t(by_row, upper_all[:, :main]).astype(bf16)
        last = dot_left_t(by_row, upper_all[:, main:])
        last = last + dot_left_t(dy_all[:, at], hidden_rest[...])
        up_g[at, main:] = last.astype(bf16)
        return carry

    def lower_product(side):
        total = dot_right_t(hidden_all[half(side), :main], down_w[...])
        return total + dot_right_t(hidden_rest[half(side), :], up_w[:, main:])

    def head_half(side_at):
        side_rows = slice(side_at * pair, (side_at + 1) * pair)
        done = dot_plain(mid_all[side_rows, :], attn_w[:, win:]).astype(bf16)
        for image in range(2):
            to = slice(image * pair + side_at * rows, image * pair + (side_at + 1) * rows)
            for head in range(heads):
                lo = win_shift + head * HD
                head_grads[head, to, :HD] = done[image * rows : (image + 1) * rows, lo : lo + HD]

    cut = round_up(2 * width, LANES)

    def value_back(step, carry):
        head, span = image_head(step)
        low = ref.probs_all[step].astype(bf16)
        value_grad = dot_left_t(low, head_grads[head, span, :])
        ref.mixed_heads[head, span, :] = value_grad.astype(bf16)
        return carry

    def value_out_rows(step, carry):
        at = aligned(step * tile, tile)
        by_value = dot_left_t(first_all[:, at], qkv_grads[:, cut:qkv_lanes])
        by_out = dot_left_t(mid_all[:, at], mixed_all[...])
        both = by_value[:, win - cut :] + by_out[:, :skip]
        attn_g[at, cut:win] = by_value[:, : win - cut].astype(bf16)
        attn_g[at, win:qkv_lanes] = both.astype(bf16)
        attn_g[at, qkv_lanes:] = by_out[:, skip:].astype(bf16)
        return carry

    def attend_back(step, carry):
        head, span = image_head(step)
        queries, keys_part = head_rows[head, span, :], head_rows[heads + head, span, :]
        values, grads = head_rows[2 * heads + head, span, :], head_grads[head, span, :]
        probs = ref.probs_all[step]
        prob_grad = dot_right_t(grads, values)
        row_dot = jnp.sum(probs * prob_grad, axis=1, keepdims=True)
        score_grad = (probs * (prob_grad - row_dot)).astype(bf16)
        query_grad = dot_plain(score_grad, keys_part) * scale
        key_grad = dot_left_t(score_grad, queries) * scale
        head_rows[head, span, :] = query_grad.astype(bf16)
        head_rows[heads + head, span, :] = key_grad.astype(bf16)
        return carry

    for part in up_parts:
        part.start(inner)
    dy_sems = plain_share_z(dy_all)
    q_sems = [gather_start(*part, base) for part, base in zip(q_parts, q_base)]
    for part in up_parts:
        part.start(jnp.logical_and(outer, away))
    for part, sems in zip(q_parts, q_sems):
        gather_forward(*part, sems)
    for part in up_parts:
        part.start(jnp.logical_and(outer, home))
    o_sems = gather_start(*o_part, o_base)
    share_forward(first_all, first_sems)
    net.arrived(ref.far_vectors, vec_sem)
    share_near(first_all, first_sems)
    share_deep(first_all, first_sems)
    qkv_bias = shard_vector(7, home)[:, :qkv_lanes]
    up_bias = shard_vector(6, stay)
    for part, sems in zip(q_parts, q_sems):
        gather_finish(*part, sems)
    for part in down_parts:
        part.start(outer)
    gather_forward(*o_part, o_sems)
    plain_share_x(dy_all, dy_sems)
    for part in up_parts:
        part.beside()
    for part in down_parts:
        part.beside()
    for side_at in range(2):
        side_rows = slice(side_at * pair, (side_at + 1) * pair)
        done = dot_plain(first_all[side_rows, :], attn_w[:, :qkv_lanes])
        done = (done + qkv_bias).astype(bf16)
        for image in range(2):
            to = slice(image * pair + side_at * rows, image * pair + (side_at + 1) * rows)
            for head in range(3 * heads):
                head_rows[head, to, :HD] = done[
                    image * rows : (image + 1) * rows, head * HD : (head + 1) * HD
                ]
    lax.fori_loop(0, 2 * heads, attend, 0, unroll=2)
    pack(mixed_all, ref.mixed_heads, heads, win_shift)
    gather_finish(*o_part, o_sems)
    part_a[half(deep), :] = dot_right_t(mixed_all[half(deep), :], attn_w[:, win:])
    out_sems = sum_deep(0, part_a)
    part_a[half(near), :] = dot_right_t(mixed_all[half(near), :], attn_w[:, win:])
    sum_pass(0, part_a, out_sems)
    sum_near(0, part_a, out_sems)
    up_parts[0].second()
    up_parts[1].second()
    up_parts[0].third()
    attn_rows = sum_finish(0, part_a, out_sems)
    middle = tokens_ref[...].astype(f32) + attn_rows + out_bias
    ref.mid_rows[...] = middle
    normed, hat, inv_scale = norm_rows(middle, second_gain, second_shift)
    second_all[slot(near, kx), :] = normed.astype(bf16)
    ref.second_hat[...] = hat
    ref.row_scale[1] = jnp.broadcast_to(inv_scale, (rows, LANES))
    second_sems = wide_share_start(second_all)
    for part in down_parts:
        part.start(inner)
    up_parts[1].third()
    wide_share_forward(second_all, second_sems)
    down_parts[0].second()
    down_parts[1].second()
    down_parts[2].second()
    plain_share_forward(dy_all, dy_sems)
    up_parts[0].fourth()
    up_parts[1].fourth()
    down_parts[0].third()
    for part in up_parts:
        part.finish()
    wide_share_near(second_all, second_sems)
    raise_half(near)
    down_parts[1].third()
    wide_share_deep(second_all, second_sems)
    raise_half(deep)
    down_parts[2].third()
    down_parts[0].fourth()
    plain_share_finish(dy_all, dy_sems)
    outer_product(down_g, dy_all, hidden_all[:, :main], 0, main)
    down_reduce = wide_reduce_first(down_g, ref.land_d)
    down_parts[1].fourth()
    wide_reduce_second(down_g, ref.land_d, down_reduce)
    down_parts[2].fourth()
    for part in down_parts:
        part.finish()
    up_bias_sum = lower_half(deep)
    part_a[half(deep), :] = dot_right_t(upper_all[half(deep), :], up_w[...])
    second_sum_sems = wide_sum_deep(0, part_a)
    more_sum = lower_half(near)
    vec_own[6:7, :main] = up_bias_sum[0] + more_sum[0]
    vec_own[6:7, main:] = up_bias_sum[1] + more_sum[1]
    part_a[half(near), :] = dot_right_t(upper_all[half(near), :], up_w[...])
    wide_sum_near(0, part_a, second_sum_sems)
    lax.fori_loop(0, D // tile, up_rows, 0, unroll=True)
    up_reduce = wide_reduce_first(up_g, ref.land_u)
    wide_sum_pass(0, part_a, second_sum_sems)
    wide_reduce_second(up_g, ref.land_u, up_reduce)
    wide_reduce_third(down_g, ref.land_d, down_reduce)
    second_grad = wide_sum_finish(0, part_a, second_sum_sems)
    back, gain_sum, shift_sum = norm_back(
        second_grad, ref.second_hat[...], ref.row_scale[1][:, :1], second_gain
    )
    vec_own[3:4, :] = gain_sum[None, :]
    vec_own[4:5, :] = shift_sum[None, :]
    total = cotangent_ref[...].astype(f32) + back
    ref.mid_grad[...] = total
    low = total.astype(bf16)
    mid_all[slot(near, c), :] = low
    vec_own[2:3, :] = jnp.sum(low.astype(f32), axis=0, keepdims=True)
    mid_sems = share_start(mid_all)
    part_b[half(deep), :] = lower_product(deep)
    mlp_sems = wide_sum_deep(1, part_b)
    part_b[half(near), :] = lower_product(near)
    wide_sum_near(1, part_b, mlp_sems)
    share_forward(mid_all, mid_sems)
    share_near(mid_all, mid_sems)
    wide_reduce_cross(down_g, ref.land_d, down_reduce, when=outer)
    wide_reduce_fourth(down_g, ref.land_d, down_reduce, when=outer)
    share_deep(mid_all, mid_sems)
    head_half(0)
    head_half(1)
    wide_reduce_third(up_g, ref.land_u, up_reduce)
    wide_reduce_cross(down_g, ref.land_d, down_reduce, when=inner)
    wide_reduce_fourth(down_g, ref.land_d, down_reduce, when=inner)
    lax.fori_loop(0, 2 * heads, value_back, 0, unroll=2)
    pack(qkv_grads, ref.mixed_heads, heads, 2 * width)
    lax.fori_loop(0, D // tile, value_out_rows, 0)
    vo_args = attn_g, ref.land_vo, cut, all_lanes, net.sems(8)
    reduce_first(*vo_args)
    wide_sum_pass(1, part_b, mlp_sems)
    lax.fori_loop(0, 2 * heads, attend_back, 0, unroll=2)
    wide_reduce_fourth(up_g, ref.land_u, up_reduce, when=outer)
    pack(qkv_grads, head_rows, 2 * heads, 0)
    wide_reduce_cross(up_g, ref.land_u, up_reduce, when=outer)
    part_a[half(deep), :] = dot_right_t(
        qkv_grads[half(deep), :qkv_lanes], attn_w[:, :qkv_lanes]
    )
    first_sum_sems = sum_deep(1, part_a)
    part_a[half(near), :] = dot_right_t(
        qkv_grads[half(near), :qkv_lanes], attn_w[:, :qkv_lanes]
    )
    sum_pass(1, part_a, first_sum_sems)
    sum_near(1, part_a, first_sum_sems)
    vec_own[7:8, :] = jnp.sum(qkv_grads[...].astype(f32), axis=0, keepdims=True)
    outer_product(attn_g, first_all, qkv_grads[:, :cut], 0, cut)
    qk_args = attn_g, ref.land_qk, 0, cut, net.sems(8)
    reduce_first(*qk_args, when=away)
    wide_reduce_cross(up_g, ref.land_u, up_reduce, when=inner)
    wide_reduce_fourth(up_g, ref.land_u, up_reduce, when=inner)
    reduce_second(*vo_args)
    reduce_second(*qk_args, when=away)
    first_grad = sum_finish(1, part_a, first_sum_sems)
    back, gain_sum, shift_sum = norm_back(
        first_grad, ref.first_hat[...], ref.row_scale[0][:, :1], first_gain
    )
    vec_own[0:1, :] = gain_sum[None, :]
    vec_own[1:2, :] = shift_sum[None, :]
    vec_sem = vector_planes()
    ref.mid_grad[...] = ref.mid_grad[...] + back
    store(ref.mid_grad, out.input_grad)
    reduce_first(*qk_args, when=home)
    reduce_third(*vo_args)
    reduce_third(*qk_args, when=away)
    vec_sem = vector_chips(vec_sem)
    vec_sem = vector_core(vec_sem)
    reduce_second(*qk_args, when=home)
    vector_finish(vec_sem)
    store(ref.vec_done, out.vector_grad)
    reduce_third(*qk_args, when=home)
    ref.down_buf[...] = wide_reduce_finish(down_g, ref.land_d, down_reduce)
    store(ref.down_buf, out.down_grad)
    mlp_rows = wide_sum_finish(1, part_b, mlp_sems)
    ref.layer_buf[...] = (ref.mid_rows[...] + mlp_rows + down_bias).astype(bf16)
    store(ref.layer_buf, out.layer_out)
    ref.up_buf[...] = wide_reduce_finish(up_g, ref.land_u, up_reduce)
    store(ref.up_buf, out.up_grad)
    ref.attn_buf[:, cut:] = reduce_finish(ref.land_vo, vo_args[4])
    store(ref.attn_buf.at[:, cut:], out.attn_grad.at[:, cut:])
    ref.attn_buf[:, :cut] = reduce_finish(ref.land_qk, qk_args[4])
    store(ref.attn_buf.at[:, :cut], out.attn_grad.at[:, :cut])
    net.drain()
    assert net.used <= ref.recv_sems.shape[0]
    for copy in stores:
        copy.wait()


def format_kernel(shapes, *refs):
    width, units = shapes
    inputs, refs = refs[:6], refs[6:]
    outs, refs = refs[:17], refs[17:]
    held, refs = refs[:6], refs[6:]
    shaped, sems = refs[:-1], refs[-1]
    copies = [
        pltpu.make_async_copy(source, target, sems.at[number])
        for number, (source, target) in enumerate(zip(inputs, held, strict=True))
    ]
    for copy in copies:
        copy.start()
    going = []

    def put(source, number):
        copy = pltpu.make_async_copy(source, outs[number], sems.at[6 + number])
        copy.start()
        going.append(copy)

    def put_shaped(number, value):
        shaped[number - 2][...] = value
        put(shaped[number - 2], number)

    copies[0].wait()
    put(held[0], 0)
    copies[1].wait()
    put(held[1], 1)
    copies[2].wait()
    for number, place in ((4, 0), (5, 1), (6, 2), (9, 3)):
        put_shaped(number, held[2][:, place * width : (place + 1) * width])
    copies[3].wait()
    put_shaped(13, held[3][:, :units])
    copies[4].wait()
    main = held[4].shape[1]
    shaped[13][:, :main] = held[4][...]
    shaped[13][:, main:] = held[3][:, units : 2 * units - main]
    put(shaped[13], 15)
    copies[5].wait()
    for number, row, lo, size in (
        (2, 0, 0, D),
        (3, 1, 0, D),
        (10, 2, 0, D),
        (11, 3, 0, D),
        (12, 4, 0, D),
        (16, 5, 0, D),
        (14, 6, 0, units),
        (7, 7, 0, width),
        (8, 7, 2 * width, width),
    ):
        put_shaped(number, held[5][row, lo : lo + size])
    for copy in going:
        copy.wait()


def fused_step(
    tokens,
    cotangent,
    first_gain,
    first_shift,
    query_weight,
    key_weight,
    value_weight,
    query_bias,
    value_bias,
    out_weight,
    out_bias,
    second_gain,
    second_shift,
    up_weight,
    up_bias,
    down_weight,
    down_bias,
):
    bf16, f32 = jnp.bfloat16, jnp.float32
    rows, piece, width, units = (
        tokens.shape[0],
        query_weight.shape[0],
        query_weight.shape[1],
        up_weight.shape[1],
    )
    heads = width // HD
    group = 4 * rows
    qkv_lanes = round_up(3 * width, LANES)
    attn_lanes = round_up(4 * width, LANES)
    ff_lanes = round_up(units, LANES)
    main = units // LANES * LANES
    assert 2 * (units - main) <= LANES < ff_lanes - main + 1
    win = 3 * width // LANES * LANES
    given = dict(
        query_w=query_weight,
        key_w=key_weight,
        value_w=value_weight,
        out_w=out_weight.T,
        first_gain=first_gain,
        first_shift=first_shift,
        out_bias=out_bias,
        second_gain=second_gain,
        second_shift=second_shift,
        down_bias=down_bias,
        up_bias=up_bias,
        query_bias=query_bias,
        value_bias=value_bias,
        tokens=tokens,
        cotangent=cotangent,
        up_w=up_weight,
        down_w=down_weight.T,
    )
    place = pl.BlockSpec(memory_space=pl.ANY)
    cut = round_up(2 * width, LANES)
    raw_outs = dict(
        layer_out=jax.ShapeDtypeStruct((rows, D), bf16),
        input_grad=jax.ShapeDtypeStruct((rows, D), f32),
        attn_grad=jax.ShapeDtypeStruct((piece, attn_lanes), f32),
        up_grad=jax.ShapeDtypeStruct((piece, ff_lanes), f32),
        down_grad=jax.ShapeDtypeStruct((piece, main), f32),
        vector_grad=jax.ShapeDtypeStruct((8, D), f32),
    )
    scratch = dict(
        attn_piece=pltpu.VMEM((piece, attn_lanes), bf16),
        up_piece=pltpu.VMEM((piece, ff_lanes), bf16),
        down_piece=pltpu.VMEM((piece, main), bf16),
        up_wait=pltpu.VMEM((piece, ff_lanes), bf16),
        down_wait=pltpu.VMEM((piece, main), bf16),
        attn_w=pltpu.VMEM((D, attn_lanes), bf16),
        up_w=pltpu.VMEM((D, ff_lanes), bf16),
        down_w=pltpu.VMEM((D, main), bf16),
        attn_g=pltpu.VMEM((D, attn_lanes), bf16),
        up_g=pltpu.VMEM((D, ff_lanes), bf16),
        down_g=pltpu.VMEM((D, main), bf16),
        land_vo=pltpu.VMEM((8, piece, attn_lanes - cut), bf16),
        land_qk=pltpu.VMEM((8, piece, cut), bf16),
        land_u=pltpu.VMEM((8, piece, ff_lanes), bf16),
        land_d=pltpu.VMEM((8, piece, main), bf16),
        first_all=pltpu.VMEM((group, D), bf16),
        second_all=pltpu.VMEM((group, D), bf16),
        dy_all=pltpu.VMEM((group, D), bf16),
        mid_all=pltpu.VMEM((group, D), bf16),
        head_rows=pltpu.VMEM((3 * heads, group, LANES), bf16),
        head_grads=pltpu.VMEM((heads, group, LANES), bf16),
        probs_all=pltpu.VMEM((2 * heads, 2 * rows, 2 * rows), f32),
        mixed_heads=pltpu.VMEM((heads, group, LANES), bf16),
        mixed_all=pltpu.VMEM((group, attn_lanes - win), bf16),
        hidden_all=pltpu.VMEM((group, ff_lanes), bf16),
        hidden_rest=pltpu.VMEM((group, LANES), bf16),
        slope_all=pltpu.VMEM((group, ff_lanes), f32),
        upper_all=pltpu.VMEM((group, ff_lanes), bf16),
        qkv_grads=pltpu.VMEM((group, attn_lanes), bf16),
        part_a=pltpu.VMEM((group, D), f32),
        part_b=pltpu.VMEM((group, D), f32),
        core_send=pltpu.VMEM((2, 2, rows, D), bf16),
        core_land=pltpu.VMEM((2, 2, rows, D), bf16),
        deep_send=pltpu.VMEM((2, rows, D), bf16),
        deep_land=pltpu.VMEM((2, rows, D), bf16),
        wide_send=pltpu.VMEM((2, 6, rows // 2, D), bf16),
        wide_land=pltpu.VMEM((2, 6, rows // 2, D), bf16),
        first_hat=pltpu.VMEM((rows, D), f32),
        second_hat=pltpu.VMEM((rows, D), f32),
        mid_rows=pltpu.VMEM((rows, D), f32),
        mid_grad=pltpu.VMEM((rows, D), f32),
        row_scale=pltpu.VMEM((2, rows, LANES), f32),
        vectors=pltpu.VMEM((8, D), f32),
        far_vectors=pltpu.VMEM((8, D), f32),
        vec_own=pltpu.VMEM((8, D), f32),
        by_plane=pltpu.VMEM((4, 8, D), f32),
        vec_chip=pltpu.VMEM((8, D), f32),
        by_chip=pltpu.VMEM((4, 8, D), f32),
        vec_core=pltpu.VMEM((8, D), f32),
        vec_core_land=pltpu.VMEM((8, D), f32),
        vec_done=pltpu.VMEM((8, D), f32),
        layer_buf=pltpu.VMEM((rows, D), bf16),
        attn_buf=pltpu.VMEM((piece, attn_lanes), f32),
        up_buf=pltpu.VMEM((piece, ff_lanes), f32),
        down_buf=pltpu.VMEM((piece, main), f32),
        load_sems=pltpu.SemaphoreType.DMA((len(given) + len(raw_outs) + 1,)),
        send_sems=pltpu.SemaphoreType.DMA((64,)),
        recv_sems=pltpu.SemaphoreType.DMA((112,)),
    )
    shapes = (rows, heads, width, units, qkv_lanes, piece)
    names = tuple(given), tuple(raw_outs), tuple(scratch)

    def body(*refs):
        layer_kernel(shapes, names, *refs)

    raw = pl.pallas_call(
        body,
        out_shape=tuple(raw_outs.values()),
        in_specs=[place] * len(given),
        out_specs=(place,) * len(raw_outs),
        scratch_shapes=[
            *(pltpu.VMEM(array.shape, array.dtype) for array in given.values()),
            *scratch.values(),
        ],
        compiler_params=pltpu.CompilerParams(
            collective_id=0, has_side_effects=True, vmem_limit_bytes=67043328
        ),
        name="layer",
    )(*given.values())
    raw_outs = tuple(raw_outs.values())

    vector, narrow = jax.ShapeDtypeStruct((D,), f32), jax.ShapeDtypeStruct((width,), f32)
    attn_out = jax.ShapeDtypeStruct((piece, width), f32)
    ff_out = jax.ShapeDtypeStruct((piece, units), f32)
    outs = (
        *raw_outs[:2],
        vector,
        vector,
        attn_out,
        attn_out,
        attn_out,
        narrow,
        narrow,
        attn_out,
        vector,
        vector,
        vector,
        ff_out,
        jax.ShapeDtypeStruct((units,), f32),
        ff_out,
        vector,
    )

    def format_body(*refs):
        format_kernel((width, units), *refs)

    done = pl.pallas_call(
        format_body,
        out_shape=outs,
        in_specs=[place] * 6,
        out_specs=(place,) * 17,
        scratch_shapes=[
            *(pltpu.VMEM(item.shape, item.dtype) for item in raw_outs),
            *(pltpu.VMEM(item.shape, item.dtype) for item in outs[2:]),
            pltpu.SemaphoreType.DMA((6 + 17,)),
        ],
        compiler_params=pltpu.CompilerParams(vmem_limit_bytes=67043328),
        name="outputs",
    )(*raw)
    done = list(done)
    done[9], done[15] = done[9].T, done[15].T
    return tuple(done)


def pick_step(mesh):
    if mesh.shape["fsdp"] == 8 and mesh.shape["tensor"] == 4:
        return fused_step
    return on_device


def solution(mesh):
    return jax.shard_map(
        pick_step(mesh),
        mesh=mesh,
        in_specs=(
            P(("fsdp", "tensor"), None),
            P(("fsdp", "tensor"), None),
            P(),
            P(),
            P("fsdp", "tensor"),
            P("fsdp", "tensor"),
            P("fsdp", "tensor"),
            P("tensor"),
            P("tensor"),
            P("tensor", "fsdp"),
            P(),
            P(),
            P(),
            P("fsdp", "tensor"),
            P("tensor"),
            P("tensor", "fsdp"),
            P(),
        ),
        out_specs=(
            P(("fsdp", "tensor"), None),
            P(("fsdp", "tensor"), None),
            P(),
            P(),
            P("fsdp", "tensor"),
            P("fsdp", "tensor"),
            P("fsdp", "tensor"),
            P("tensor"),
            P("tensor"),
            P("tensor", "fsdp"),
            P(),
            P(),
            P(),
            P("fsdp", "tensor"),
            P("tensor"),
            P("tensor", "fsdp"),
            P(),
        ),
        check_vma=False,
    )
```

```python
import math
from types import SimpleNamespace

import jax
import jax.numpy as jnp
from jax import lax
from jax.experimental import pallas as pl
from jax.experimental.pallas import tpu as pltpu
from jax.sharding import PartitionSpec as P

D = 1152
HD = 72
FF = 4304
SEQ = 256


norm_eps = 1e-06
gelu_coef = 0.7978845608028654
cubic_coef = 0.044715


def dot_plain(left, right):
    return jnp.dot(left, right, preferred_element_type=jnp.float32)


def dot_right_t(left, right):
    return lax.dot_general(
        left, right, (((1,), (1,)), ((), ())), preferred_element_type=jnp.float32
    )


def dot_left_t(left, right):
    return lax.dot_general(
        left, right, (((0,), (0,)), ((), ())), preferred_element_type=jnp.float32
    )


def norm_rows(values, gain, shift):
    row_mean = jnp.mean(values, axis=1, keepdims=True)
    centred = values - row_mean
    inv_scale = lax.rsqrt(jnp.mean(centred * centred, axis=1, keepdims=True) + norm_eps)
    normed = centred * inv_scale
    return (normed * gain + shift, normed, inv_scale)


def norm_back(out_grad, normed, inv_scale, gain):
    scaled_grad = out_grad * gain
    grad_mean = jnp.mean(scaled_grad, axis=1, keepdims=True)
    cross_mean = jnp.mean(scaled_grad * normed, axis=1, keepdims=True)
    in_grad = inv_scale * (scaled_grad - grad_mean - normed * cross_mean)
    return (in_grad, jnp.sum(out_grad * normed, axis=0), jnp.sum(out_grad, axis=0))


def gelu_pair(upper):
    tangent = jnp.tanh(gelu_coef * (upper + cubic_coef * upper * upper * upper))
    gelu_value = 0.5 * upper * (1.0 + tangent)
    gelu_slope = 0.5 * (1.0 + tangent) + 0.5 * upper * (1.0 - tangent * tangent) * gelu_coef * (
        1.0 + 3.0 * cubic_coef * upper * upper
    )
    return (gelu_value, gelu_slope)


def split_heads(block_rows, head_count):
    col_width = block_rows.shape[1] // 3
    img_count = block_rows.shape[0] // SEQ
    shape_four = (img_count, SEQ, head_count, HD)
    queries = block_rows[:, :col_width].reshape(shape_four)
    keys_part = block_rows[:, col_width : 2 * col_width].reshape(shape_four)
    values = block_rows[:, 2 * col_width :].reshape(shape_four)
    return (queries, keys_part, values, shape_four)


def attend_forward(block_rows, head_count):
    queries, keys_part, values, shape_four = split_heads(block_rows, head_count)
    scores = jnp.einsum(
        "nqhd,nkhd->nhqk", queries, keys_part, preferred_element_type=jnp.float32
    ) * HD ** (-0.5)
    peak = jnp.max(scores, axis=-1, keepdims=True)
    expo = jnp.exp(scores - peak)
    totals = jnp.sum(expo, axis=-1, keepdims=True)
    prob_low = (expo / totals).astype(jnp.bfloat16)
    mixed = jnp.einsum("nhqk,nkhd->nqhd", prob_low, values, preferred_element_type=jnp.float32)
    row_total = block_rows.shape[0]
    mixed = mixed.reshape(row_total, head_count * HD).astype(jnp.bfloat16)
    return (mixed, (peak + jnp.log(totals))[..., 0])


def attend_backward(inputs, head_count):
    block_rows, grad_block, log_total = inputs
    queries, keys_part, values, shape_four = split_heads(block_rows, head_count)
    grad_out = grad_block.reshape(shape_four)
    scores = jnp.einsum(
        "nqhd,nkhd->nhqk", queries, keys_part, preferred_element_type=jnp.float32
    ) * HD ** (-0.5)
    probs = jnp.exp(scores - log_total[..., None])
    prob_low = probs.astype(jnp.bfloat16)
    value_grad = jnp.einsum(
        "nhqk,nqhd->nkhd", prob_low, grad_out, preferred_element_type=jnp.float32
    )
    prob_grad = jnp.einsum("nqhd,nkhd->nhqk", grad_out, values, preferred_element_type=jnp.float32)
    row_dot = jnp.sum(probs * prob_grad, axis=-1, keepdims=True)
    score_grad = (probs * (prob_grad - row_dot)).astype(jnp.bfloat16)
    query_grad = jnp.einsum(
        "nhqk,nkhd->nqhd", score_grad, keys_part, preferred_element_type=jnp.float32
    ) * HD ** (-0.5)
    key_grad = jnp.einsum(
        "nhqk,nqhd->nkhd", score_grad, queries, preferred_element_type=jnp.float32
    ) * HD ** (-0.5)
    row_total = block_rows.shape[0]
    col_width = head_count * HD
    return jnp.concatenate(
        (
            query_grad.reshape(row_total, col_width),
            key_grad.reshape(row_total, col_width),
            value_grad.reshape(row_total, col_width),
        ),
        axis=1,
    ).astype(jnp.bfloat16)


def on_device(
    tokens,
    cotangent,
    first_gain,
    first_shift,
    query_weight,
    key_weight,
    value_weight,
    query_bias,
    value_bias,
    out_weight,
    out_bias,
    second_gain,
    second_shift,
    up_weight,
    up_bias,
    down_weight,
    down_bias,
):
    full_query, full_key, full_value, full_outp, full_up, full_down = (
        lax.all_gather(query_weight, "fsdp", axis=0, tiled=True),
        lax.all_gather(key_weight, "fsdp", axis=0, tiled=True),
        lax.all_gather(value_weight, "fsdp", axis=0, tiled=True),
        lax.all_gather(out_weight, "fsdp", axis=1, tiled=True),
        lax.all_gather(up_weight, "fsdp", axis=0, tiled=True),
        lax.all_gather(down_weight, "fsdp", axis=1, tiled=True),
    )
    qkv_weight = jnp.concatenate((full_query, full_key, full_value), axis=1)
    local_width = full_query.shape[1]
    ffn_width = full_up.shape[1]
    head_count = local_width // HD
    token_rows = tokens.astype(jnp.float32)
    first_out, first_hat, first_scale = norm_rows(token_rows, first_gain, first_shift)
    all_first = lax.all_gather(first_out.astype(jnp.bfloat16), "tensor", axis=0, tiled=True)
    qkv_bias = jnp.concatenate((query_bias, jnp.zeros_like(query_bias), value_bias))
    qkv_rows = (dot_plain(all_first, qkv_weight) + qkv_bias).astype(jnp.bfloat16)
    group_rows = qkv_rows.shape[0]
    images = group_rows // SEQ
    per_block = math.gcd(images, max(1, 512 // SEQ))
    blocks = images // per_block
    stacked = qkv_rows.reshape(blocks, per_block * SEQ, 3 * local_width)

    def forward_block(block_rows):
        return attend_forward(block_rows, head_count)

    head_out, log_total = lax.map(forward_block, stacked)
    head_out = head_out.reshape(group_rows, local_width)
    attn_rows = lax.psum_scatter(
        dot_plain(head_out, full_outp), "tensor", scatter_dimension=0, tiled=True
    )
    mid_rows = token_rows + attn_rows + out_bias
    second_out, second_hat, second_scale = norm_rows(mid_rows, second_gain, second_shift)
    all_second = lax.all_gather(second_out.astype(jnp.bfloat16), "tensor", axis=0, tiled=True)
    up_pre = dot_plain(all_second, full_up) + up_bias
    hidden_value, hidden_slope = gelu_pair(up_pre)
    hidden_low = hidden_value.astype(jnp.bfloat16)
    mlp_rows = lax.psum_scatter(
        dot_plain(hidden_low, full_down).astype(jnp.bfloat16),
        "tensor",
        scatter_dimension=0,
        tiled=True,
    ).astype(jnp.float32)
    layer_out = (mid_rows + mlp_rows + down_bias).astype(jnp.bfloat16)
    out_grad = cotangent.astype(jnp.float32)
    all_out_grad = lax.all_gather(cotangent, "tensor", axis=0, tiled=True)
    down_grad = dot_left_t(hidden_low, all_out_grad)
    hidden_grad = dot_right_t(all_out_grad, full_down)
    upper_low = (hidden_grad * hidden_slope).astype(jnp.bfloat16)
    up_bias_grad = jnp.sum(upper_low.astype(jnp.float32), axis=0)
    up_grad = dot_left_t(all_second, upper_low)
    second_grad = lax.psum_scatter(
        dot_right_t(upper_low, full_up), "tensor", scatter_dimension=0, tiled=True
    )
    back_second, second_gain_grad, second_shift_grad = norm_back(
        second_grad, second_hat, second_scale, second_gain
    )
    mid_grad = out_grad + back_second
    mid_low = mid_grad.astype(jnp.bfloat16)
    all_mid_grad = lax.all_gather(mid_low, "tensor", axis=0, tiled=True)
    outp_grad = dot_left_t(head_out, all_mid_grad)
    head_grad = dot_right_t(all_mid_grad, full_outp).astype(jnp.bfloat16)

    def backward_block(inputs):
        return attend_backward(inputs, head_count)

    qkv_grad = lax.map(
        backward_block,
        (stacked, head_grad.reshape(blocks, per_block * SEQ, local_width), log_total),
    )
    qkv_grad = qkv_grad.reshape(group_rows, 3 * local_width)
    qkv_weight_grad = dot_left_t(all_first, qkv_grad)
    qkv_bias_grad = jnp.sum(qkv_grad.astype(jnp.float32), axis=0)
    first_grad = lax.psum_scatter(
        dot_right_t(qkv_grad, qkv_weight).astype(jnp.bfloat16),
        "tensor",
        scatter_dimension=0,
        tiled=True,
    ).astype(jnp.float32)
    back_first, first_gain_grad, first_shift_grad = norm_back(
        first_grad, first_hat, first_scale, first_gain
    )
    input_grad = mid_grad + back_first
    out_bias_grad = jnp.sum(mid_low.astype(jnp.float32), axis=0)
    down_bias_grad = jnp.sum(out_grad, axis=0)
    small_terms = jnp.concatenate(
        (
            first_gain_grad,
            first_shift_grad,
            out_bias_grad,
            second_gain_grad,
            second_shift_grad,
            down_bias_grad,
        )
    )
    tensor_index = lax.axis_index("tensor")
    head_terms = jnp.zeros((2 * D + FF,), jnp.float32)
    head_terms = lax.dynamic_update_slice(
        head_terms, qkv_bias_grad[:local_width], (tensor_index * local_width,)
    )
    head_terms = lax.dynamic_update_slice(
        head_terms, qkv_bias_grad[2 * local_width :], (D + tensor_index * local_width,)
    )
    head_terms = lax.dynamic_update_slice(
        head_terms, up_bias_grad, (2 * D + tensor_index * ffn_width,)
    )
    small_sums, head_sums = lax.psum((small_terms, head_terms), ("fsdp", "tensor"))
    query_bias_total = lax.dynamic_slice(head_sums, (tensor_index * local_width,), (local_width,))
    value_bias_total = lax.dynamic_slice(
        head_sums, (D + tensor_index * local_width,), (local_width,)
    )
    up_bias_total = lax.dynamic_slice(head_sums, (2 * D + tensor_index * ffn_width,), (ffn_width,))
    query_part, key_part, value_part, outp_part, up_part, down_part = (
        lax.psum_scatter(qkv_weight_grad[:, :local_width], "fsdp", scatter_dimension=0, tiled=True),
        lax.psum_scatter(
            qkv_weight_grad[:, local_width : 2 * local_width],
            "fsdp",
            scatter_dimension=0,
            tiled=True,
        ),
        lax.psum_scatter(
            qkv_weight_grad[:, 2 * local_width :], "fsdp", scatter_dimension=0, tiled=True
        ),
        lax.psum_scatter(outp_grad, "fsdp", scatter_dimension=1, tiled=True),
        lax.psum_scatter(up_grad, "fsdp", scatter_dimension=0, tiled=True),
        lax.psum_scatter(down_grad, "fsdp", scatter_dimension=1, tiled=True),
    )
    return (
        layer_out,
        input_grad,
        small_sums[0:D],
        small_sums[D : 2 * D],
        query_part,
        key_part,
        value_part,
        query_bias_total,
        value_bias_total,
        outp_part,
        small_sums[2 * D : 3 * D],
        small_sums[3 * D : 4 * D],
        small_sums[4 * D : 5 * D],
        up_part,
        up_bias_total,
        down_part,
        small_sums[5 * D : 6 * D],
    )


MESH_IDS = pl.DeviceIdType.MESH
LANES = 128


def round_up(value, step):
    return -(-value // step) * step


def row_cuts(count, parts):
    edges = [min(count, round_up(count * at // parts, 16)) for at in range(parts + 1)]
    return list(zip(edges[:-1], edges[1:]))


class Remote:
    def __init__(self, send_sems, recv_sems):
        self.send_sems, self.recv_sems = send_sems, recv_sems
        self.used = 0
        self.sent = 0
        self.slots = [None] * send_sems.shape[0]

    def sem(self):
        self.used += 1
        return self.used - 1

    def sems(self, count):
        return [self.sem() for _ in range(count)]

    def release(self, slot):
        if self.slots[slot] is not None:
            copy, when = self.slots[slot]
            guarded(when, copy.wait_send)

    def send(self, src, dst, device, recv, when=None):
        slot = self.sent % len(self.slots)
        self.sent += 1
        self.release(slot)
        copy = pltpu.make_async_remote_copy(
            src_ref=src,
            dst_ref=dst,
            send_sem=self.send_sems.at[slot],
            recv_sem=self.recv_sems.at[recv],
            device_id=device,
            device_id_type=MESH_IDS,
        )
        guarded(when, copy.start)
        self.slots[slot] = copy, when

    def local(self, src, dst, sem, when):
        copy = pltpu.make_async_copy(src, dst, self.recv_sems.at[sem])
        guarded(when, copy.start)

    def arrived(self, dst, sem):
        pltpu.make_async_copy(dst, dst, self.recv_sems.at[sem]).wait()

    def drain(self):
        for slot in range(len(self.slots)):
            self.release(slot)


def guarded(when, action):
    if when is None:
        action()
    else:
        pl.when(when)(action)


def layer_kernel(shapes, names, *refs):
    rows, heads, width, units, qkv_lanes, piece = shapes
    inputs, outputs, scratch = names
    hbm = SimpleNamespace(**dict(zip(inputs, refs[: len(inputs)], strict=True)))
    refs = refs[len(inputs) :]
    out = SimpleNamespace(**dict(zip(outputs, refs[: len(outputs)], strict=True)))
    refs = refs[len(outputs) :]
    held = SimpleNamespace(**dict(zip(inputs, refs[: len(inputs)], strict=True)))
    refs = refs[len(inputs) :]
    ref = SimpleNamespace(**dict(zip(scratch, refs, strict=True)))
    bf16, f32 = jnp.bfloat16, jnp.float32
    attn_w, up_w, down_w = ref.attn_w, ref.up_w, ref.down_w
    attn_g, up_g, down_g = ref.attn_g, ref.up_g, ref.down_g
    first_all, second_all = ref.first_all, ref.second_all
    dy_all, mid_all = ref.dy_all, ref.mid_all
    head_rows, head_grads = ref.head_rows, ref.head_grads
    mixed_all, hidden_all, upper_all = ref.mixed_all, ref.hidden_all, ref.upper_all
    slope_all, qkv_grads = ref.slope_all, ref.qkv_grads
    part_a, part_b, vectors = ref.part_a, ref.part_b, ref.vectors
    pair, fourth = 2 * rows, rows // 2
    out_base = 3 * width
    win = out_base // LANES * LANES
    win_shift = out_base - win
    skip = qkv_lanes - win
    all_lanes, ff_lanes = attn_w.shape[1], up_w.shape[1]
    main = units // LANES * LANES
    rest = units - main

    f = lax.axis_index("fsdp")
    t = lax.axis_index("tensor")
    c, k = lax.rem(f, 2), lax.div(f, 2)
    kx, ky = lax.rem(k, 2), lax.div(k, 2)
    zl, zh = lax.rem(t, 2), lax.div(t, 2)
    oc, ox = 1 - c, 1 - kx
    k_x, k_y, k_d = ky * 2 + ox, (1 - ky) * 2 + kx, (1 - ky) * 2 + ox
    home = c == zh
    away = jnp.logical_not(home)
    stay = kx == zh
    outer = zl == zh
    inner = jnp.logical_not(outer)
    move = jnp.logical_not(stay)
    far_t = (1 - zh) * 2 + zl
    dev_x = {"fsdp": 2 * k_x + c, "tensor": t}
    dev_y = {"fsdp": 2 * k_y + c, "tensor": t}
    dev_c = {"fsdp": 2 * k + oc, "tensor": t}
    dev_z = {"fsdp": f, "tensor": zh * 2 + (1 - zl)}
    dev_far = {"fsdp": f, "tensor": far_t}
    dev_far_other = {"fsdp": 2 * k + oc, "tensor": far_t}
    net = Remote(ref.send_sems, ref.recv_sems)

    def aligned(start, size):
        return pl.ds(pl.multiple_of(start, math.gcd(size, LANES)), size)

    def piece_at(index):
        return pl.ds(pl.multiple_of(index * piece, piece), piece)

    def block(buf, index, lo=0, hi=None):
        return buf.at[piece_at(index), lo : buf.shape[1] if hi is None else hi]

    near, deep = zl * pair, (1 - zl) * pair

    def slot(side, place):
        return aligned(side + place * rows, rows)

    def spread_start(src, buf, lo, hi):
        base, _ = net.sems(2)
        source, target = src.at[:, lo:hi], block(buf, f, lo, hi)
        net.local(source, target, base + c, home)
        to = {"fsdp": 2 * k + zh, "tensor": t}
        net.send(source, target, to, base + c, when=away)
        to = {"fsdp": 2 * k + zh, "tensor": far_t}
        net.send(source, target, to, base + c)
        return base

    def gather_start(buf, lo, hi, base):
        sems = net.sems(3)
        a_own, b_own = block(buf, 2 * k, lo, hi), block(buf, 2 * k + 1, lo, hi)
        net.arrived(a_own, base)
        net.send(a_own, a_own, dev_x, sems[0])
        net.arrived(b_own, base + 1)
        net.send(b_own, b_own, dev_y, sems[1])
        net.send(a_own, a_own, dev_y, sems[2])
        net.send(b_own, b_own, dev_x, sems[2])
        return sems

    def gather_forward(buf, lo, hi, sems):
        a_x, b_y = block(buf, 2 * k_x, lo, hi), block(buf, 2 * k_y + 1, lo, hi)
        net.arrived(a_x, sems[0])
        net.send(a_x, a_x, dev_y, sems[2])
        net.arrived(b_y, sems[1])
        net.send(b_y, b_y, dev_x, sems[2])

    def gather_finish(buf, lo, hi, sems):
        net.arrived(buf.at[0 : 4 * piece, lo:hi], sems[2])

    f_x, f_y, f_d = 2 * k_x + c, 2 * k_y + c, 2 * k_d + c

    class WideGather:
        def __init__(self, src, buf, wait_at, lo, hi):
            self.buf, self.lo, self.size = buf, lo, hi - lo
            self.src, self.wait_at = src.at[lo:hi, :], wait_at.at[lo:hi, :]
            self.sems = net.sems(6)

        def at(self, index):
            start = pl.multiple_of(index * piece + self.lo, 16)
            return self.buf.at[pl.ds(start, self.size), :]

        def start(self, when):
            own, sems = self.at(f), self.sems
            stay_now, move_now = jnp.logical_and(stay, when), jnp.logical_and(move, when)
            net.local(self.src, own, sems[4], stay_now)
            net.send(self.src, own, dev_far, sems[0], when=stay_now)
            net.send(self.src, self.wait_at, dev_far, sems[0], when=move_now)

        def beside(self):
            net.send(self.src, self.at(f), dev_x, self.sems[1], when=move)

        def second(self):
            own, sems = self.at(f), self.sems

            @pl.when(stay)
            def _():
                net.arrived(self.wait_at, sems[0])

            @pl.when(move)
            def _():
                net.arrived(own, sems[0])

            net.send(self.wait_at, own, dev_x, sems[1], when=stay)

            @pl.when(stay)
            def _():
                net.arrived(own, sems[4])

            net.send(own, own, dev_y, sems[2])
            net.send(own, own, dev_c, sems[3])

        def third(self):
            got = self.at(f_x)
            net.arrived(got, self.sems[1])
            net.send(got, got, dev_y, self.sems[5])
            net.send(got, got, dev_c, self.sems[3])

        def fourth(self):
            for index, sem in ((f_y, 2), (f_d, 5)):
                got = self.at(index)
                net.arrived(got, self.sems[sem])
                net.send(got, got, dev_c, self.sems[3])

        def finish(self):
            net.arrived(self.buf.at[0 : 4 * self.size, :], self.sems[3])

    def share_start(buf):
        sems = net.sems(3)
        own = buf.at[slot(near, c)]
        net.send(own, own, dev_z, sems[0])
        net.send(own, own, dev_c, sems[1])
        return sems

    def share_near(buf, sems):
        net.arrived(buf.at[slot(near, oc)], sems[1])

    def share_forward(buf, sems):
        got = buf.at[slot(deep, c)]
        net.arrived(got, sems[0])
        net.send(got, got, dev_c, sems[2])

    def share_deep(buf, sems):
        net.arrived(buf.at[slot(deep, oc)], sems[2])

    def sum_deep(which, part):
        sems = net.sems(3)
        send = ref.core_send.at[which, 0]
        send[...] = part[slot(deep, oc), :].astype(bf16)
        net.send(send, ref.core_land.at[which, 0], dev_c, sems[0])
        return sems

    def sum_pass(which, part, sems):
        land, send = ref.core_land.at[which, 0], ref.deep_send.at[which]
        net.arrived(land, sems[0])
        send[...] = (part[slot(deep, c), :] + land[...].astype(f32)).astype(bf16)
        net.send(send, ref.deep_land.at[which], dev_z, sems[1])

    def sum_near(which, part, sems):
        send = ref.core_send.at[which, 1]
        send[...] = part[slot(near, oc), :].astype(bf16)
        net.send(send, ref.core_land.at[which, 1], dev_c, sems[2])

    def sum_finish(which, part, sems):
        beside, across = ref.core_land.at[which, 1], ref.deep_land.at[which]
        net.arrived(beside, sems[2])
        total = part[slot(near, c), :] + beside[...].astype(f32)
        net.arrived(across, sems[1])
        return total + across[...].astype(f32)

    def quarter(side, place, which):
        return aligned(side + place * rows + which * fourth, fourth)

    def wide_share_start(buf):
        sems = net.sems(4)
        first, second = buf.at[quarter(near, kx, 0)], buf.at[quarter(near, kx, 1)]
        net.send(first, first, dev_z, sems[0])
        net.send(second, second, dev_x, sems[1])
        net.send(second, second, dev_z, sems[3])
        net.send(first, first, dev_x, sems[2])
        return sems

    def wide_share_forward(buf, sems):
        from_z, from_x = buf.at[quarter(deep, kx, 0)], buf.at[quarter(near, ox, 1)]
        net.arrived(from_z, sems[0])
        net.send(from_z, from_z, dev_x, sems[3])
        net.arrived(from_x, sems[1])
        net.send(from_x, from_x, dev_z, sems[3])

    def wide_share_near(buf, sems):
        net.arrived(buf.at[quarter(near, ox, 0)], sems[2])

    def wide_share_deep(buf, sems):
        net.arrived(buf.at[0 : 3 * fourth, :], sems[3])

    def plain_share_z(buf):
        sems = net.sems(3)
        own = buf.at[slot(near, kx)]
        net.send(own, own, dev_z, sems[0])
        return sems

    def plain_share_x(buf, sems):
        own = buf.at[slot(near, kx)]
        net.send(own, own, dev_x, sems[1])

    def plain_share_forward(buf, sems):
        got = buf.at[slot(near, ox)]
        net.arrived(got, sems[1])
        net.send(got, got, dev_z, sems[2])

    def plain_share_finish(buf, sems):
        net.arrived(buf.at[slot(deep, kx)], sems[0])
        net.arrived(buf.at[slot(deep, ox)], sems[2])

    def wide_send(which, number):
        return ref.wide_send.at[which, number]

    def wide_land(which, number):
        return ref.wide_land.at[which, number]

    def wide_push(which, number, value, device, sem):
        wide_send(which, number)[...] = value.astype(bf16)
        net.send(wide_send(which, number), wide_land(which, number), device, sem)

    def wide_sum_deep(which, part):
        sems = net.sems(6)
        wide_push(which, 0, part[quarter(deep, ox, 0), :], dev_x, sems[0])
        wide_push(which, 1, part[quarter(deep, ox, 1), :], dev_z, sems[1])
        wide_push(which, 2, part[quarter(deep, kx, 1), :], dev_z, sems[2])
        return sems

    def wide_sum_near(which, part, sems):
        wide_push(which, 3, part[quarter(near, ox, 0), :], dev_x, sems[3])

    def wide_sum_pass(which, part, sems):
        net.arrived(wide_land(which, 0), sems[0])
        total = part[quarter(deep, kx, 0), :] + wide_land(which, 0)[...].astype(f32)
        wide_push(which, 4, total, dev_z, sems[4])
        net.arrived(wide_land(which, 1), sems[1])
        total = part[quarter(near, ox, 1), :] + wide_land(which, 1)[...].astype(f32)
        wide_push(which, 5, total, dev_x, sems[5])

    def wide_sum_finish(which, part, sems):
        halves = []
        for half_at, (by_z, by_x) in enumerate(((4, 3), (2, 5))):
            net.arrived(wide_land(which, by_z), sems[by_z])
            net.arrived(wide_land(which, by_x), sems[by_x])
            halves.append(
                part[quarter(near, kx, half_at), :]
                + wide_land(which, by_z)[...].astype(f32)
                + wide_land(which, by_x)[...].astype(f32)
            )
        return jnp.concatenate(halves, axis=0)

    def add_into(grad, index, lo, hi, land):
        at = piece_at(index)
        total = grad[at, lo:hi].astype(f32) + land[...].astype(f32)
        grad[at, lo:hi] = total.astype(bf16)

    def reduce_route(core, by_y):
        if core == 0 or by_y:
            return dev_y, 2 * k_y + core, 2 * k_x + core, dev_x
        return dev_x, 2 * k_x + core, 2 * k_y + core, dev_y

    def reduce_first(grad, land, lo, hi, sems, by_y=False, when=None):
        for distant in (True, False):
            for core in range(2):
                device, index, _, _ = reduce_route(core, by_y)
                index, number = (2 * k_d + core, 1 + 2 * core) if distant else (index, 2 * core)
                source = block(grad, index, lo, hi)
                net.send(source, land.at[number], device, sems[number], when=when)

    def reduce_second(grad, land, lo, hi, sems, by_y=False, when=None):
        def collect(index, number):
            def action():
                net.arrived(land.at[number], sems[number])
                add_into(grad, index, lo, hi, land.at[number])

            guarded(when, action)

        for core in range(2):
            _, _, index, device = reduce_route(core, by_y)
            collect(index, 1 + 2 * core)
            source = block(grad, index, lo, hi)
            net.send(source, land.at[4 + core], device, sems[4 + core], when=when)
        for core in range(2):
            collect(2 * k + core, 2 * core)

    def reduce_third(grad, land, lo, hi, sems, when=None):
        def here(condition):
            return condition if when is None else jnp.logical_and(when, condition)

        for core in range(2):

            def collect(core=core):
                net.arrived(land.at[4 + core], sems[4 + core])
                add_into(grad, 2 * k + core, lo, hi, land.at[4 + core])

            guarded(when, collect)
            source = block(grad, 2 * k + core, lo, hi)
            mine, other = jnp.logical_and(home, c == core), jnp.logical_and(home, c != core)
            net.local(source, land.at[6], sems[6], here(mine))
            to = {"fsdp": 2 * k + core, "tensor": t}
            net.send(source, land.at[6], to, sems[6], when=here(other))
            to = {"fsdp": 2 * k + core, "tensor": far_t}
            net.send(source, land.at[7], to, sems[7], when=here(away))

    def reduce_finish(land, sems):
        net.arrived(land.at[6], sems[6])
        net.arrived(land.at[7], sems[7])
        return land[6].astype(f32) + land[7].astype(f32)

    def wide_reduce_first(grad, land):
        sems = net.sems(6)
        for number, index in enumerate((f_d, f_y, f, f_x)):
            sem = sems[0] if number < 2 else sems[1]
            net.send(block(grad, index + oc - c), land.at[number], dev_c, sem)
        return sems

    def wide_reduce_second(grad, land, sems):
        net.arrived(land.at[0:2], sems[0])
        for number, index in enumerate((f_d, f_y)):
            add_into(grad, index, 0, grad.shape[1], land.at[number])
            net.send(block(grad, index), land.at[4 + number], dev_y, sems[4 + number])
        net.arrived(land.at[2:4], sems[1])
        for number, index in ((2, f), (3, f_x)):
            add_into(grad, index, 0, grad.shape[1], land.at[number])

    def wide_reduce_third(grad, land, sems):
        net.arrived(land.at[4], sems[4])
        add_into(grad, f_x, 0, grad.shape[1], land.at[4])
        net.send(block(grad, f_x), land.at[6], dev_x, sems[2])
        net.arrived(land.at[5], sems[5])
        add_into(grad, f, 0, grad.shape[1], land.at[5])

    def wide_reduce_cross(grad, land, sems, when):
        now = jnp.logical_and(move, when)
        net.send(block(grad, f), land.at[7], dev_far, sems[3], when=now)

    def wide_reduce_fourth(grad, land, sems, when):
        guarded(when, lambda: net.arrived(land.at[6], sems[2]))
        now = jnp.logical_and(stay, when)
        net.send(land.at[6], land.at[7], dev_far, sems[3], when=now)

    def wide_reduce_finish(grad, land, sems):
        kept = jnp.where(stay, grad[piece_at(f), :].astype(f32), land[6].astype(f32))
        net.arrived(land.at[7], sems[3])
        return kept + land[7].astype(f32)

    vec_own, by_plane, by_chip = ref.vec_own, ref.by_plane, ref.by_chip
    plane_peers = [lax.rem(t + step, 4) for step in range(1, 4)]
    chip_peers = [lax.rem(k + step, 4) for step in range(1, 4)]

    def vector_planes():
        by_plane[t] = vec_own[...]
        sem = net.sem()
        for plane in plane_peers:
            net.send(vec_own, by_plane.at[t], {"fsdp": f, "tensor": plane}, sem)
        return sem

    def vector_chips(sem):
        net.arrived(by_plane.at[0:3], sem)
        both = ref.vec_chip
        total = by_plane[0] + by_plane[1] + by_plane[2] + by_plane[3]
        shard = by_plane[zl] + by_plane[2 + zl]
        both[0:6, :] = total[0:6, :]
        both[6:8, :] = shard[6:8, :]
        by_chip[k] = both[...]
        sem = net.sem()
        for chip in chip_peers:
            net.send(both, by_chip.at[k], {"fsdp": 2 * chip + c, "tensor": t}, sem)
        return sem

    def vector_core(sem):
        net.arrived(by_chip.at[0:3], sem)
        held = ref.vec_core
        total = by_chip[0] + by_chip[1] + by_chip[2] + by_chip[3]
        units_total = by_chip[zh] + by_chip[2 + zh]
        held[0:6, :] = total[0:6, :]
        held[6:7, :] = units_total[6:7, :]
        held[7:8, :] = total[7:8, :]
        sem = net.sem()
        net.send(held, ref.vec_core_land, dev_c, sem)
        return sem

    def vector_finish(sem):
        held, land, done = ref.vec_core, ref.vec_core_land, ref.vec_done
        net.arrived(land, sem)
        done[0:7, :] = held[0:7, :] + land[0:7, :]
        done[7:8, :] = jnp.where(home, held[7:8, :], land[7:8, :])

    barrier = pltpu.get_barrier_semaphore()
    peers = (dev_x, dev_y, dev_c, dev_z, dev_far, dev_far_other)
    for peer in peers:
        pl.semaphore_signal(barrier, inc=1, device_id=peer, device_id_type=MESH_IDS)

    coming = {}
    for number, name in enumerate(inputs):
        copy = pltpu.make_async_copy(
            getattr(hbm, name), getattr(held, name), ref.load_sems.at[number]
        )
        copy.start()
        coming[name] = copy
    coming = SimpleNamespace(**coming)
    stores = []

    def store(source, target):
        sem = ref.load_sems.at[len(inputs) + len(stores)]
        copy = pltpu.make_async_copy(source, target, sem)
        copy.start()
        stores.append(copy)

    attn_piece = ref.attn_piece
    if all_lanes > 4 * width:
        attn_piece[:, 4 * width :] = jnp.zeros((piece, all_lanes - 4 * width), bf16)
    for number, (copy, raw) in enumerate(
        (
            (coming.query_w, held.query_w),
            (coming.key_w, held.key_w),
            (coming.value_w, held.value_w),
            (coming.out_w, held.out_w),
        )
    ):
        copy.wait()
        attn_piece[:, number * width : (number + 1) * width] = raw[...]
    vectors[...] = jnp.zeros_like(vectors)
    for number, (copy, raw) in enumerate(
        (
            (coming.first_gain, held.first_gain),
            (coming.first_shift, held.first_shift),
            (coming.out_bias, held.out_bias),
            (coming.second_gain, held.second_gain),
            (coming.second_shift, held.second_shift),
            (coming.down_bias, held.down_bias),
        )
    ):
        copy.wait()
        vectors[number : number + 1, :] = raw[...].reshape(1, D)
    coming.up_bias.wait()
    vectors[6:7, :units] = held.up_bias[...].reshape(1, units)
    coming.query_bias.wait()
    vectors[7:8, :width] = held.query_bias[...].reshape(1, width)
    coming.value_bias.wait()
    vectors[7:8, 2 * width : 3 * width] = held.value_bias[...].reshape(1, width)
    first_gain, first_shift = vectors[0:1, :], vectors[1:2, :]
    out_bias, second_gain = vectors[2:3, :], vectors[3:4, :]
    second_shift, down_bias = vectors[4:5, :], vectors[5:6, :]
    tokens_ref, cotangent_ref = held.tokens, held.cotangent
    coming.tokens.wait()
    coming.cotangent.wait()
    token_rows = tokens_ref[...].astype(f32)
    normed, hat, inv_scale = norm_rows(token_rows, first_gain, first_shift)
    first_all[slot(near, c), :] = normed.astype(bf16)
    ref.first_hat[...] = hat
    ref.row_scale[0] = jnp.broadcast_to(inv_scale, (rows, LANES))

    pl.semaphore_wait(barrier, len(peers))

    first_sems = share_start(first_all)
    lane_cut = round_up(qkv_lanes // 2, LANES)
    q_parts = [(attn_w, 0, lane_cut), (attn_w, lane_cut, qkv_lanes)]
    o_part = (attn_w, qkv_lanes, all_lanes)
    q_base = [spread_start(attn_piece, *part) for part in q_parts]
    o_base = spread_start(attn_piece, *o_part)
    vec_sem = net.sem()
    net.send(vectors, ref.far_vectors, dev_far, vec_sem)
    up_parts = [
        WideGather(ref.up_piece, up_w, ref.up_wait, lo, hi)
        for lo, hi in ((0, 64), (64, 144))
    ]
    down_parts = [
        WideGather(ref.down_piece, down_w, ref.down_wait, lo, hi)
        for lo, hi in row_cuts(piece, 3)
    ]

    coming.up_w.wait()
    coming.down_w.wait()
    ref.up_piece[:, main:] = jnp.zeros((piece, LANES), bf16)
    ref.up_piece[:, :units] = held.up_w[...]
    ref.up_piece[:, units : units + rest] = held.down_w[:, main:]
    ref.down_piece[...] = held.down_w[:, :main]
    dy_all[slot(near, kx), :] = cotangent_ref[...]
    vec_own[5:6, :] = jnp.sum(cotangent_ref[...].astype(f32), axis=0, keepdims=True)
    head_rows[...] = jnp.zeros_like(head_rows)
    head_grads[...] = jnp.zeros_like(head_grads)
    mixed_all[...] = jnp.zeros_like(mixed_all)
    qkv_grads[...] = jnp.zeros_like(qkv_grads)

    def shard_vector(row, own):
        return jnp.where(own, vectors[row : row + 1, :], ref.far_vectors[row : row + 1, :])

    scale = HD ** (-0.5)

    def image_head(step):
        head, image = lax.rem(step, heads), lax.div(step, heads)
        return head, aligned(image * pair, pair)

    def attend(step, carry):
        head, span = image_head(step)
        queries, keys_part = head_rows[head, span, :], head_rows[heads + head, span, :]
        values = head_rows[2 * heads + head, span, :]
        scores = dot_right_t(queries, keys_part) * scale
        expo = jnp.exp(scores - jnp.max(scores, axis=1, keepdims=True))
        probs = expo / jnp.sum(expo, axis=1, keepdims=True)
        ref.probs_all[step] = probs
        mixed = dot_plain(probs.astype(bf16), values)
        ref.mixed_heads[head, span, :] = mixed.astype(bf16)
        return carry

    def pack(target, source, count, base):
        for side_at in range(2):
            for image in range(2):
                at = slice(side_at * pair + image * rows, side_at * pair + (image + 1) * rows)
                take = slice(image * pair + side_at * rows, image * pair + (side_at + 1) * rows)
                for head in range(count):
                    lo = base + head * HD
                    target[at, lo : lo + HD] = source[head, take, :HD]

    def half(side):
        return aligned(side, pair)

    chunk = 32

    in_rest = lax.broadcasted_iota(jnp.int32, (chunk, LANES), 1) < rest

    hidden_rest = ref.hidden_rest

    def raise_half(side):
        part_b[half(side), :] = dot_plain(second_all[half(side), :], up_w[...])

        def gelu_rows(step, carry):
            at = aligned(side + step * chunk, chunk)
            value, slope = gelu_pair(part_b[at, :] + up_bias)
            last = jnp.where(in_rest, value[:, main:], 0.0)
            hidden_all[at, :main] = value[:, :main].astype(bf16)
            hidden_all[at, main:] = last.astype(bf16)
            hidden_rest[at, :] = pltpu.roll(last, rest, 1).astype(bf16)
            slope_all[at, :] = slope
            return carry

        lax.fori_loop(0, pair // chunk, gelu_rows, 0)

    tile = 3 * LANES

    def outer_product(grad, left, right, lo, hi):
        def rows_of(step, carry):
            at = aligned(step * tile, tile)
            grad[at, lo:hi] = dot_left_t(left[:, at], right).astype(bf16)
            return carry

        lax.fori_loop(0, D // tile, rows_of, 0, unroll=True)

    def lower_half(side):
        part_b[half(side), :main] = dot_plain(dy_all[half(side), :], down_w[...])
        part_b[half(side), main:] = dot_plain(dy_all[half(side), :], up_w[:, main:])

        def slope_rows(step, totals):
            at = aligned(side + step * chunk, chunk)
            last = pltpu.roll(part_b[at, main:], LANES - rest, 1)
            last = jnp.where(in_rest, last * slope_all[at, main:], 0.0).astype(bf16)
            low = (part_b[at, :main] * slope_all[at, :main]).astype(bf16)
            upper_all[at, :main] = low
            upper_all[at, main:] = last
            return (
                totals[0] + jnp.sum(low.astype(f32), axis=0, keepdims=True),
                totals[1] + jnp.sum(last.astype(f32), axis=0, keepdims=True),
            )

        start = jnp.zeros((1, main), f32), jnp.zeros((1, LANES), f32)
        return lax.fori_loop(0, pair // chunk, slope_rows, start)

    def up_rows(step, carry):
        at = aligned(step * tile, tile)
        by_row = second_all[:, at]
        up_g[at, :main] = dot_left_t(by_row, upper_all[:, :main]).astype(bf16)
        last = dot_left_t(by_row, upper_all[:, main:])
        last = last + dot_left_t(dy_all[:, at], hidden_rest[...])
        up_g[at, main:] = last.astype(bf16)
        return carry

    def lower_product(side):
        total = dot_right_t(hidden_all[half(side), :main], down_w[...])
        return total + dot_right_t(hidden_rest[half(side), :], up_w[:, main:])

    def head_half(side_at):
        side_rows = slice(side_at * pair, (side_at + 1) * pair)
        done = dot_plain(mid_all[side_rows, :], attn_w[:, win:]).astype(bf16)
        for image in range(2):
            to = slice(image * pair + side_at * rows, image * pair + (side_at + 1) * rows)
            for head in range(heads):
                lo = win_shift + head * HD
                head_grads[head, to, :HD] = done[image * rows : (image + 1) * rows, lo : lo + HD]

    cut = round_up(2 * width, LANES)

    def value_back(step, carry):
        head, span = image_head(step)
        low = ref.probs_all[step].astype(bf16)
        value_grad = dot_left_t(low, head_grads[head, span, :])
        ref.mixed_heads[head, span, :] = value_grad.astype(bf16)
        return carry

    def value_out_rows(step, carry):
        at = aligned(step * tile, tile)
        by_value = dot_left_t(first_all[:, at], qkv_grads[:, cut:qkv_lanes])
        by_out = dot_left_t(mid_all[:, at], mixed_all[...])
        both = by_value[:, win - cut :] + by_out[:, :skip]
        attn_g[at, cut:win] = by_value[:, : win - cut].astype(bf16)
        attn_g[at, win:qkv_lanes] = both.astype(bf16)
        attn_g[at, qkv_lanes:] = by_out[:, skip:].astype(bf16)
        return carry

    def attend_back(step, carry):
        head, span = image_head(step)
        queries, keys_part = head_rows[head, span, :], head_rows[heads + head, span, :]
        values, grads = head_rows[2 * heads + head, span, :], head_grads[head, span, :]
        probs = ref.probs_all[step]
        prob_grad = dot_right_t(grads, values)
        row_dot = jnp.sum(probs * prob_grad, axis=1, keepdims=True)
        score_grad = (probs * (prob_grad - row_dot)).astype(bf16)
        query_grad = dot_plain(score_grad, keys_part) * scale
        key_grad = dot_left_t(score_grad, queries) * scale
        head_rows[head, span, :] = query_grad.astype(bf16)
        head_rows[heads + head, span, :] = key_grad.astype(bf16)
        return carry

    for part in up_parts:
        part.start(inner)
    dy_sems = plain_share_z(dy_all)
    q_sems = [gather_start(*part, base) for part, base in zip(q_parts, q_base)]
    for part in up_parts:
        part.start(jnp.logical_and(outer, away))
    for part, sems in zip(q_parts, q_sems):
        gather_forward(*part, sems)
    for part in up_parts:
        part.start(jnp.logical_and(outer, home))
    o_sems = gather_start(*o_part, o_base)
    share_forward(first_all, first_sems)
    net.arrived(ref.far_vectors, vec_sem)
    share_near(first_all, first_sems)
    share_deep(first_all, first_sems)
    qkv_bias = shard_vector(7, home)[:, :qkv_lanes]
    up_bias = shard_vector(6, stay)
    for part, sems in zip(q_parts, q_sems):
        gather_finish(*part, sems)
    for part in down_parts:
        part.start(outer)
    gather_forward(*o_part, o_sems)
    plain_share_x(dy_all, dy_sems)
    for part in up_parts:
        part.beside()
    for part in down_parts:
        part.beside()
    for side_at in range(2):
        side_rows = slice(side_at * pair, (side_at + 1) * pair)
        done = dot_plain(first_all[side_rows, :], attn_w[:, :qkv_lanes])
        done = (done + qkv_bias).astype(bf16)
        for image in range(2):
            to = slice(image * pair + side_at * rows, image * pair + (side_at + 1) * rows)
            for head in range(3 * heads):
                head_rows[head, to, :HD] = done[
                    image * rows : (image + 1) * rows, head * HD : (head + 1) * HD
                ]
    lax.fori_loop(0, 2 * heads, attend, 0, unroll=4)
    pack(mixed_all, ref.mixed_heads, heads, win_shift)
    gather_finish(*o_part, o_sems)
    part_a[half(deep), :] = dot_right_t(mixed_all[half(deep), :], attn_w[:, win:])
    out_sems = sum_deep(0, part_a)
    part_a[half(near), :] = dot_right_t(mixed_all[half(near), :], attn_w[:, win:])
    sum_pass(0, part_a, out_sems)
    sum_near(0, part_a, out_sems)
    up_parts[0].second()
    up_parts[1].second()
    up_parts[0].third()
    attn_rows = sum_finish(0, part_a, out_sems)
    middle = tokens_ref[...].astype(f32) + attn_rows + out_bias
    ref.mid_rows[...] = middle
    normed, hat, inv_scale = norm_rows(middle, second_gain, second_shift)
    second_all[slot(near, kx), :] = normed.astype(bf16)
    ref.second_hat[...] = hat
    ref.row_scale[1] = jnp.broadcast_to(inv_scale, (rows, LANES))
    second_sems = wide_share_start(second_all)
    for part in down_parts:
        part.start(inner)
    up_parts[1].third()
    wide_share_forward(second_all, second_sems)
    down_parts[0].second()
    down_parts[1].second()
    down_parts[2].second()
    plain_share_forward(dy_all, dy_sems)
    up_parts[0].fourth()
    up_parts[1].fourth()
    down_parts[0].third()
    for part in up_parts:
        part.finish()
    wide_share_near(second_all, second_sems)
    raise_half(near)
    down_parts[1].third()
    wide_share_deep(second_all, second_sems)
    raise_half(deep)
    down_parts[2].third()
    down_parts[0].fourth()
    plain_share_finish(dy_all, dy_sems)
    outer_product(down_g, dy_all, hidden_all[:, :main], 0, main)
    down_reduce = wide_reduce_first(down_g, ref.land_d)
    down_parts[1].fourth()
    wide_reduce_second(down_g, ref.land_d, down_reduce)
    down_parts[2].fourth()
    for part in down_parts:
        part.finish()
    up_bias_sum = lower_half(deep)
    part_a[half(deep), :] = dot_right_t(upper_all[half(deep), :], up_w[...])
    second_sum_sems = wide_sum_deep(0, part_a)
    more_sum = lower_half(near)
    vec_own[6:7, :main] = up_bias_sum[0] + more_sum[0]
    vec_own[6:7, main:] = up_bias_sum[1] + more_sum[1]
    part_a[half(near), :] = dot_right_t(upper_all[half(near), :], up_w[...])
    wide_sum_near(0, part_a, second_sum_sems)
    lax.fori_loop(0, D // tile, up_rows, 0, unroll=True)
    up_reduce = wide_reduce_first(up_g, ref.land_u)
    wide_sum_pass(0, part_a, second_sum_sems)
    wide_reduce_second(up_g, ref.land_u, up_reduce)
    wide_reduce_third(down_g, ref.land_d, down_reduce)
    second_grad = wide_sum_finish(0, part_a, second_sum_sems)
    back, gain_sum, shift_sum = norm_back(
        second_grad, ref.second_hat[...], ref.row_scale[1][:, :1], second_gain
    )
    vec_own[3:4, :] = gain_sum[None, :]
    vec_own[4:5, :] = shift_sum[None, :]
    total = cotangent_ref[...].astype(f32) + back
    ref.mid_grad[...] = total
    low = total.astype(bf16)
    mid_all[slot(near, c), :] = low
    vec_own[2:3, :] = jnp.sum(low.astype(f32), axis=0, keepdims=True)
    mid_sems = share_start(mid_all)
    part_b[half(deep), :] = lower_product(deep)
    mlp_sems = wide_sum_deep(1, part_b)
    part_b[half(near), :] = lower_product(near)
    wide_sum_near(1, part_b, mlp_sems)
    share_forward(mid_all, mid_sems)
    wide_reduce_cross(down_g, ref.land_d, down_reduce, when=outer)
    share_near(mid_all, mid_sems)
    wide_reduce_fourth(down_g, ref.land_d, down_reduce, when=outer)
    share_deep(mid_all, mid_sems)
    head_half(0)
    head_half(1)
    wide_reduce_third(up_g, ref.land_u, up_reduce)
    wide_reduce_cross(down_g, ref.land_d, down_reduce, when=inner)
    wide_reduce_fourth(down_g, ref.land_d, down_reduce, when=inner)
    lax.fori_loop(0, 2 * heads, value_back, 0, unroll=2)
    pack(qkv_grads, ref.mixed_heads, heads, 2 * width)
    lax.fori_loop(0, D // tile, value_out_rows, 0)
    vo_args = attn_g, ref.land_vo, cut, all_lanes, net.sems(8)
    reduce_first(*vo_args)
    wide_sum_pass(1, part_b, mlp_sems)
    lax.fori_loop(0, 2 * heads, attend_back, 0, unroll=2)
    wide_reduce_fourth(up_g, ref.land_u, up_reduce, when=outer)
    pack(qkv_grads, head_rows, 2 * heads, 0)
    wide_reduce_cross(up_g, ref.land_u, up_reduce, when=outer)
    part_a[half(deep), :] = dot_right_t(
        qkv_grads[half(deep), :qkv_lanes], attn_w[:, :qkv_lanes]
    )
    first_sum_sems = sum_deep(1, part_a)
    part_a[half(near), :] = dot_right_t(
        qkv_grads[half(near), :qkv_lanes], attn_w[:, :qkv_lanes]
    )
    sum_pass(1, part_a, first_sum_sems)
    sum_near(1, part_a, first_sum_sems)
    vec_own[7:8, :] = jnp.sum(qkv_grads[...].astype(f32), axis=0, keepdims=True)
    outer_product(attn_g, first_all, qkv_grads[:, :cut], 0, cut)
    qk_args = attn_g, ref.land_qk, 0, cut, net.sems(8)
    reduce_first(*qk_args, when=away)
    wide_reduce_fourth(up_g, ref.land_u, up_reduce, when=inner)
    reduce_second(*vo_args)
    wide_reduce_cross(up_g, ref.land_u, up_reduce, when=inner)
    reduce_second(*qk_args, when=away)
    first_grad = sum_finish(1, part_a, first_sum_sems)
    back, gain_sum, shift_sum = norm_back(
        first_grad, ref.first_hat[...], ref.row_scale[0][:, :1], first_gain
    )
    vec_own[0:1, :] = gain_sum[None, :]
    vec_own[1:2, :] = shift_sum[None, :]
    vec_sem = vector_planes()
    ref.mid_grad[...] = ref.mid_grad[...] + back
    store(ref.mid_grad, out.input_grad)
    reduce_first(*qk_args, when=home)
    reduce_third(*vo_args)
    reduce_third(*qk_args, when=away)
    vec_sem = vector_chips(vec_sem)
    vec_sem = vector_core(vec_sem)
    reduce_second(*qk_args, when=home)
    vector_finish(vec_sem)
    store(ref.vec_done, out.vector_grad)
    reduce_third(*qk_args, when=home)
    ref.down_buf[...] = wide_reduce_finish(down_g, ref.land_d, down_reduce)
    store(ref.down_buf, out.down_grad)
    mlp_rows = wide_sum_finish(1, part_b, mlp_sems)
    ref.layer_buf[...] = (ref.mid_rows[...] + mlp_rows + down_bias).astype(bf16)
    store(ref.layer_buf, out.layer_out)
    ref.up_buf[...] = wide_reduce_finish(up_g, ref.land_u, up_reduce)
    store(ref.up_buf, out.up_grad)
    ref.attn_buf[:, cut:] = reduce_finish(ref.land_vo, vo_args[4])
    store(ref.attn_buf.at[:, cut:], out.attn_grad.at[:, cut:])
    ref.attn_buf[:, :cut] = reduce_finish(ref.land_qk, qk_args[4])
    store(ref.attn_buf.at[:, :cut], out.attn_grad.at[:, :cut])
    net.drain()
    assert net.used <= ref.recv_sems.shape[0]
    for copy in stores:
        copy.wait()


def format_kernel(shapes, *refs):
    width, units = shapes
    inputs, refs = refs[:6], refs[6:]
    outs, refs = refs[:17], refs[17:]
    held, refs = refs[:6], refs[6:]
    shaped, sems = refs[:-1], refs[-1]
    copies = [
        pltpu.make_async_copy(source, target, sems.at[number])
        for number, (source, target) in enumerate(zip(inputs, held, strict=True))
    ]
    for copy in copies:
        copy.start()
    going = []

    def put(source, number):
        copy = pltpu.make_async_copy(source, outs[number], sems.at[6 + number])
        copy.start()
        going.append(copy)

    def put_shaped(number, value):
        shaped[number - 2][...] = value
        put(shaped[number - 2], number)

    copies[0].wait()
    put(held[0], 0)
    copies[1].wait()
    put(held[1], 1)
    copies[2].wait()
    for number, place in ((4, 0), (5, 1), (6, 2), (9, 3)):
        put_shaped(number, held[2][:, place * width : (place + 1) * width])
    copies[3].wait()
    put_shaped(13, held[3][:, :units])
    copies[4].wait()
    main = held[4].shape[1]
    shaped[13][:, :main] = held[4][...]
    shaped[13][:, main:] = held[3][:, units : 2 * units - main]
    put(shaped[13], 15)
    copies[5].wait()
    for number, row, lo, size in (
        (2, 0, 0, D),
        (3, 1, 0, D),
        (10, 2, 0, D),
        (11, 3, 0, D),
        (12, 4, 0, D),
        (16, 5, 0, D),
        (14, 6, 0, units),
        (7, 7, 0, width),
        (8, 7, 2 * width, width),
    ):
        put_shaped(number, held[5][row, lo : lo + size])
    for copy in going:
        copy.wait()


def fused_step(
    tokens,
    cotangent,
    first_gain,
    first_shift,
    query_weight,
    key_weight,
    value_weight,
    query_bias,
    value_bias,
    out_weight,
    out_bias,
    second_gain,
    second_shift,
    up_weight,
    up_bias,
    down_weight,
    down_bias,
):
    bf16, f32 = jnp.bfloat16, jnp.float32
    rows, piece, width, units = (
        tokens.shape[0],
        query_weight.shape[0],
        query_weight.shape[1],
        up_weight.shape[1],
    )
    heads = width // HD
    group = 4 * rows
    qkv_lanes = round_up(3 * width, LANES)
    attn_lanes = round_up(4 * width, LANES)
    ff_lanes = round_up(units, LANES)
    main = units // LANES * LANES
    assert 2 * (units - main) <= LANES < ff_lanes - main + 1
    win = 3 * width // LANES * LANES
    given = dict(
        query_w=query_weight,
        key_w=key_weight,
        value_w=value_weight,
        out_w=out_weight.T,
        first_gain=first_gain,
        first_shift=first_shift,
        out_bias=out_bias,
        second_gain=second_gain,
        second_shift=second_shift,
        down_bias=down_bias,
        up_bias=up_bias,
        query_bias=query_bias,
        value_bias=value_bias,
        tokens=tokens,
        cotangent=cotangent,
        up_w=up_weight,
        down_w=down_weight.T,
    )
    place = pl.BlockSpec(memory_space=pl.ANY)
    cut = round_up(2 * width, LANES)
    raw_outs = dict(
        layer_out=jax.ShapeDtypeStruct((rows, D), bf16),
        input_grad=jax.ShapeDtypeStruct((rows, D), f32),
        attn_grad=jax.ShapeDtypeStruct((piece, attn_lanes), f32),
        up_grad=jax.ShapeDtypeStruct((piece, ff_lanes), f32),
        down_grad=jax.ShapeDtypeStruct((piece, main), f32),
        vector_grad=jax.ShapeDtypeStruct((8, D), f32),
    )
    scratch = dict(
        attn_piece=pltpu.VMEM((piece, attn_lanes), bf16),
        up_piece=pltpu.VMEM((piece, ff_lanes), bf16),
        down_piece=pltpu.VMEM((piece, main), bf16),
        up_wait=pltpu.VMEM((piece, ff_lanes), bf16),
        down_wait=pltpu.VMEM((piece, main), bf16),
        attn_w=pltpu.VMEM((D, attn_lanes), bf16),
        up_w=pltpu.VMEM((D, ff_lanes), bf16),
        down_w=pltpu.VMEM((D, main), bf16),
        attn_g=pltpu.VMEM((D, attn_lanes), bf16),
        up_g=pltpu.VMEM((D, ff_lanes), bf16),
        down_g=pltpu.VMEM((D, main), bf16),
        land_vo=pltpu.VMEM((8, piece, attn_lanes - cut), bf16),
        land_qk=pltpu.VMEM((8, piece, cut), bf16),
        land_u=pltpu.VMEM((8, piece, ff_lanes), bf16),
        land_d=pltpu.VMEM((8, piece, main), bf16),
        first_all=pltpu.VMEM((group, D), bf16),
        second_all=pltpu.VMEM((group, D), bf16),
        dy_all=pltpu.VMEM((group, D), bf16),
        mid_all=pltpu.VMEM((group, D), bf16),
        head_rows=pltpu.VMEM((3 * heads, group, LANES), bf16),
        head_grads=pltpu.VMEM((heads, group, LANES), bf16),
        probs_all=pltpu.VMEM((2 * heads, 2 * rows, 2 * rows), f32),
        mixed_heads=pltpu.VMEM((heads, group, LANES), bf16),
        mixed_all=pltpu.VMEM((group, attn_lanes - win), bf16),
        hidden_all=pltpu.VMEM((group, ff_lanes), bf16),
        hidden_rest=pltpu.VMEM((group, LANES), bf16),
        slope_all=pltpu.VMEM((group, ff_lanes), f32),
        upper_all=pltpu.VMEM((group, ff_lanes), bf16),
        qkv_grads=pltpu.VMEM((group, attn_lanes), bf16),
        part_a=pltpu.VMEM((group, D), f32),
        part_b=pltpu.VMEM((group, D), f32),
        core_send=pltpu.VMEM((2, 2, rows, D), bf16),
        core_land=pltpu.VMEM((2, 2, rows, D), bf16),
        deep_send=pltpu.VMEM((2, rows, D), bf16),
        deep_land=pltpu.VMEM((2, rows, D), bf16),
        wide_send=pltpu.VMEM((2, 6, rows // 2, D), bf16),
        wide_land=pltpu.VMEM((2, 6, rows // 2, D), bf16),
        first_hat=pltpu.VMEM((rows, D), f32),
        second_hat=pltpu.VMEM((rows, D), f32),
        mid_rows=pltpu.VMEM((rows, D), f32),
        mid_grad=pltpu.VMEM((rows, D), f32),
        row_scale=pltpu.VMEM((2, rows, LANES), f32),
        vectors=pltpu.VMEM((8, D), f32),
        far_vectors=pltpu.VMEM((8, D), f32),
        vec_own=pltpu.VMEM((8, D), f32),
        by_plane=pltpu.VMEM((4, 8, D), f32),
        vec_chip=pltpu.VMEM((8, D), f32),
        by_chip=pltpu.VMEM((4, 8, D), f32),
        vec_core=pltpu.VMEM((8, D), f32),
        vec_core_land=pltpu.VMEM((8, D), f32),
        vec_done=pltpu.VMEM((8, D), f32),
        layer_buf=pltpu.VMEM((rows, D), bf16),
        attn_buf=pltpu.VMEM((piece, attn_lanes), f32),
        up_buf=pltpu.VMEM((piece, ff_lanes), f32),
        down_buf=pltpu.VMEM((piece, main), f32),
        load_sems=pltpu.SemaphoreType.DMA((len(given) + len(raw_outs) + 1,)),
        send_sems=pltpu.SemaphoreType.DMA((64,)),
        recv_sems=pltpu.SemaphoreType.DMA((112,)),
    )
    shapes = (rows, heads, width, units, qkv_lanes, piece)
    names = tuple(given), tuple(raw_outs), tuple(scratch)

    def body(*refs):
        layer_kernel(shapes, names, *refs)

    raw = pl.pallas_call(
        body,
        out_shape=tuple(raw_outs.values()),
        in_specs=[place] * len(given),
        out_specs=(place,) * len(raw_outs),
        scratch_shapes=[
            *(pltpu.VMEM(array.shape, array.dtype) for array in given.values()),
            *scratch.values(),
        ],
        compiler_params=pltpu.CompilerParams(
            collective_id=0, has_side_effects=True, vmem_limit_bytes=67043328
        ),
        name="layer",
    )(*given.values())
    raw_outs = tuple(raw_outs.values())

    vector, narrow = jax.ShapeDtypeStruct((D,), f32), jax.ShapeDtypeStruct((width,), f32)
    attn_out = jax.ShapeDtypeStruct((piece, width), f32)
    ff_out = jax.ShapeDtypeStruct((piece, units), f32)
    outs = (
        *raw_outs[:2],
        vector,
        vector,
        attn_out,
        attn_out,
        attn_out,
        narrow,
        narrow,
        attn_out,
        vector,
        vector,
        vector,
        ff_out,
        jax.ShapeDtypeStruct((units,), f32),
        ff_out,
        vector,
    )

    def format_body(*refs):
        format_kernel((width, units), *refs)

    done = pl.pallas_call(
        format_body,
        out_shape=outs,
        in_specs=[place] * 6,
        out_specs=(place,) * 17,
        scratch_shapes=[
            *(pltpu.VMEM(item.shape, item.dtype) for item in raw_outs),
            *(pltpu.VMEM(item.shape, item.dtype) for item in outs[2:]),
            pltpu.SemaphoreType.DMA((6 + 17,)),
        ],
        compiler_params=pltpu.CompilerParams(vmem_limit_bytes=67043328),
        name="outputs",
    )(*raw)
    done = list(done)
    done[9], done[15] = done[9].T, done[15].T
    return tuple(done)


def pick_step(mesh):
    if mesh.shape["fsdp"] == 8 and mesh.shape["tensor"] == 4:
        return fused_step
    return on_device


def solution(mesh):
    return jax.shard_map(
        pick_step(mesh),
        mesh=mesh,
        in_specs=(
            P(("fsdp", "tensor"), None),
            P(("fsdp", "tensor"), None),
            P(),
            P(),
            P("fsdp", "tensor"),
            P("fsdp", "tensor"),
            P("fsdp", "tensor"),
            P("tensor"),
            P("tensor"),
            P("tensor", "fsdp"),
            P(),
            P(),
            P(),
            P("fsdp", "tensor"),
            P("tensor"),
            P("tensor", "fsdp"),
            P(),
        ),
        out_specs=(
            P(("fsdp", "tensor"), None),
            P(("fsdp", "tensor"), None),
            P(),
            P(),
            P("fsdp", "tensor"),
            P("fsdp", "tensor"),
            P("fsdp", "tensor"),
            P("tensor"),
            P("tensor"),
            P("tensor", "fsdp"),
            P(),
            P(),
            P(),
            P("fsdp", "tensor"),
            P("tensor"),
            P("tensor", "fsdp"),
            P(),
        ),
        check_vma=False,
    )
```

```python
import math
from types import SimpleNamespace

import jax
import jax.numpy as jnp
from jax import lax
from jax.experimental import pallas as pl
from jax.experimental.pallas import tpu as pltpu
from jax.sharding import PartitionSpec as P

D = 1152
HD = 72
FF = 4304
SEQ = 256


norm_eps = 1e-06
gelu_coef = 0.7978845608028654
cubic_coef = 0.044715


def dot_plain(left, right):
    return jnp.dot(left, right, preferred_element_type=jnp.float32)


def dot_right_t(left, right):
    return lax.dot_general(
        left, right, (((1,), (1,)), ((), ())), preferred_element_type=jnp.float32
    )


def dot_left_t(left, right):
    return lax.dot_general(
        left, right, (((0,), (0,)), ((), ())), preferred_element_type=jnp.float32
    )


def norm_rows(values, gain, shift):
    row_mean = jnp.mean(values, axis=1, keepdims=True)
    centred = values - row_mean
    inv_scale = lax.rsqrt(jnp.mean(centred * centred, axis=1, keepdims=True) + norm_eps)
    normed = centred * inv_scale
    return (normed * gain + shift, normed, inv_scale)


def norm_back(out_grad, normed, inv_scale, gain):
    scaled_grad = out_grad * gain
    grad_mean = jnp.mean(scaled_grad, axis=1, keepdims=True)
    cross_mean = jnp.mean(scaled_grad * normed, axis=1, keepdims=True)
    in_grad = inv_scale * (scaled_grad - grad_mean - normed * cross_mean)
    return (in_grad, jnp.sum(out_grad * normed, axis=0), jnp.sum(out_grad, axis=0))


def gelu_pair(upper):
    tangent = jnp.tanh(gelu_coef * (upper + cubic_coef * upper * upper * upper))
    gelu_value = 0.5 * upper * (1.0 + tangent)
    gelu_slope = 0.5 * (1.0 + tangent) + 0.5 * upper * (1.0 - tangent * tangent) * gelu_coef * (
        1.0 + 3.0 * cubic_coef * upper * upper
    )
    return (gelu_value, gelu_slope)


def split_heads(block_rows, head_count):
    col_width = block_rows.shape[1] // 3
    img_count = block_rows.shape[0] // SEQ
    shape_four = (img_count, SEQ, head_count, HD)
    queries = block_rows[:, :col_width].reshape(shape_four)
    keys_part = block_rows[:, col_width : 2 * col_width].reshape(shape_four)
    values = block_rows[:, 2 * col_width :].reshape(shape_four)
    return (queries, keys_part, values, shape_four)


def attend_forward(block_rows, head_count):
    queries, keys_part, values, shape_four = split_heads(block_rows, head_count)
    scores = jnp.einsum(
        "nqhd,nkhd->nhqk", queries, keys_part, preferred_element_type=jnp.float32
    ) * HD ** (-0.5)
    peak = jnp.max(scores, axis=-1, keepdims=True)
    expo = jnp.exp(scores - peak)
    totals = jnp.sum(expo, axis=-1, keepdims=True)
    prob_low = (expo / totals).astype(jnp.bfloat16)
    mixed = jnp.einsum("nhqk,nkhd->nqhd", prob_low, values, preferred_element_type=jnp.float32)
    row_total = block_rows.shape[0]
    mixed = mixed.reshape(row_total, head_count * HD).astype(jnp.bfloat16)
    return (mixed, (peak + jnp.log(totals))[..., 0])


def attend_backward(inputs, head_count):
    block_rows, grad_block, log_total = inputs
    queries, keys_part, values, shape_four = split_heads(block_rows, head_count)
    grad_out = grad_block.reshape(shape_four)
    scores = jnp.einsum(
        "nqhd,nkhd->nhqk", queries, keys_part, preferred_element_type=jnp.float32
    ) * HD ** (-0.5)
    probs = jnp.exp(scores - log_total[..., None])
    prob_low = probs.astype(jnp.bfloat16)
    value_grad = jnp.einsum(
        "nhqk,nqhd->nkhd", prob_low, grad_out, preferred_element_type=jnp.float32
    )
    prob_grad = jnp.einsum("nqhd,nkhd->nhqk", grad_out, values, preferred_element_type=jnp.float32)
    row_dot = jnp.sum(probs * prob_grad, axis=-1, keepdims=True)
    score_grad = (probs * (prob_grad - row_dot)).astype(jnp.bfloat16)
    query_grad = jnp.einsum(
        "nhqk,nkhd->nqhd", score_grad, keys_part, preferred_element_type=jnp.float32
    ) * HD ** (-0.5)
    key_grad = jnp.einsum(
        "nhqk,nqhd->nkhd", score_grad, queries, preferred_element_type=jnp.float32
    ) * HD ** (-0.5)
    row_total = block_rows.shape[0]
    col_width = head_count * HD
    return jnp.concatenate(
        (
            query_grad.reshape(row_total, col_width),
            key_grad.reshape(row_total, col_width),
            value_grad.reshape(row_total, col_width),
        ),
        axis=1,
    ).astype(jnp.bfloat16)


def on_device(
    tokens,
    cotangent,
    first_gain,
    first_shift,
    query_weight,
    key_weight,
    value_weight,
    query_bias,
    value_bias,
    out_weight,
    out_bias,
    second_gain,
    second_shift,
    up_weight,
    up_bias,
    down_weight,
    down_bias,
):
    full_query, full_key, full_value, full_outp, full_up, full_down = (
        lax.all_gather(query_weight, "fsdp", axis=0, tiled=True),
        lax.all_gather(key_weight, "fsdp", axis=0, tiled=True),
        lax.all_gather(value_weight, "fsdp", axis=0, tiled=True),
        lax.all_gather(out_weight, "fsdp", axis=1, tiled=True),
        lax.all_gather(up_weight, "fsdp", axis=0, tiled=True),
        lax.all_gather(down_weight, "fsdp", axis=1, tiled=True),
    )
    qkv_weight = jnp.concatenate((full_query, full_key, full_value), axis=1)
    local_width = full_query.shape[1]
    ffn_width = full_up.shape[1]
    head_count = local_width // HD
    token_rows = tokens.astype(jnp.float32)
    first_out, first_hat, first_scale = norm_rows(token_rows, first_gain, first_shift)
    all_first = lax.all_gather(first_out.astype(jnp.bfloat16), "tensor", axis=0, tiled=True)
    qkv_bias = jnp.concatenate((query_bias, jnp.zeros_like(query_bias), value_bias))
    qkv_rows = (dot_plain(all_first, qkv_weight) + qkv_bias).astype(jnp.bfloat16)
    group_rows = qkv_rows.shape[0]
    images = group_rows // SEQ
    per_block = math.gcd(images, max(1, 512 // SEQ))
    blocks = images // per_block
    stacked = qkv_rows.reshape(blocks, per_block * SEQ, 3 * local_width)

    def forward_block(block_rows):
        return attend_forward(block_rows, head_count)

    head_out, log_total = lax.map(forward_block, stacked)
    head_out = head_out.reshape(group_rows, local_width)
    attn_rows = lax.psum_scatter(
        dot_plain(head_out, full_outp), "tensor", scatter_dimension=0, tiled=True
    )
    mid_rows = token_rows + attn_rows + out_bias
    second_out, second_hat, second_scale = norm_rows(mid_rows, second_gain, second_shift)
    all_second = lax.all_gather(second_out.astype(jnp.bfloat16), "tensor", axis=0, tiled=True)
    up_pre = dot_plain(all_second, full_up) + up_bias
    hidden_value, hidden_slope = gelu_pair(up_pre)
    hidden_low = hidden_value.astype(jnp.bfloat16)
    mlp_rows = lax.psum_scatter(
        dot_plain(hidden_low, full_down).astype(jnp.bfloat16),
        "tensor",
        scatter_dimension=0,
        tiled=True,
    ).astype(jnp.float32)
    layer_out = (mid_rows + mlp_rows + down_bias).astype(jnp.bfloat16)
    out_grad = cotangent.astype(jnp.float32)
    all_out_grad = lax.all_gather(cotangent, "tensor", axis=0, tiled=True)
    down_grad = dot_left_t(hidden_low, all_out_grad)
    hidden_grad = dot_right_t(all_out_grad, full_down)
    upper_low = (hidden_grad * hidden_slope).astype(jnp.bfloat16)
    up_bias_grad = jnp.sum(upper_low.astype(jnp.float32), axis=0)
    up_grad = dot_left_t(all_second, upper_low)
    second_grad = lax.psum_scatter(
        dot_right_t(upper_low, full_up), "tensor", scatter_dimension=0, tiled=True
    )
    back_second, second_gain_grad, second_shift_grad = norm_back(
        second_grad, second_hat, second_scale, second_gain
    )
    mid_grad = out_grad + back_second
    mid_low = mid_grad.astype(jnp.bfloat16)
    all_mid_grad = lax.all_gather(mid_low, "tensor", axis=0, tiled=True)
    outp_grad = dot_left_t(head_out, all_mid_grad)
    head_grad = dot_right_t(all_mid_grad, full_outp).astype(jnp.bfloat16)

    def backward_block(inputs):
        return attend_backward(inputs, head_count)

    qkv_grad = lax.map(
        backward_block,
        (stacked, head_grad.reshape(blocks, per_block * SEQ, local_width), log_total),
    )
    qkv_grad = qkv_grad.reshape(group_rows, 3 * local_width)
    qkv_weight_grad = dot_left_t(all_first, qkv_grad)
    qkv_bias_grad = jnp.sum(qkv_grad.astype(jnp.float32), axis=0)
    first_grad = lax.psum_scatter(
        dot_right_t(qkv_grad, qkv_weight).astype(jnp.bfloat16),
        "tensor",
        scatter_dimension=0,
        tiled=True,
    ).astype(jnp.float32)
    back_first, first_gain_grad, first_shift_grad = norm_back(
        first_grad, first_hat, first_scale, first_gain
    )
    input_grad = mid_grad + back_first
    out_bias_grad = jnp.sum(mid_low.astype(jnp.float32), axis=0)
    down_bias_grad = jnp.sum(out_grad, axis=0)
    small_terms = jnp.concatenate(
        (
            first_gain_grad,
            first_shift_grad,
            out_bias_grad,
            second_gain_grad,
            second_shift_grad,
            down_bias_grad,
        )
    )
    tensor_index = lax.axis_index("tensor")
    head_terms = jnp.zeros((2 * D + FF,), jnp.float32)
    head_terms = lax.dynamic_update_slice(
        head_terms, qkv_bias_grad[:local_width], (tensor_index * local_width,)
    )
    head_terms = lax.dynamic_update_slice(
        head_terms, qkv_bias_grad[2 * local_width :], (D + tensor_index * local_width,)
    )
    head_terms = lax.dynamic_update_slice(
        head_terms, up_bias_grad, (2 * D + tensor_index * ffn_width,)
    )
    small_sums, head_sums = lax.psum((small_terms, head_terms), ("fsdp", "tensor"))
    query_bias_total = lax.dynamic_slice(head_sums, (tensor_index * local_width,), (local_width,))
    value_bias_total = lax.dynamic_slice(
        head_sums, (D + tensor_index * local_width,), (local_width,)
    )
    up_bias_total = lax.dynamic_slice(head_sums, (2 * D + tensor_index * ffn_width,), (ffn_width,))
    query_part, key_part, value_part, outp_part, up_part, down_part = (
        lax.psum_scatter(qkv_weight_grad[:, :local_width], "fsdp", scatter_dimension=0, tiled=True),
        lax.psum_scatter(
            qkv_weight_grad[:, local_width : 2 * local_width],
            "fsdp",
            scatter_dimension=0,
            tiled=True,
        ),
        lax.psum_scatter(
            qkv_weight_grad[:, 2 * local_width :], "fsdp", scatter_dimension=0, tiled=True
        ),
        lax.psum_scatter(outp_grad, "fsdp", scatter_dimension=1, tiled=True),
        lax.psum_scatter(up_grad, "fsdp", scatter_dimension=0, tiled=True),
        lax.psum_scatter(down_grad, "fsdp", scatter_dimension=1, tiled=True),
    )
    return (
        layer_out,
        input_grad,
        small_sums[0:D],
        small_sums[D : 2 * D],
        query_part,
        key_part,
        value_part,
        query_bias_total,
        value_bias_total,
        outp_part,
        small_sums[2 * D : 3 * D],
        small_sums[3 * D : 4 * D],
        small_sums[4 * D : 5 * D],
        up_part,
        up_bias_total,
        down_part,
        small_sums[5 * D : 6 * D],
    )


MESH_IDS = pl.DeviceIdType.MESH
LANES = 128


def round_up(value, step):
    return -(-value // step) * step


def row_cuts(count, parts):
    edges = [min(count, round_up(count * at // parts, 16)) for at in range(parts + 1)]
    return list(zip(edges[:-1], edges[1:]))


class Remote:
    def __init__(self, send_sems, recv_sems):
        self.send_sems, self.recv_sems = send_sems, recv_sems
        self.used = 0
        self.sent = 0
        self.slots = [None] * send_sems.shape[0]

    def sem(self):
        self.used += 1
        return self.used - 1

    def sems(self, count):
        return [self.sem() for _ in range(count)]

    def release(self, slot):
        if self.slots[slot] is not None:
            copy, when = self.slots[slot]
            guarded(when, copy.wait_send)

    def send(self, src, dst, device, recv, when=None):
        slot = self.sent % len(self.slots)
        self.sent += 1
        self.release(slot)
        copy = pltpu.make_async_remote_copy(
            src_ref=src,
            dst_ref=dst,
            send_sem=self.send_sems.at[slot],
            recv_sem=self.recv_sems.at[recv],
            device_id=device,
            device_id_type=MESH_IDS,
        )
        guarded(when, copy.start)
        self.slots[slot] = copy, when

    def local(self, src, dst, sem, when):
        copy = pltpu.make_async_copy(src, dst, self.recv_sems.at[sem])
        guarded(when, copy.start)

    def arrived(self, dst, sem):
        pltpu.make_async_copy(dst, dst, self.recv_sems.at[sem]).wait()

    def drain(self):
        for slot in range(len(self.slots)):
            self.release(slot)


def guarded(when, action):
    if when is None:
        action()
    else:
        pl.when(when)(action)


def layer_kernel(shapes, names, *refs):
    rows, heads, width, units, qkv_lanes, piece = shapes
    inputs, outputs, scratch = names
    hbm = SimpleNamespace(**dict(zip(inputs, refs[: len(inputs)], strict=True)))
    refs = refs[len(inputs) :]
    out = SimpleNamespace(**dict(zip(outputs, refs[: len(outputs)], strict=True)))
    refs = refs[len(outputs) :]
    held = SimpleNamespace(**dict(zip(inputs, refs[: len(inputs)], strict=True)))
    refs = refs[len(inputs) :]
    ref = SimpleNamespace(**dict(zip(scratch, refs, strict=True)))
    bf16, f32 = jnp.bfloat16, jnp.float32
    attn_w, up_w, down_w = ref.attn_w, ref.up_w, ref.down_w
    attn_g, up_g, down_g = ref.attn_g, ref.up_g, ref.down_g
    first_all, second_all = ref.first_all, ref.second_all
    dy_all, mid_all = ref.dy_all, ref.mid_all
    head_rows, head_grads = ref.head_rows, ref.head_grads
    mixed_all, hidden_all, upper_all = ref.mixed_all, ref.hidden_all, ref.upper_all
    slope_all, qkv_grads = ref.slope_all, ref.qkv_grads
    part_a, part_b, vectors = ref.part_a, ref.part_b, ref.vectors
    pair, fourth = 2 * rows, rows // 2
    out_base = 3 * width
    win = out_base // LANES * LANES
    win_shift = out_base - win
    skip = qkv_lanes - win
    all_lanes, ff_lanes = attn_w.shape[1], up_w.shape[1]
    main = units // LANES * LANES
    rest = units - main

    f = lax.axis_index("fsdp")
    t = lax.axis_index("tensor")
    c, k = lax.rem(f, 2), lax.div(f, 2)
    kx, ky = lax.rem(k, 2), lax.div(k, 2)
    zl, zh = lax.rem(t, 2), lax.div(t, 2)
    oc, ox = 1 - c, 1 - kx
    k_x, k_y, k_d = ky * 2 + ox, (1 - ky) * 2 + kx, (1 - ky) * 2 + ox
    home = c == zh
    away = jnp.logical_not(home)
    stay = kx == zh
    outer = zl == zh
    inner = jnp.logical_not(outer)
    move = jnp.logical_not(stay)
    far_t = (1 - zh) * 2 + zl
    dev_x = {"fsdp": 2 * k_x + c, "tensor": t}
    dev_y = {"fsdp": 2 * k_y + c, "tensor": t}
    dev_c = {"fsdp": 2 * k + oc, "tensor": t}
    dev_z = {"fsdp": f, "tensor": zh * 2 + (1 - zl)}
    dev_far = {"fsdp": f, "tensor": far_t}
    dev_far_other = {"fsdp": 2 * k + oc, "tensor": far_t}
    net = Remote(ref.send_sems, ref.recv_sems)

    def aligned(start, size):
        return pl.ds(pl.multiple_of(start, math.gcd(size, LANES)), size)

    def piece_at(index):
        return pl.ds(pl.multiple_of(index * piece, piece), piece)

    def block(buf, index, lo=0, hi=None):
        return buf.at[piece_at(index), lo : buf.shape[1] if hi is None else hi]

    near, deep = zl * pair, (1 - zl) * pair

    def slot(side, place):
        return aligned(side + place * rows, rows)

    def spread_start(src, buf, lo, hi):
        base, _ = net.sems(2)
        source, target = src.at[:, lo:hi], block(buf, f, lo, hi)
        net.local(source, target, base + c, home)
        to = {"fsdp": 2 * k + zh, "tensor": t}
        net.send(source, target, to, base + c, when=away)
        to = {"fsdp": 2 * k + zh, "tensor": far_t}
        net.send(source, target, to, base + c)
        return base

    def gather_start(buf, lo, hi, base):
        sems = net.sems(3)
        a_own, b_own = block(buf, 2 * k, lo, hi), block(buf, 2 * k + 1, lo, hi)
        net.arrived(a_own, base)
        net.send(a_own, a_own, dev_x, sems[0])
        net.arrived(b_own, base + 1)
        net.send(b_own, b_own, dev_y, sems[1])
        net.send(a_own, a_own, dev_y, sems[2])
        net.send(b_own, b_own, dev_x, sems[2])
        return sems

    def gather_forward(buf, lo, hi, sems):
        a_x, b_y = block(buf, 2 * k_x, lo, hi), block(buf, 2 * k_y + 1, lo, hi)
        net.arrived(a_x, sems[0])
        net.send(a_x, a_x, dev_y, sems[2])
        net.arrived(b_y, sems[1])
        net.send(b_y, b_y, dev_x, sems[2])

    def gather_finish(buf, lo, hi, sems):
        net.arrived(buf.at[0 : 4 * piece, lo:hi], sems[2])

    f_x, f_y, f_d = 2 * k_x + c, 2 * k_y + c, 2 * k_d + c

    class WideGather:
        def __init__(self, src, buf, wait_at, lo, hi):
            self.buf, self.lo, self.size = buf, lo, hi - lo
            self.src, self.wait_at = src.at[lo:hi, :], wait_at.at[lo:hi, :]
            self.sems = net.sems(6)

        def at(self, index):
            start = pl.multiple_of(index * piece + self.lo, 16)
            return self.buf.at[pl.ds(start, self.size), :]

        def start(self, when):
            own, sems = self.at(f), self.sems
            stay_now, move_now = jnp.logical_and(stay, when), jnp.logical_and(move, when)
            net.local(self.src, own, sems[4], stay_now)
            net.send(self.src, own, dev_far, sems[0], when=stay_now)
            net.send(self.src, self.wait_at, dev_far, sems[0], when=move_now)

        def beside(self):
            net.send(self.src, self.at(f), dev_x, self.sems[1], when=move)

        def second(self):
            own, sems = self.at(f), self.sems

            @pl.when(stay)
            def _():
                net.arrived(self.wait_at, sems[0])

            @pl.when(move)
            def _():
                net.arrived(own, sems[0])

            net.send(self.wait_at, own, dev_x, sems[1], when=stay)

            @pl.when(stay)
            def _():
                net.arrived(own, sems[4])

            net.send(own, own, dev_y, sems[2])
            net.send(own, own, dev_c, sems[3])

        def third(self):
            got = self.at(f_x)
            net.arrived(got, self.sems[1])
            net.send(got, got, dev_y, self.sems[5])
            net.send(got, got, dev_c, self.sems[3])

        def fourth(self):
            for index, sem in ((f_y, 2), (f_d, 5)):
                got = self.at(index)
                net.arrived(got, self.sems[sem])
                net.send(got, got, dev_c, self.sems[3])

        def finish(self):
            net.arrived(self.buf.at[0 : 4 * self.size, :], self.sems[3])

    def share_start(buf):
        sems = net.sems(3)
        own = buf.at[slot(near, c)]
        net.send(own, own, dev_z, sems[0])
        net.send(own, own, dev_c, sems[1])
        return sems

    def share_near(buf, sems):
        net.arrived(buf.at[slot(near, oc)], sems[1])

    def share_forward(buf, sems):
        got = buf.at[slot(deep, c)]
        net.arrived(got, sems[0])
        net.send(got, got, dev_c, sems[2])

    def share_deep(buf, sems):
        net.arrived(buf.at[slot(deep, oc)], sems[2])

    def sum_deep(which, part):
        sems = net.sems(3)
        send = ref.core_send.at[which, 0]
        send[...] = part[slot(deep, oc), :].astype(bf16)
        net.send(send, ref.core_land.at[which, 0], dev_c, sems[0])
        return sems

    def sum_pass(which, part, sems):
        land, send = ref.core_land.at[which, 0], ref.deep_send.at[which]
        net.arrived(land, sems[0])
        send[...] = (part[slot(deep, c), :] + land[...].astype(f32)).astype(bf16)
        net.send(send, ref.deep_land.at[which], dev_z, sems[1])

    def sum_near(which, part, sems):
        send = ref.core_send.at[which, 1]
        send[...] = part[slot(near, oc), :].astype(bf16)
        net.send(send, ref.core_land.at[which, 1], dev_c, sems[2])

    def sum_finish(which, part, sems):
        beside, across = ref.core_land.at[which, 1], ref.deep_land.at[which]
        net.arrived(beside, sems[2])
        total = part[slot(near, c), :] + beside[...].astype(f32)
        net.arrived(across, sems[1])
        return total + across[...].astype(f32)

    def quarter(side, place, which):
        return aligned(side + place * rows + which * fourth, fourth)

    def wide_share_start(buf):
        sems = net.sems(4)
        first, second = buf.at[quarter(near, kx, 0)], buf.at[quarter(near, kx, 1)]
        net.send(first, first, dev_z, sems[0])
        net.send(second, second, dev_x, sems[1])
        net.send(second, second, dev_z, sems[3])
        net.send(first, first, dev_x, sems[2])
        return sems

    def wide_share_forward(buf, sems):
        from_z, from_x = buf.at[quarter(deep, kx, 0)], buf.at[quarter(near, ox, 1)]
        net.arrived(from_z, sems[0])
        net.send(from_z, from_z, dev_x, sems[3])
        net.arrived(from_x, sems[1])
        net.send(from_x, from_x, dev_z, sems[3])

    def wide_share_near(buf, sems):
        net.arrived(buf.at[quarter(near, ox, 0)], sems[2])

    def wide_share_deep(buf, sems):
        net.arrived(buf.at[0 : 3 * fourth, :], sems[3])

    def plain_share_z(buf):
        sems = net.sems(3)
        own = buf.at[slot(near, kx)]
        net.send(own, own, dev_z, sems[0])
        return sems

    def plain_share_x(buf, sems):
        own = buf.at[slot(near, kx)]
        net.send(own, own, dev_x, sems[1])

    def plain_share_forward(buf, sems):
        got = buf.at[slot(near, ox)]
        net.arrived(got, sems[1])
        net.send(got, got, dev_z, sems[2])

    def plain_share_finish(buf, sems):
        net.arrived(buf.at[slot(deep, kx)], sems[0])
        net.arrived(buf.at[slot(deep, ox)], sems[2])

    def wide_send(which, number):
        return ref.wide_send.at[which, number]

    def wide_land(which, number):
        return ref.wide_land.at[which, number]

    def wide_push(which, number, value, device, sem):
        wide_send(which, number)[...] = value.astype(bf16)
        net.send(wide_send(which, number), wide_land(which, number), device, sem)

    def wide_sum_deep(which, part):
        sems = net.sems(6)
        wide_push(which, 0, part[quarter(deep, ox, 0), :], dev_x, sems[0])
        wide_push(which, 1, part[quarter(deep, ox, 1), :], dev_z, sems[1])
        wide_push(which, 2, part[quarter(deep, kx, 1), :], dev_z, sems[2])
        return sems

    def wide_sum_near(which, part, sems):
        wide_push(which, 3, part[quarter(near, ox, 0), :], dev_x, sems[3])

    def wide_sum_pass(which, part, sems):
        net.arrived(wide_land(which, 0), sems[0])
        total = part[quarter(deep, kx, 0), :] + wide_land(which, 0)[...].astype(f32)
        wide_push(which, 4, total, dev_z, sems[4])
        net.arrived(wide_land(which, 1), sems[1])
        total = part[quarter(near, ox, 1), :] + wide_land(which, 1)[...].astype(f32)
        wide_push(which, 5, total, dev_x, sems[5])

    def wide_sum_finish(which, part, sems):
        halves = []
        for half_at, (by_z, by_x) in enumerate(((4, 3), (2, 5))):
            net.arrived(wide_land(which, by_z), sems[by_z])
            net.arrived(wide_land(which, by_x), sems[by_x])
            halves.append(
                part[quarter(near, kx, half_at), :]
                + wide_land(which, by_z)[...].astype(f32)
                + wide_land(which, by_x)[...].astype(f32)
            )
        return jnp.concatenate(halves, axis=0)

    def add_into(grad, index, lo, hi, land):
        at = piece_at(index)
        total = grad[at, lo:hi].astype(f32) + land[...].astype(f32)
        grad[at, lo:hi] = total.astype(bf16)

    def reduce_route(core, by_y):
        if core == 0 or by_y:
            return dev_y, 2 * k_y + core, 2 * k_x + core, dev_x
        return dev_x, 2 * k_x + core, 2 * k_y + core, dev_y

    def reduce_first(grad, land, lo, hi, sems, by_y=False, when=None):
        for distant in (True, False):
            for core in range(2):
                device, index, _, _ = reduce_route(core, by_y)
                index, number = (2 * k_d + core, 1 + 2 * core) if distant else (index, 2 * core)
                source = block(grad, index, lo, hi)
                net.send(source, land.at[number], device, sems[number], when=when)

    def reduce_second(grad, land, lo, hi, sems, by_y=False, when=None):
        def collect(index, number):
            def action():
                net.arrived(land.at[number], sems[number])
                add_into(grad, index, lo, hi, land.at[number])

            guarded(when, action)

        for core in range(2):
            _, _, index, device = reduce_route(core, by_y)
            collect(index, 1 + 2 * core)
            source = block(grad, index, lo, hi)
            net.send(source, land.at[4 + core], device, sems[4 + core], when=when)
        for core in range(2):
            collect(2 * k + core, 2 * core)

    def reduce_third(grad, land, lo, hi, sems, when=None):
        def here(condition):
            return condition if when is None else jnp.logical_and(when, condition)

        for core in range(2):

            def collect(core=core):
                net.arrived(land.at[4 + core], sems[4 + core])
                add_into(grad, 2 * k + core, lo, hi, land.at[4 + core])

            guarded(when, collect)
            source = block(grad, 2 * k + core, lo, hi)
            mine, other = jnp.logical_and(home, c == core), jnp.logical_and(home, c != core)
            net.local(source, land.at[6], sems[6], here(mine))
            to = {"fsdp": 2 * k + core, "tensor": t}
            net.send(source, land.at[6], to, sems[6], when=here(other))
            to = {"fsdp": 2 * k + core, "tensor": far_t}
            net.send(source, land.at[7], to, sems[7], when=here(away))

    def reduce_finish(land, sems):
        net.arrived(land.at[6], sems[6])
        net.arrived(land.at[7], sems[7])
        return land[6].astype(f32) + land[7].astype(f32)

    def wide_reduce_first(grad, land):
        sems = net.sems(6)
        for number, index in enumerate((f_d, f_y, f, f_x)):
            sem = sems[0] if number < 2 else sems[1]
            net.send(block(grad, index + oc - c), land.at[number], dev_c, sem)
        return sems

    def wide_reduce_second(grad, land, sems):
        net.arrived(land.at[0:2], sems[0])
        for number, index in enumerate((f_d, f_y)):
            add_into(grad, index, 0, grad.shape[1], land.at[number])
            net.send(block(grad, index), land.at[4 + number], dev_y, sems[4 + number])
        net.arrived(land.at[2:4], sems[1])
        for number, index in ((2, f), (3, f_x)):
            add_into(grad, index, 0, grad.shape[1], land.at[number])

    def wide_reduce_third(grad, land, sems):
        net.arrived(land.at[4], sems[4])
        add_into(grad, f_x, 0, grad.shape[1], land.at[4])
        net.send(block(grad, f_x), land.at[6], dev_x, sems[2])
        net.arrived(land.at[5], sems[5])
        add_into(grad, f, 0, grad.shape[1], land.at[5])

    def wide_reduce_cross(grad, land, sems, when):
        now = jnp.logical_and(move, when)
        net.send(block(grad, f), land.at[7], dev_far, sems[3], when=now)

    def wide_reduce_fourth(grad, land, sems, when):
        guarded(when, lambda: net.arrived(land.at[6], sems[2]))
        now = jnp.logical_and(stay, when)
        net.send(land.at[6], land.at[7], dev_far, sems[3], when=now)

    def wide_reduce_finish(grad, land, sems):
        kept = jnp.where(stay, grad[piece_at(f), :].astype(f32), land[6].astype(f32))
        net.arrived(land.at[7], sems[3])
        return kept + land[7].astype(f32)

    vec_own, by_plane, by_chip = ref.vec_own, ref.by_plane, ref.by_chip
    plane_peers = [lax.rem(t + step, 4) for step in range(1, 4)]
    chip_peers = [lax.rem(k + step, 4) for step in range(1, 4)]

    def vector_planes():
        by_plane[t] = vec_own[...]
        sem = net.sem()
        for plane in plane_peers:
            net.send(vec_own, by_plane.at[t], {"fsdp": f, "tensor": plane}, sem)
        return sem

    def vector_chips(sem):
        net.arrived(by_plane.at[0:3], sem)
        both = ref.vec_chip
        total = by_plane[0] + by_plane[1] + by_plane[2] + by_plane[3]
        shard = by_plane[zl] + by_plane[2 + zl]
        both[0:6, :] = total[0:6, :]
        both[6:8, :] = shard[6:8, :]
        by_chip[k] = both[...]
        sem = net.sem()
        for chip in chip_peers:
            net.send(both, by_chip.at[k], {"fsdp": 2 * chip + c, "tensor": t}, sem)
        return sem

    def vector_core(sem):
        net.arrived(by_chip.at[0:3], sem)
        held = ref.vec_core
        total = by_chip[0] + by_chip[1] + by_chip[2] + by_chip[3]
        units_total = by_chip[zh] + by_chip[2 + zh]
        held[0:6, :] = total[0:6, :]
        held[6:7, :] = units_total[6:7, :]
        held[7:8, :] = total[7:8, :]
        sem = net.sem()
        net.send(held, ref.vec_core_land, dev_c, sem)
        return sem

    def vector_finish(sem):
        held, land, done = ref.vec_core, ref.vec_core_land, ref.vec_done
        net.arrived(land, sem)
        done[0:7, :] = held[0:7, :] + land[0:7, :]
        done[7:8, :] = jnp.where(home, held[7:8, :], land[7:8, :])

    barrier = pltpu.get_barrier_semaphore()
    peers = (dev_x, dev_y, dev_c, dev_z, dev_far, dev_far_other)
    for peer in peers:
        pl.semaphore_signal(barrier, inc=1, device_id=peer, device_id_type=MESH_IDS)

    coming = {}
    for number, name in enumerate(inputs):
        copy = pltpu.make_async_copy(
            getattr(hbm, name), getattr(held, name), ref.load_sems.at[number]
        )
        copy.start()
        coming[name] = copy
    coming = SimpleNamespace(**coming)
    stores = []

    def store(source, target):
        sem = ref.load_sems.at[len(inputs) + len(stores)]
        copy = pltpu.make_async_copy(source, target, sem)
        copy.start()
        stores.append(copy)

    attn_piece = ref.attn_piece
    if all_lanes > 4 * width:
        attn_piece[:, 4 * width :] = jnp.zeros((piece, all_lanes - 4 * width), bf16)
    for number, (copy, raw) in enumerate(
        (
            (coming.query_w, held.query_w),
            (coming.key_w, held.key_w),
            (coming.value_w, held.value_w),
            (coming.out_w, held.out_w),
        )
    ):
        copy.wait()
        attn_piece[:, number * width : (number + 1) * width] = raw[...]
    vectors[...] = jnp.zeros_like(vectors)
    for number, (copy, raw) in enumerate(
        (
            (coming.first_gain, held.first_gain),
            (coming.first_shift, held.first_shift),
            (coming.out_bias, held.out_bias),
            (coming.second_gain, held.second_gain),
            (coming.second_shift, held.second_shift),
            (coming.down_bias, held.down_bias),
        )
    ):
        copy.wait()
        vectors[number : number + 1, :] = raw[...].reshape(1, D)
    coming.up_bias.wait()
    vectors[6:7, :units] = held.up_bias[...].reshape(1, units)
    coming.query_bias.wait()
    vectors[7:8, :width] = held.query_bias[...].reshape(1, width)
    coming.value_bias.wait()
    vectors[7:8, 2 * width : 3 * width] = held.value_bias[...].reshape(1, width)
    first_gain, first_shift = vectors[0:1, :], vectors[1:2, :]
    out_bias, second_gain = vectors[2:3, :], vectors[3:4, :]
    second_shift, down_bias = vectors[4:5, :], vectors[5:6, :]
    tokens_ref, cotangent_ref = held.tokens, held.cotangent
    coming.tokens.wait()
    coming.cotangent.wait()
    token_rows = tokens_ref[...].astype(f32)
    normed, hat, inv_scale = norm_rows(token_rows, first_gain, first_shift)
    first_all[slot(near, c), :] = normed.astype(bf16)
    ref.first_hat[...] = hat
    ref.row_scale[0] = jnp.broadcast_to(inv_scale, (rows, LANES))

    pl.semaphore_wait(barrier, len(peers))

    first_sems = share_start(first_all)
    lane_cut = round_up(qkv_lanes // 2, LANES)
    q_parts = [(attn_w, 0, lane_cut), (attn_w, lane_cut, qkv_lanes)]
    o_part = (attn_w, qkv_lanes, all_lanes)
    q_base = [spread_start(attn_piece, *part) for part in q_parts]
    o_base = spread_start(attn_piece, *o_part)
    vec_sem = net.sem()
    net.send(vectors, ref.far_vectors, dev_far, vec_sem)
    up_parts = [
        WideGather(ref.up_piece, up_w, ref.up_wait, lo, hi)
        for lo, hi in ((0, 64), (64, 144))
    ]
    down_parts = [
        WideGather(ref.down_piece, down_w, ref.down_wait, lo, hi)
        for lo, hi in row_cuts(piece, 3)
    ]

    coming.up_w.wait()
    coming.down_w.wait()
    ref.up_piece[:, main:] = jnp.zeros((piece, LANES), bf16)
    ref.up_piece[:, :units] = held.up_w[...]
    ref.up_piece[:, units : units + rest] = held.down_w[:, main:]
    ref.down_piece[...] = held.down_w[:, :main]
    dy_all[slot(near, kx), :] = cotangent_ref[...]
    vec_own[5:6, :] = jnp.sum(cotangent_ref[...].astype(f32), axis=0, keepdims=True)
    head_rows[...] = jnp.zeros_like(head_rows)
    head_grads[...] = jnp.zeros_like(head_grads)
    mixed_all[...] = jnp.zeros_like(mixed_all)
    qkv_grads[...] = jnp.zeros_like(qkv_grads)

    def shard_vector(row, own):
        return jnp.where(own, vectors[row : row + 1, :], ref.far_vectors[row : row + 1, :])

    scale = HD ** (-0.5)

    def image_head(step):
        head, image = lax.rem(step, heads), lax.div(step, heads)
        return head, aligned(image * pair, pair)

    def attend(step, carry):
        head, span = image_head(step)
        queries, keys_part = head_rows[head, span, :], head_rows[heads + head, span, :]
        values = head_rows[2 * heads + head, span, :]
        scores = dot_right_t(queries, keys_part) * scale
        expo = jnp.exp(scores - jnp.max(scores, axis=1, keepdims=True))
        probs = expo / jnp.sum(expo, axis=1, keepdims=True)
        ref.probs_all[step] = probs
        mixed = dot_plain(probs.astype(bf16), values)
        ref.mixed_heads[head, span, :] = mixed.astype(bf16)
        return carry

    def pack(target, source, count, base):
        for side_at in range(2):
            for image in range(2):
                at = slice(side_at * pair + image * rows, side_at * pair + (image + 1) * rows)
                take = slice(image * pair + side_at * rows, image * pair + (side_at + 1) * rows)
                for head in range(count):
                    lo = base + head * HD
                    target[at, lo : lo + HD] = source[head, take, :HD]

    def half(side):
        return aligned(side, pair)

    chunk = 32

    in_rest = lax.broadcasted_iota(jnp.int32, (chunk, LANES), 1) < rest

    hidden_rest = ref.hidden_rest

    def raise_half(side):
        part_b[half(side), :] = dot_plain(second_all[half(side), :], up_w[...])

        def gelu_rows(step, carry):
            at = aligned(side + step * chunk, chunk)
            value, slope = gelu_pair(part_b[at, :] + up_bias)
            last = jnp.where(in_rest, value[:, main:], 0.0)
            hidden_all[at, :main] = value[:, :main].astype(bf16)
            hidden_all[at, main:] = last.astype(bf16)
            hidden_rest[at, :] = pltpu.roll(last, rest, 1).astype(bf16)
            slope_all[at, :] = slope
            return carry

        lax.fori_loop(0, pair // chunk, gelu_rows, 0)

    tile = 3 * LANES

    def outer_product(grad, left, right, lo, hi):
        def rows_of(step, carry):
            at = aligned(step * tile, tile)
            grad[at, lo:hi] = dot_left_t(left[:, at], right).astype(bf16)
            return carry

        lax.fori_loop(0, D // tile, rows_of, 0, unroll=True)

    def lower_half(side):
        part_b[half(side), :main] = dot_plain(dy_all[half(side), :], down_w[...])
        part_b[half(side), main:] = dot_plain(dy_all[half(side), :], up_w[:, main:])

        def slope_rows(step, totals):
            at = aligned(side + step * chunk, chunk)
            last = pltpu.roll(part_b[at, main:], LANES - rest, 1)
            last = jnp.where(in_rest, last * slope_all[at, main:], 0.0).astype(bf16)
            low = (part_b[at, :main] * slope_all[at, :main]).astype(bf16)
            upper_all[at, :main] = low
            upper_all[at, main:] = last
            return (
                totals[0] + jnp.sum(low.astype(f32), axis=0, keepdims=True),
                totals[1] + jnp.sum(last.astype(f32), axis=0, keepdims=True),
            )

        start = jnp.zeros((1, main), f32), jnp.zeros((1, LANES), f32)
        return lax.fori_loop(0, pair // chunk, slope_rows, start)

    def up_rows(step, carry):
        at = aligned(step * tile, tile)
        by_row = second_all[:, at]
        up_g[at, :main] = dot_left_t(by_row, upper_all[:, :main]).astype(bf16)
        last = dot_left_t(by_row, upper_all[:, main:])
        last = last + dot_left_t(dy_all[:, at], hidden_rest[...])
        up_g[at, main:] = last.astype(bf16)
        return carry

    def lower_product(side):
        total = dot_right_t(hidden_all[half(side), :main], down_w[...])
        return total + dot_right_t(hidden_rest[half(side), :], up_w[:, main:])

    def head_half(side_at):
        side_rows = slice(side_at * pair, (side_at + 1) * pair)
        done = dot_plain(mid_all[side_rows, :], attn_w[:, win:]).astype(bf16)
        for image in range(2):
            to = slice(image * pair + side_at * rows, image * pair + (side_at + 1) * rows)
            for head in range(heads):
                lo = win_shift + head * HD
                head_grads[head, to, :HD] = done[image * rows : (image + 1) * rows, lo : lo + HD]

    cut = round_up(2 * width, LANES)

    def value_back(step, carry):
        head, span = image_head(step)
        low = ref.probs_all[step].astype(bf16)
        value_grad = dot_left_t(low, head_grads[head, span, :])
        ref.mixed_heads[head, span, :] = value_grad.astype(bf16)
        return carry

    def value_out_rows(step, carry):
        at = aligned(step * tile, tile)
        by_value = dot_left_t(first_all[:, at], qkv_grads[:, cut:qkv_lanes])
        by_out = dot_left_t(mid_all[:, at], mixed_all[...])
        both = by_value[:, win - cut :] + by_out[:, :skip]
        attn_g[at, cut:win] = by_value[:, : win - cut].astype(bf16)
        attn_g[at, win:qkv_lanes] = both.astype(bf16)
        attn_g[at, qkv_lanes:] = by_out[:, skip:].astype(bf16)
        return carry

    def attend_back(step, carry):
        head, span = image_head(step)
        queries, keys_part = head_rows[head, span, :], head_rows[heads + head, span, :]
        values, grads = head_rows[2 * heads + head, span, :], head_grads[head, span, :]
        probs = ref.probs_all[step]
        prob_grad = dot_right_t(grads, values)
        row_dot = jnp.sum(probs * prob_grad, axis=1, keepdims=True)
        score_grad = (probs * (prob_grad - row_dot)).astype(bf16)
        query_grad = dot_plain(score_grad, keys_part) * scale
        key_grad = dot_left_t(score_grad, queries) * scale
        head_rows[head, span, :] = query_grad.astype(bf16)
        head_rows[heads + head, span, :] = key_grad.astype(bf16)
        return carry

    for part in up_parts:
        part.start(inner)
    dy_sems = plain_share_z(dy_all)
    q_sems = [gather_start(*part, base) for part, base in zip(q_parts, q_base)]
    for part in up_parts:
        part.start(jnp.logical_and(outer, away))
    for part, sems in zip(q_parts, q_sems):
        gather_forward(*part, sems)
    for part in up_parts:
        part.start(jnp.logical_and(outer, home))
    o_sems = gather_start(*o_part, o_base)
    share_forward(first_all, first_sems)
    net.arrived(ref.far_vectors, vec_sem)
    share_near(first_all, first_sems)
    share_deep(first_all, first_sems)
    qkv_bias = shard_vector(7, home)[:, :qkv_lanes]
    up_bias = shard_vector(6, stay)
    for part, sems in zip(q_parts, q_sems):
        gather_finish(*part, sems)
    for part in down_parts:
        part.start(outer)
    gather_forward(*o_part, o_sems)
    plain_share_x(dy_all, dy_sems)
    for part in up_parts:
        part.beside()
    for part in down_parts:
        part.beside()
    for side_at in range(2):
        side_rows = slice(side_at * pair, (side_at + 1) * pair)
        done = dot_plain(first_all[side_rows, :], attn_w[:, :qkv_lanes])
        done = (done + qkv_bias).astype(bf16)
        for image in range(2):
            to = slice(image * pair + side_at * rows, image * pair + (side_at + 1) * rows)
            for head in range(3 * heads):
                head_rows[head, to, :HD] = done[
                    image * rows : (image + 1) * rows, head * HD : (head + 1) * HD
                ]
    lax.fori_loop(0, 2 * heads, attend, 0, unroll=4)
    pack(mixed_all, ref.mixed_heads, heads, win_shift)
    gather_finish(*o_part, o_sems)
    part_a[half(deep), :] = dot_right_t(mixed_all[half(deep), :], attn_w[:, win:])
    out_sems = sum_deep(0, part_a)
    part_a[half(near), :] = dot_right_t(mixed_all[half(near), :], attn_w[:, win:])
    sum_pass(0, part_a, out_sems)
    sum_near(0, part_a, out_sems)
    up_parts[0].second()
    up_parts[1].second()
    up_parts[0].third()
    attn_rows = sum_finish(0, part_a, out_sems)
    middle = tokens_ref[...].astype(f32) + attn_rows + out_bias
    ref.mid_rows[...] = middle
    normed, hat, inv_scale = norm_rows(middle, second_gain, second_shift)
    second_all[slot(near, kx), :] = normed.astype(bf16)
    ref.second_hat[...] = hat
    ref.row_scale[1] = jnp.broadcast_to(inv_scale, (rows, LANES))
    second_sems = wide_share_start(second_all)
    for part in down_parts:
        part.start(inner)
    up_parts[1].third()
    wide_share_forward(second_all, second_sems)
    down_parts[0].second()
    down_parts[1].second()
    down_parts[2].second()
    plain_share_forward(dy_all, dy_sems)
    up_parts[0].fourth()
    up_parts[1].fourth()
    down_parts[0].third()
    for part in up_parts:
        part.finish()
    wide_share_near(second_all, second_sems)
    raise_half(near)
    down_parts[1].third()
    wide_share_deep(second_all, second_sems)
    raise_half(deep)
    down_parts[2].third()
    down_parts[0].fourth()
    plain_share_finish(dy_all, dy_sems)
    outer_product(down_g, dy_all, hidden_all[:, :main], 0, main)
    down_reduce = wide_reduce_first(down_g, ref.land_d)
    down_parts[1].fourth()
    wide_reduce_second(down_g, ref.land_d, down_reduce)
    down_parts[2].fourth()
    for part in down_parts:
        part.finish()
    up_bias_sum = lower_half(deep)
    part_a[half(deep), :] = dot_right_t(upper_all[half(deep), :], up_w[...])
    second_sum_sems = wide_sum_deep(0, part_a)
    more_sum = lower_half(near)
    vec_own[6:7, :main] = up_bias_sum[0] + more_sum[0]
    vec_own[6:7, main:] = up_bias_sum[1] + more_sum[1]
    part_a[half(near), :] = dot_right_t(upper_all[half(near), :], up_w[...])
    wide_sum_near(0, part_a, second_sum_sems)
    lax.fori_loop(0, D // tile, up_rows, 0, unroll=True)
    up_reduce = wide_reduce_first(up_g, ref.land_u)
    wide_sum_pass(0, part_a, second_sum_sems)
    wide_reduce_second(up_g, ref.land_u, up_reduce)
    wide_reduce_third(down_g, ref.land_d, down_reduce)
    second_grad = wide_sum_finish(0, part_a, second_sum_sems)
    back, gain_sum, shift_sum = norm_back(
        second_grad, ref.second_hat[...], ref.row_scale[1][:, :1], second_gain
    )
    vec_own[3:4, :] = gain_sum[None, :]
    vec_own[4:5, :] = shift_sum[None, :]
    total = cotangent_ref[...].astype(f32) + back
    ref.mid_grad[...] = total
    low = total.astype(bf16)
    mid_all[slot(near, c), :] = low
    vec_own[2:3, :] = jnp.sum(low.astype(f32), axis=0, keepdims=True)
    mid_sems = share_start(mid_all)
    part_b[half(deep), :] = lower_product(deep)
    mlp_sems = wide_sum_deep(1, part_b)
    part_b[half(near), :] = lower_product(near)
    wide_sum_near(1, part_b, mlp_sems)
    share_forward(mid_all, mid_sems)
    wide_reduce_cross(down_g, ref.land_d, down_reduce, when=outer)
    share_near(mid_all, mid_sems)
    wide_reduce_fourth(down_g, ref.land_d, down_reduce, when=outer)
    share_deep(mid_all, mid_sems)
    head_half(0)
    head_half(1)
    wide_reduce_third(up_g, ref.land_u, up_reduce)
    wide_reduce_cross(down_g, ref.land_d, down_reduce, when=inner)
    wide_reduce_fourth(down_g, ref.land_d, down_reduce, when=inner)
    lax.fori_loop(0, 2 * heads, value_back, 0, unroll=2)
    pack(qkv_grads, ref.mixed_heads, heads, 2 * width)
    lax.fori_loop(0, D // tile, value_out_rows, 0)
    vo_args = attn_g, ref.land_vo, cut, all_lanes, net.sems(8)
    reduce_first(*vo_args)
    wide_sum_pass(1, part_b, mlp_sems)
    lax.fori_loop(0, 2 * heads, attend_back, 0, unroll=2)
    wide_reduce_fourth(up_g, ref.land_u, up_reduce, when=outer)
    pack(qkv_grads, head_rows, 2 * heads, 0)
    wide_reduce_cross(up_g, ref.land_u, up_reduce, when=outer)
    part_a[half(deep), :] = dot_right_t(
        qkv_grads[half(deep), :qkv_lanes], attn_w[:, :qkv_lanes]
    )
    first_sum_sems = sum_deep(1, part_a)
    part_a[half(near), :] = dot_right_t(
        qkv_grads[half(near), :qkv_lanes], attn_w[:, :qkv_lanes]
    )
    sum_pass(1, part_a, first_sum_sems)
    sum_near(1, part_a, first_sum_sems)
    vec_own[7:8, :] = jnp.sum(qkv_grads[...].astype(f32), axis=0, keepdims=True)
    outer_product(attn_g, first_all, qkv_grads[:, :cut], 0, cut)
    qk_args = attn_g, ref.land_qk, 0, cut, net.sems(8)
    reduce_first(*qk_args, when=away)
    wide_reduce_fourth(up_g, ref.land_u, up_reduce, when=inner)
    reduce_second(*vo_args)
    wide_reduce_cross(up_g, ref.land_u, up_reduce, when=inner)
    reduce_second(*qk_args, when=away)
    first_grad = sum_finish(1, part_a, first_sum_sems)
    back, gain_sum, shift_sum = norm_back(
        first_grad, ref.first_hat[...], ref.row_scale[0][:, :1], first_gain
    )
    vec_own[0:1, :] = gain_sum[None, :]
    vec_own[1:2, :] = shift_sum[None, :]
    vec_sem = vector_planes()
    ref.mid_grad[...] = ref.mid_grad[...] + back
    store(ref.mid_grad, out.input_grad)
    reduce_first(*qk_args, when=home)
    reduce_third(*vo_args)
    reduce_third(*qk_args, when=away)
    vec_sem = vector_chips(vec_sem)
    vec_sem = vector_core(vec_sem)
    reduce_second(*qk_args, when=home)
    vector_finish(vec_sem)
    store(ref.vec_done, out.vector_grad)
    reduce_third(*qk_args, when=home)
    ref.down_buf[...] = wide_reduce_finish(down_g, ref.land_d, down_reduce)
    store(ref.down_buf, out.down_grad)
    mlp_rows = wide_sum_finish(1, part_b, mlp_sems)
    ref.layer_buf[...] = (ref.mid_rows[...] + mlp_rows + down_bias).astype(bf16)
    store(ref.layer_buf, out.layer_out)
    ref.up_buf[...] = wide_reduce_finish(up_g, ref.land_u, up_reduce)
    store(ref.up_buf, out.up_grad)
    ref.attn_buf[:, cut:] = reduce_finish(ref.land_vo, vo_args[4])
    store(ref.attn_buf.at[:, cut:], out.attn_grad.at[:, cut:])
    ref.attn_buf[:, :cut] = reduce_finish(ref.land_qk, qk_args[4])
    store(ref.attn_buf.at[:, :cut], out.attn_grad.at[:, :cut])
    net.drain()
    assert net.used <= ref.recv_sems.shape[0]
    for copy in stores:
        copy.wait()


def format_kernel(shapes, *refs):
    width, units = shapes
    inputs, refs = refs[:6], refs[6:]
    outs, refs = refs[:17], refs[17:]
    held, refs = refs[:6], refs[6:]
    shaped, sems = refs[:-1], refs[-1]
    copies = [
        pltpu.make_async_copy(source, target, sems.at[number])
        for number, (source, target) in enumerate(zip(inputs, held, strict=True))
    ]
    for copy in copies:
        copy.start()
    going = []

    def put(source, number):
        copy = pltpu.make_async_copy(source, outs[number], sems.at[6 + number])
        copy.start()
        going.append(copy)

    def put_shaped(number, value):
        shaped[number - 2][...] = value
        put(shaped[number - 2], number)

    copies[0].wait()
    put(held[0], 0)
    copies[1].wait()
    put(held[1], 1)
    copies[2].wait()
    for number, place in ((4, 0), (5, 1), (6, 2), (9, 3)):
        put_shaped(number, held[2][:, place * width : (place + 1) * width])
    copies[3].wait()
    put_shaped(13, held[3][:, :units])
    copies[4].wait()
    main = held[4].shape[1]
    shaped[13][:, :main] = held[4][...]
    shaped[13][:, main:] = held[3][:, units : 2 * units - main]
    put(shaped[13], 15)
    copies[5].wait()
    for number, row, lo, size in (
        (2, 0, 0, D),
        (3, 1, 0, D),
        (10, 2, 0, D),
        (11, 3, 0, D),
        (12, 4, 0, D),
        (16, 5, 0, D),
        (14, 6, 0, units),
        (7, 7, 0, width),
        (8, 7, 2 * width, width),
    ):
        put_shaped(number, held[5][row, lo : lo + size])
    for copy in going:
        copy.wait()


def fused_step(
    tokens,
    cotangent,
    first_gain,
    first_shift,
    query_weight,
    key_weight,
    value_weight,
    query_bias,
    value_bias,
    out_weight,
    out_bias,
    second_gain,
    second_shift,
    up_weight,
    up_bias,
    down_weight,
    down_bias,
):
    bf16, f32 = jnp.bfloat16, jnp.float32
    rows, piece, width, units = (
        tokens.shape[0],
        query_weight.shape[0],
        query_weight.shape[1],
        up_weight.shape[1],
    )
    heads = width // HD
    group = 4 * rows
    qkv_lanes = round_up(3 * width, LANES)
    attn_lanes = round_up(4 * width, LANES)
    ff_lanes = round_up(units, LANES)
    main = units // LANES * LANES
    assert 2 * (units - main) <= LANES < ff_lanes - main + 1
    win = 3 * width // LANES * LANES
    given = dict(
        query_w=query_weight,
        key_w=key_weight,
        value_w=value_weight,
        out_w=out_weight.T,
        first_gain=first_gain,
        first_shift=first_shift,
        out_bias=out_bias,
        second_gain=second_gain,
        second_shift=second_shift,
        down_bias=down_bias,
        up_bias=up_bias,
        query_bias=query_bias,
        value_bias=value_bias,
        tokens=tokens,
        cotangent=cotangent,
        up_w=up_weight,
        down_w=down_weight.T,
    )
    place = pl.BlockSpec(memory_space=pl.ANY)
    cut = round_up(2 * width, LANES)
    raw_outs = dict(
        layer_out=jax.ShapeDtypeStruct((rows, D), bf16),
        input_grad=jax.ShapeDtypeStruct((rows, D), f32),
        attn_grad=jax.ShapeDtypeStruct((piece, attn_lanes), f32),
        up_grad=jax.ShapeDtypeStruct((piece, ff_lanes), f32),
        down_grad=jax.ShapeDtypeStruct((piece, main), f32),
        vector_grad=jax.ShapeDtypeStruct((8, D), f32),
    )
    scratch = dict(
        attn_piece=pltpu.VMEM((piece, attn_lanes), bf16),
        up_piece=pltpu.VMEM((piece, ff_lanes), bf16),
        down_piece=pltpu.VMEM((piece, main), bf16),
        up_wait=pltpu.VMEM((piece, ff_lanes), bf16),
        down_wait=pltpu.VMEM((piece, main), bf16),
        attn_w=pltpu.VMEM((D, attn_lanes), bf16),
        up_w=pltpu.VMEM((D, ff_lanes), bf16),
        down_w=pltpu.VMEM((D, main), bf16),
        attn_g=pltpu.VMEM((D, attn_lanes), bf16),
        up_g=pltpu.VMEM((D, ff_lanes), bf16),
        down_g=pltpu.VMEM((D, main), bf16),
        land_vo=pltpu.VMEM((8, piece, attn_lanes - cut), bf16),
        land_qk=pltpu.VMEM((8, piece, cut), bf16),
        land_u=pltpu.VMEM((8, piece, ff_lanes), bf16),
        land_d=pltpu.VMEM((8, piece, main), bf16),
        first_all=pltpu.VMEM((group, D), bf16),
        second_all=pltpu.VMEM((group, D), bf16),
        dy_all=pltpu.VMEM((group, D), bf16),
        mid_all=pltpu.VMEM((group, D), bf16),
        head_rows=pltpu.VMEM((3 * heads, group, LANES), bf16),
        head_grads=pltpu.VMEM((heads, group, LANES), bf16),
        probs_all=pltpu.VMEM((2 * heads, 2 * rows, 2 * rows), f32),
        mixed_heads=pltpu.VMEM((heads, group, LANES), bf16),
        mixed_all=pltpu.VMEM((group, attn_lanes - win), bf16),
        hidden_all=pltpu.VMEM((group, ff_lanes), bf16),
        hidden_rest=pltpu.VMEM((group, LANES), bf16),
        slope_all=pltpu.VMEM((group, ff_lanes), f32),
        upper_all=pltpu.VMEM((group, ff_lanes), bf16),
        qkv_grads=pltpu.VMEM((group, attn_lanes), bf16),
        part_a=pltpu.VMEM((group, D), f32),
        part_b=pltpu.VMEM((group, D), f32),
        core_send=pltpu.VMEM((2, 2, rows, D), bf16),
        core_land=pltpu.VMEM((2, 2, rows, D), bf16),
        deep_send=pltpu.VMEM((2, rows, D), bf16),
        deep_land=pltpu.VMEM((2, rows, D), bf16),
        wide_send=pltpu.VMEM((2, 6, rows // 2, D), bf16),
        wide_land=pltpu.VMEM((2, 6, rows // 2, D), bf16),
        first_hat=pltpu.VMEM((rows, D), f32),
        second_hat=pltpu.VMEM((rows, D), f32),
        mid_rows=pltpu.VMEM((rows, D), f32),
        mid_grad=pltpu.VMEM((rows, D), f32),
        row_scale=pltpu.VMEM((2, rows, LANES), f32),
        vectors=pltpu.VMEM((8, D), f32),
        far_vectors=pltpu.VMEM((8, D), f32),
        vec_own=pltpu.VMEM((8, D), f32),
        by_plane=pltpu.VMEM((4, 8, D), f32),
        vec_chip=pltpu.VMEM((8, D), f32),
        by_chip=pltpu.VMEM((4, 8, D), f32),
        vec_core=pltpu.VMEM((8, D), f32),
        vec_core_land=pltpu.VMEM((8, D), f32),
        vec_done=pltpu.VMEM((8, D), f32),
        layer_buf=pltpu.VMEM((rows, D), bf16),
        attn_buf=pltpu.VMEM((piece, attn_lanes), f32),
        up_buf=pltpu.VMEM((piece, ff_lanes), f32),
        down_buf=pltpu.VMEM((piece, main), f32),
        load_sems=pltpu.SemaphoreType.DMA((len(given) + len(raw_outs) + 1,)),
        send_sems=pltpu.SemaphoreType.DMA((48,)),
        recv_sems=pltpu.SemaphoreType.DMA((108,)),
    )
    shapes = (rows, heads, width, units, qkv_lanes, piece)
    names = tuple(given), tuple(raw_outs), tuple(scratch)

    def body(*refs):
        layer_kernel(shapes, names, *refs)

    raw = pl.pallas_call(
        body,
        out_shape=tuple(raw_outs.values()),
        in_specs=[place] * len(given),
        out_specs=(place,) * len(raw_outs),
        scratch_shapes=[
            *(pltpu.VMEM(array.shape, array.dtype) for array in given.values()),
            *scratch.values(),
        ],
        compiler_params=pltpu.CompilerParams(
            collective_id=0, has_side_effects=True, vmem_limit_bytes=67043328
        ),
        name="layer",
    )(*given.values())
    raw_outs = tuple(raw_outs.values())

    vector, narrow = jax.ShapeDtypeStruct((D,), f32), jax.ShapeDtypeStruct((width,), f32)
    attn_out = jax.ShapeDtypeStruct((piece, width), f32)
    ff_out = jax.ShapeDtypeStruct((piece, units), f32)
    outs = (
        *raw_outs[:2],
        vector,
        vector,
        attn_out,
        attn_out,
        attn_out,
        narrow,
        narrow,
        attn_out,
        vector,
        vector,
        vector,
        ff_out,
        jax.ShapeDtypeStruct((units,), f32),
        ff_out,
        vector,
    )

    def format_body(*refs):
        format_kernel((width, units), *refs)

    done = pl.pallas_call(
        format_body,
        out_shape=outs,
        in_specs=[place] * 6,
        out_specs=(place,) * 17,
        scratch_shapes=[
            *(pltpu.VMEM(item.shape, item.dtype) for item in raw_outs),
            *(pltpu.VMEM(item.shape, item.dtype) for item in outs[2:]),
            pltpu.SemaphoreType.DMA((6 + 17,)),
        ],
        compiler_params=pltpu.CompilerParams(vmem_limit_bytes=67043328),
        name="outputs",
    )(*raw)
    done = list(done)
    done[9], done[15] = done[9].T, done[15].T
    return tuple(done)


def pick_step(mesh):
    if mesh.shape["fsdp"] == 8 and mesh.shape["tensor"] == 4:
        return fused_step
    return on_device


def solution(mesh):
    return jax.shard_map(
        pick_step(mesh),
        mesh=mesh,
        in_specs=(
            P(("fsdp", "tensor"), None),
            P(("fsdp", "tensor"), None),
            P(),
            P(),
            P("fsdp", "tensor"),
            P("fsdp", "tensor"),
            P("fsdp", "tensor"),
            P("tensor"),
            P("tensor"),
            P("tensor", "fsdp"),
            P(),
            P(),
            P(),
            P("fsdp", "tensor"),
            P("tensor"),
            P("tensor", "fsdp"),
            P(),
        ),
        out_specs=(
            P(("fsdp", "tensor"), None),
            P(("fsdp", "tensor"), None),
            P(),
            P(),
            P("fsdp", "tensor"),
            P("fsdp", "tensor"),
            P("fsdp", "tensor"),
            P("tensor"),
            P("tensor"),
            P("tensor", "fsdp"),
            P(),
            P(),
            P(),
            P("fsdp", "tensor"),
            P("tensor"),
            P("tensor", "fsdp"),
            P(),
        ),
        check_vma=False,
    )
```
